32 devices in a mesh: freq: 2 (over x), tile: 16 (over z, y, core).
Axes of the slice: x: 2, y: 2, z: 4, core: 2. Of those that a mesh axis runs over, the one named last changes fastest.
Arguments:
- data: float32 [4, 2048, 256], P('freq', 'tile'), parts along dimension 0, may hold values from -6 to 6
- x_init: float32 [4, 8192, 256], P('freq', 'tile'), parts along dimension 0, may hold values from -6 to 6
- ufac: bfloat16 [4, 2048, 256], P('freq', 'tile'), parts along dimension 0, may hold values from -0.1875 to 0.1875
- vfac: bfloat16 [4, 4, 16, 8192], P('freq', None, None, 'tile'), parts along dimension 0, may hold values from -0.25 to 0.25
Outputs:
- solution: float32 [4, 8192, 256], P('freq', 'tile'), parts along dimension 0
- residual: float32 [4, 2048, 256], P('freq', 'tile'), parts along dimension 0
The draws below stay inside these ranges and needn't reach their ends.
There are 2 independent parts, one for each index of `freq`. The reference program is written for one: setup_inputs(seed, part) draws one part's arguments, and reference() takes and returns one part's arrays. A program takes and returns all parts, laid end to end along the dimension named above; each array names one. Nothing has to cross between parts.
All inputs are finite; a program needn't handle non-finite values.
Results may differ from the reference program's by a relative error of at most 0.0058.
Values may be sent and summed in bfloat16 or wider, within the bound.
No kernel may reach another device: no remote copies, remote signals or barrier semaphores. Data moves between devices by JAX's collectives and lax.ppermute only.
A program may use at most 64 MiB of HBM per device.

```python
import jax
import jax.numpy as jnp

TILE = 512
RANK = 16
NV = 256
ITERS = 2
TROWS = 4
NR = 2048
NS = 8192
N_TILE = 16


def level_of(rng, shape, shards, low, top_value):
    def one(dim, blocks):
        heights = jax.random.uniform(jax.random.fold_in(jax.random.fold_in(rng, 6), dim), (blocks,), jnp.float32, low / len(shards), top_value / len(shards))
        return jnp.repeat(jnp.exp(heights), shape[dim] // blocks).reshape((-1,) + (1,) * (len(shape) - dim - 1))

    loudness = one(*shards[0])
    for cut in shards[1:]:
        loudness = loudness * one(*cut)
    return loudness


def bell_draw(own_key, shape, width, most, shards=(), dtype=jnp.bfloat16):
    entries = jax.random.normal(own_key, shape, jnp.float32) * width
    if len(shards) > 0:
        entries = level_of(own_key, shape, shards, -0.22, 0.18) * entries
    return jnp.clip(entries, min=-most, max=most).astype(dtype)


def setup_inputs(seed: int = 0, part: int = 0) -> dict:
    key_list = jax.random.split(jax.random.key(seed), 5)
    part_splits = jax.random.split(jax.random.fold_in(key_list[4], part), 5)
    return {
        "data": bell_draw(part_splits[0], (2, NR, NV), 1.0, 6.0, ((1, 16),), jnp.float32),
        "x_init": bell_draw(part_splits[1], (2, NS, NV), 1.0, 6.0, ((1, 16),), jnp.float32),
        "ufac": bell_draw(part_splits[2], (2, NR, N_TILE * RANK), (4 * N_TILE * RANK) ** -0.5, 0.1875, ((1, 16),)),
        "vfac": bell_draw(part_splits[3], (2, TROWS, RANK, NS), TILE ** -0.5, 0.25, ((3, 16),)),
    }


step_size = 0.4
threshold = 0.4

def complex_product(pattern, factors, vectors, conjugate):

    def single(factor_part, vector_part):
        return jnp.einsum(pattern, factor_part.astype(jnp.float32), vector_part.astype(jnp.float32))
    if conjugate:
        real_part = single(factors[0], vectors[0]) + single(factors[1], vectors[1])
        imag_part = single(factors[0], vectors[1]) - single(factors[1], vectors[0])
    else:
        real_part = single(factors[0], vectors[0]) - single(factors[1], vectors[1])
        imag_part = single(factors[0], vectors[1]) + single(factors[1], vectors[0])
    return jnp.stack([real_part, imag_part])

def shrink(values):
    magnitude = jnp.sqrt(values[0] * values[0] + values[1] * values[1])
    shrink_factor = jnp.maximum(magnitude - threshold, 0.0) / jnp.maximum(magnitude, threshold)
    return values * shrink_factor

def reference(data, x_init, ufac, vfac):
    right_tiles = vfac.reshape(2, TROWS, RANK, N_TILE, TILE)
    left_tiles = ufac.reshape(2, TROWS, TILE, N_TILE, RANK)
    estimate = x_init
    misfit = data
    for iteration in range(ITERS):
        xlow = estimate.astype(jnp.bfloat16).reshape(2, N_TILE, TILE, NV)
        coeffs = complex_product('irjk,jkv->irjv', right_tiles, xlow, True).astype(jnp.bfloat16)
        predicted = complex_product('itjr,irjv->itv', left_tiles, coeffs, False).reshape(2, NR, NV)
        misfit = data - predicted
        misfit_low = misfit.astype(jnp.bfloat16).reshape(2, TROWS, TILE, NV)
        adjoint_coeffs = complex_product('itjr,itv->irjv', left_tiles, misfit_low, True).astype(jnp.bfloat16)
        gradient = complex_product('irjk,irjv->jkv', right_tiles, adjoint_coeffs, False).reshape(2, NS, NV)
        estimate = shrink(estimate + step_size * gradient)
    return (estimate, misfit)
```

```python
import functools

import jax
import jax.numpy as jnp
from jax import lax
from jax.experimental import pallas as pl
from jax.experimental.pallas import tpu as pltpu
from jax.sharding import PartitionSpec as P

ITERS = 2
STEP = 0.4
THRESHOLD = 0.4

f32 = jnp.float32
bf16 = jnp.bfloat16


def dot(a, b, dims=((1,), (0,))):
    return lax.dot_general(a, b, (dims, ((), ())), preferred_element_type=f32)


def swap_halves(a):
    return pltpu.roll(a, a.shape[1] // 2, 1)


def left_half(a):
    return lax.broadcasted_iota(jnp.int32, a.shape, 1) < a.shape[1] // 2


def times_i(a):
    s = swap_halves(a)
    return jnp.where(left_half(a), -s, s)


def interleave(re, im):
    low = left_half(re)
    return (
        jnp.where(low, re, swap_halves(im)),
        jnp.where(low, swap_halves(re), im),
    )


def slices_of(re, im, width):
    out = []
    for k in range(re.shape[1] // (2 * width)):
        cut = slice(2 * width * k, 2 * width * (k + 1))
        out.extend(interleave(re[:, cut], im[:, cut]))
    return out


def group_index(group):
    return lax.rem(lax.axis_index("tile"), group)


def prepare_kernel(data, ufac, to_far, to_near, own, *, group, width):
    rows = data.shape[1]
    folds = ufac.shape[2] // (4 * width)
    step = rows // folds
    q = group_index(group)
    stage = slices_of(data[0], data[1], width)

    def place(scratch):
        for s, block in enumerate(stage):
            scratch[jnp.bitwise_xor(q, s)] = block
        own[...] = scratch[0]

        def split(block):
            high = block.astype(bf16)
            low = (block - high.astype(f32)).astype(bf16)
            return high, low

        for ref, base, b in ((to_near, 0, 1), (to_far, 0, 2), (to_far, step, 3)):
            high, low = split(scratch[b])
            for g in range(folds):
                cut = slice(g * step, (g + 1) * step)
                lane = 4 * width * g
                ref[base:base + step, lane:lane + 2 * width] = high[cut]
                ref[base:base + step, lane + 2 * width:lane + 4 * width] = low[cut]

    pl.run_scoped(place, pltpu.VMEM((group, rows, 2 * width), f32))
    for part in range(2):
        to_near[step + rows * part:step + rows * (part + 1)] = ufac[part]
        to_far[2 * step + rows * part:2 * step + rows * (part + 1)] = ufac[part]


def send_coeffs(vcat, xr, xi, out, *, group, width):
    half = vcat.shape[0] // 2
    t1 = dot(vcat, xr)
    t2 = dot(vcat, xi)
    cr = t1[:half] + t2[half:]
    ci = t2[:half] - t1[half:]
    rank = out.shape[1]
    blocks = slices_of(cr, ci, width)
    for i in range(half // rank):
        for q in range(group):
            out[i * group + q] = blocks[q][i * rank:(i + 1) * rank].astype(bf16)


def flat_factors(vfac):
    parts, rows, rank, count = vfac.shape
    return vfac[...].reshape(parts * rows * rank, count)


def first_kernel(x, vfac, out, *, group, width):
    send_coeffs(flat_factors(vfac), x[0].astype(bf16), x[1].astype(bf16), out, group=group, width=width)


def row_kernel(coeffs, own, ufac, near, far, far_near, adjoint, *maybe_misfit, width):
    lanes = 2 * width
    rows = own.shape[0]
    c = coeffs[...].reshape(-1, lanes)
    ci = times_i(c.astype(f32)).astype(bf16)

    folds = ufac.shape[2] // (2 * lanes)
    step = rows // folds

    def joined(ref, base):
        cuts = [ref[base:base + step, 2 * lanes * g:2 * lanes * (g + 1)].astype(f32) for g in range(folds)]
        pair = jnp.concatenate(cuts, axis=0)
        return pair[:, :lanes] + pair[:, lanes:]

    def factors(ref, base):
        return ref[base:base + rows], ref[base + rows:base + 2 * rows]

    blocks = (
        (own[...], (ufac[0], ufac[1])),
        (joined(near, 0), factors(near, step)),
        (joined(far, 0), factors(far, 2 * step)),
        (joined(far_near, step), factors(far_near, 2 * step)),
    )
    total = None
    for b, (wave, (ur, ui)) in enumerate(blocks):
        misfit = wave - (dot(ur, c) + dot(ui, ci))
        if maybe_misfit:
            maybe_misfit[0][b] = misfit
        mt = misfit.T.astype(bf16)
        mr, mi = mt[:width], mt[width:]
        turned = jnp.concatenate([mi, -mr], axis=0)
        term = dot(mt, ur) + dot(turned, ui)
        total = term if total is None else total + term
    flat = total.T.astype(bf16)
    rank = adjoint.shape[1]
    for j in range(adjoint.shape[0]):
        adjoint[j] = flat[j * rank:(j + 1) * rank]


def updated(adjoint, x, vcat, *, group, width):
    count, rank, lanes = adjoint.shape
    rows = count // group
    a = adjoint[...].astype(f32).reshape(rows, group, rank, lanes)
    re, im = [], []
    for k in range(group // 2):
        even = a[:, 2 * k].reshape(rows * rank, lanes)
        odd = a[:, 2 * k + 1].reshape(rows * rank, lanes)
        r, i = interleave(even, odd)
        re.append(r)
        im.append(i)
    re = jnp.concatenate(re, axis=1)
    im = jnp.concatenate(im, axis=1)
    real_side = jnp.concatenate([re, -im], axis=0).astype(bf16)
    imag_side = jnp.concatenate([im, re], axis=0).astype(bf16)
    gr = dot(vcat, real_side, ((0,), (0,)))
    gi = dot(vcat, imag_side, ((0,), (0,)))
    sr = x[0] + STEP * gr
    si = x[1] + STEP * gi
    magnitude = jnp.sqrt(sr * sr + si * si)
    factor = jnp.maximum(magnitude - THRESHOLD, 0.0) / jnp.maximum(magnitude, THRESHOLD)
    return sr * factor, si * factor


def middle_kernel(adjoint, x, vfac, x_new, out, *, group, width):
    vcat = flat_factors(vfac)
    xr, xi = updated(adjoint, x, vcat, group=group, width=width)
    x_new[0] = xr
    x_new[1] = xi
    send_coeffs(vcat, xr.astype(bf16), xi.astype(bf16), out, group=group, width=width)


def last_kernel(adjoint, x, vfac, x_new, *, group, width):
    xr, xi = updated(adjoint, x, flat_factors(vfac), group=group, width=width)
    x_new[0] = xr
    x_new[1] = xi


def residual_kernel(misfit, near, far, far_near, out, *, group, width):
    q = group_index(group)

    def place(scratch):
        scratch[0] = misfit[0]
        scratch[1] = near[...]
        scratch[2] = far[0]
        scratch[3] = far_near[1]
        pieces = [scratch[jnp.bitwise_xor(q, s)] for s in range(group)]
        for k in range(group // 2):
            re, im = interleave(pieces[2 * k], pieces[2 * k + 1])
            out[0, :, 2 * width * k:2 * width * (k + 1)] = re
            out[1, :, 2 * width * k:2 * width * (k + 1)] = im

    pl.run_scoped(place, pltpu.VMEM(misfit.shape, f32))


def call(kernel, out_shape, *args, **static):
    return pl.pallas_call(
        functools.partial(kernel, **static),
        out_shape=out_shape,
        name=kernel.__name__,
    )(*args)


def body(data, x_init, ufac, vfac):
    tiles = lax.axis_size("tile")
    tile_rows, rank, _ = vfac.shape[1:]
    rows = data.shape[1]
    points = data.shape[2]
    group = tiles // tile_rows
    assert group == 4
    width = points // group
    lanes = 2 * width
    static = dict(group=group, width=width)
    shape = jax.ShapeDtypeStruct

    def exchange(value, bit):
        return lax.ppermute(value, "tile", [(s, s ^ bit) for s in range(tiles)])

    def spread(value):
        return lax.all_to_all(value, "tile", split_axis=0, concat_axis=0, tiled=True)

    wide = ufac.shape[2]
    step = rows * 2 * lanes // wide
    assert wide % (2 * lanes) == 0 and step % 16 == 0
    to_far, to_near, own = call(
        prepare_kernel,
        (
            shape((2 * rows + 2 * step, wide), bf16),
            shape((2 * rows + step, wide), bf16),
            shape((rows, lanes), f32),
        ),
        data, ufac, **static,
    )
    far = exchange(to_far, 2)
    near = exchange(to_near, 1)
    far_near = exchange(far, 1)

    chunks = shape((tiles, rank, lanes), bf16)
    coeffs = call(first_kernel, chunks, x_init, vfac, **static)
    estimate = x_init
    for iteration in range(ITERS):
        last = iteration == ITERS - 1
        outs = (chunks, shape((group, rows, lanes), f32)) if last else (chunks,)
        row = call(row_kernel, outs, spread(coeffs), own, ufac, near, far, far_near, width=width)
        if last:
            misfit = row[1]
            misfit_far = exchange(misfit[2:], 2)
            misfit_near = exchange(misfit[1], 1)
            misfit_far_near = exchange(misfit_far, 1)
        adjoint = spread(row[0])
        if last:
            estimate = call(last_kernel, shape(x_init.shape, f32), adjoint, estimate, vfac, **static)
        else:
            estimate, coeffs = call(
                middle_kernel, (shape(x_init.shape, f32), chunks), adjoint, estimate, vfac, **static
            )
    residual = call(
        residual_kernel, shape(data.shape, f32), misfit, misfit_near, misfit_far, misfit_far_near, **static
    )
    return (estimate, residual)


def solution(mesh):
    in_specs = (
        P("freq", "tile", None),
        P("freq", "tile", None),
        P("freq", "tile", None),
        P("freq", None, None, "tile"),
    )
    out_specs = (P("freq", "tile", None), P("freq", "tile", None))
    return jax.shard_map(body, mesh=mesh, in_specs=in_specs, out_specs=out_specs, check_vma=False)
```

```python
import functools

import jax
import jax.numpy as jnp
from jax import lax
from jax.experimental import pallas as pl
from jax.experimental.pallas import tpu as pltpu
from jax.sharding import PartitionSpec as P

ITERS = 2
STEP = 0.4
THRESHOLD = 0.4
VMEM_LIMIT = 24 << 20

f32 = jnp.float32
bf16 = jnp.bfloat16


def dot(a, b, dims=((1,), (0,))):
    return lax.dot_general(a, b, (dims, ((), ())), preferred_element_type=f32)


def swap_halves(a):
    return pltpu.roll(a, a.shape[1] // 2, 1)


def left_half(a):
    return lax.broadcasted_iota(jnp.int32, a.shape, 1) < a.shape[1] // 2


def times_i(a):
    s = swap_halves(a)
    return jnp.where(left_half(a), -s, s)


def interleave(re, im):
    low = left_half(re)
    return (
        jnp.where(low, re, swap_halves(im)),
        jnp.where(low, swap_halves(re), im),
    )


def slices_of(re, im, width):
    out = []
    for k in range(re.shape[1] // (2 * width)):
        cut = slice(2 * width * k, 2 * width * (k + 1))
        out.extend(interleave(re[:, cut], im[:, cut]))
    return out


def group_index(group):
    return lax.rem(lax.axis_index("tile"), group)


def prepare_kernel(data, ufac, to_far, to_near, own, *, group, width):
    rows = data.shape[1]
    folds = ufac.shape[2] // (4 * width)
    step = rows // folds
    q = group_index(group)
    stage = slices_of(data[0], data[1], width)

    def place(scratch):
        for s, block in enumerate(stage):
            scratch[jnp.bitwise_xor(q, s)] = block
        own[...] = scratch[0]

        def split(block):
            high = block.astype(bf16)
            low = (block - high.astype(f32)).astype(bf16)
            return high, low

        for ref, base, b in ((to_near, 0, 1), (to_far, 0, 2), (to_far, step, 3)):
            high, low = split(scratch[b])
            for g in range(folds):
                cut = slice(g * step, (g + 1) * step)
                lane = 4 * width * g
                ref[base:base + step, lane:lane + 2 * width] = high[cut]
                ref[base:base + step, lane + 2 * width:lane + 4 * width] = low[cut]

    pl.run_scoped(place, pltpu.VMEM((group, rows, 2 * width), f32))
    for part in range(2):
        to_near[step + rows * part:step + rows * (part + 1)] = ufac[part]
        to_far[2 * step + rows * part:2 * step + rows * (part + 1)] = ufac[part]


def send_coeffs(vcat, xr, xi, out, *, group, width):
    half = vcat.shape[0] // 2
    t1 = dot(vcat, xr)
    t2 = dot(vcat, xi)
    cr = t1[:half] + t2[half:]
    ci = t2[:half] - t1[half:]
    rank = out.shape[1]
    blocks = slices_of(cr, ci, width)
    for i in range(half // rank):
        for q in range(group):
            out[i * group + q] = blocks[q][i * rank:(i + 1) * rank].astype(bf16)


def flat_factors(vfac):
    parts, rows, rank, count = vfac.shape
    return vfac[...].reshape(parts * rows * rank, count)


def first_kernel(x, vfac, out, *, group, width):
    send_coeffs(flat_factors(vfac), x[0].astype(bf16), x[1].astype(bf16), out, group=group, width=width)


def row_kernel(coeffs, own, ufac, near, far, far_near, adjoint, *maybe_misfit, width):
    lanes = 2 * width
    rows = own.shape[0]
    c = coeffs[...].reshape(-1, lanes)
    ci = times_i(c.astype(f32)).astype(bf16)

    folds = ufac.shape[2] // (2 * lanes)
    step = rows // folds

    def joined(ref, base):
        cuts = [ref[base:base + step, 2 * lanes * g:2 * lanes * (g + 1)].astype(f32) for g in range(folds)]
        pair = jnp.concatenate(cuts, axis=0)
        return pair[:, :lanes] + pair[:, lanes:]

    def factors(ref, base):
        return ref[base:base + rows], ref[base + rows:base + 2 * rows]

    blocks = (
        (own[...], (ufac[0], ufac[1])),
        (joined(near, 0), factors(near, step)),
        (joined(far, 0), factors(far, 2 * step)),
        (joined(far_near, step), factors(far_near, 2 * step)),
    )
    total = None
    for b, (wave, (ur, ui)) in enumerate(blocks):
        misfit = wave - (dot(ur, c) + dot(ui, ci))
        if maybe_misfit:
            if b < 2:
                maybe_misfit[b][...] = misfit
            else:
                maybe_misfit[2][b - 2] = misfit
        mt = misfit.T.astype(bf16)
        mr, mi = mt[:width], mt[width:]
        turned = jnp.concatenate([mi, -mr], axis=0)
        term = dot(mt, ur) + dot(turned, ui)
        total = term if total is None else total + term
    flat = total.T.astype(bf16)
    rank = adjoint.shape[1]
    for j in range(adjoint.shape[0]):
        adjoint[j] = flat[j * rank:(j + 1) * rank]


def updated(adjoint, x, vcat, *, group, width):
    count, rank, lanes = adjoint.shape
    rows = count // group
    a = adjoint[...].astype(f32).reshape(rows, group, rank, lanes)
    re, im = [], []
    for k in range(group // 2):
        even = a[:, 2 * k].reshape(rows * rank, lanes)
        odd = a[:, 2 * k + 1].reshape(rows * rank, lanes)
        r, i = interleave(even, odd)
        re.append(r)
        im.append(i)
    re = jnp.concatenate(re, axis=1)
    im = jnp.concatenate(im, axis=1)
    real_side = jnp.concatenate([re, -im], axis=0).astype(bf16)
    imag_side = jnp.concatenate([im, re], axis=0).astype(bf16)
    gr = dot(vcat, real_side, ((0,), (0,)))
    gi = dot(vcat, imag_side, ((0,), (0,)))
    sr = x[0] + STEP * gr
    si = x[1] + STEP * gi
    magnitude = jnp.sqrt(sr * sr + si * si)
    factor = jnp.maximum(magnitude - THRESHOLD, 0.0) / jnp.maximum(magnitude, THRESHOLD)
    return sr * factor, si * factor


def middle_kernel(adjoint, x, vfac, x_new, out, *, group, width):
    vcat = flat_factors(vfac)
    xr, xi = updated(adjoint, x, vcat, group=group, width=width)
    x_new[0] = xr
    x_new[1] = xi
    send_coeffs(vcat, xr.astype(bf16), xi.astype(bf16), out, group=group, width=width)


def last_kernel(adjoint, x, vfac, x_new, *, group, width):
    def run(stage, sems):
        parts = updated(adjoint, x, flat_factors(vfac), group=group, width=width)
        copies = []
        for k, part in enumerate(parts):
            stage[k] = part
            copies.append(pltpu.make_async_copy(stage.at[k], x_new.at[k], sems.at[k]))
            copies[-1].start()
        for copy in copies:
            copy.wait()

    pl.run_scoped(run, pltpu.VMEM(x.shape, f32), pltpu.SemaphoreType.DMA((2,)))


def residual_kernel(misfit, near, far, far_near, out, *, group, width):
    q = group_index(group)

    def place(scratch, stage, sem):
        scratch[0] = misfit[...]
        scratch[1] = near[...]
        scratch[2] = far[0]
        scratch[3] = far_near[1]
        pieces = [scratch[jnp.bitwise_xor(q, s)] for s in range(group)]
        for k in range(group // 2):
            re, im = interleave(pieces[2 * k], pieces[2 * k + 1])
            stage[0, :, 2 * width * k:2 * width * (k + 1)] = re
            stage[1, :, 2 * width * k:2 * width * (k + 1)] = im
        copy = pltpu.make_async_copy(stage, out, sem)
        copy.start()
        copy.wait()

    pl.run_scoped(
        place,
        pltpu.VMEM((group,) + misfit.shape, f32),
        pltpu.VMEM(out.shape, f32),
        pltpu.SemaphoreType.DMA(()),
    )


def call(kernel, out_shape, *args, **static):
    on_chip = pl.BlockSpec(memory_space=pltpu.VMEM)
    off_chip = pl.BlockSpec(memory_space=pl.ANY)
    many = isinstance(out_shape, tuple)

    def spec(out):
        return off_chip if isinstance(out, jax.ShapeDtypeStruct) else on_chip

    return pl.pallas_call(
        functools.partial(kernel, **static),
        out_shape=out_shape,
        in_specs=[on_chip] * len(args),
        out_specs=tuple(map(spec, out_shape)) if many else spec(out_shape),
        compiler_params=pltpu.CompilerParams(vmem_limit_bytes=VMEM_LIMIT),
        name=kernel.__name__,
    )(*(pltpu.with_memory_space_constraint(arg, pltpu.VMEM) for arg in args))


def body(data, x_init, ufac, vfac):
    tiles = lax.axis_size("tile")
    tile_rows, rank, _ = vfac.shape[1:]
    rows = data.shape[1]
    points = data.shape[2]
    group = tiles // tile_rows
    assert group == 4
    width = points // group
    lanes = 2 * width
    static = dict(group=group, width=width)
    shape = pltpu.VMEM
    result = jax.ShapeDtypeStruct

    def exchange(value, bit):
        return lax.ppermute(value, "tile", [(s, s ^ bit) for s in range(tiles)])

    def spread(value):
        return lax.all_to_all(value, "tile", split_axis=0, concat_axis=0, tiled=True)

    wide = ufac.shape[2]
    step = rows * 2 * lanes // wide
    assert wide % (2 * lanes) == 0 and step % 16 == 0
    to_far, to_near, own = call(
        prepare_kernel,
        (
            shape((2 * rows + 2 * step, wide), bf16),
            shape((2 * rows + step, wide), bf16),
            shape((rows, lanes), f32),
        ),
        data, ufac, **static,
    )
    far = exchange(to_far, 2)
    near = exchange(to_near, 1)
    chunks = shape((tiles, rank, lanes), bf16)
    coeffs = call(first_kernel, chunks, x_init, vfac, **static)
    far_near = exchange(lax.optimization_barrier((far, coeffs))[0], 1)
    estimate = x_init
    for iteration in range(ITERS):
        last = iteration == ITERS - 1
        block = shape((rows, lanes), f32)
        outs = (chunks, block, block, shape((2, rows, lanes), f32)) if last else (chunks,)
        row = call(row_kernel, outs, spread(coeffs), own, ufac, near, far, far_near, width=width)
        if last:
            _, misfit, to_near, to_far = row
            misfit_far = exchange(to_far, 2)
            misfit_near = exchange(to_near, 1)
            misfit_far_near = exchange(misfit_far, 1)
        adjoint = spread(row[0])
        if last:
            estimate = call(last_kernel, result(x_init.shape, f32), adjoint, estimate, vfac, **static)
        else:
            estimate, coeffs = call(
                middle_kernel, (shape(x_init.shape, f32), chunks), adjoint, estimate, vfac, **static
            )
    residual = call(
        residual_kernel, result(data.shape, f32), misfit, misfit_near, misfit_far, misfit_far_near, **static
    )
    return (estimate, residual)


def solution(mesh):
    in_specs = (
        P("freq", "tile", None),
        P("freq", "tile", None),
        P("freq", "tile", None),
        P("freq", None, None, "tile"),
    )
    out_specs = (P("freq", "tile", None), P("freq", "tile", None))
    return jax.shard_map(body, mesh=mesh, in_specs=in_specs, out_specs=out_specs, check_vma=False)
```

```python
import functools

import jax
import jax.numpy as jnp
from jax import lax
from jax.experimental import pallas as pl
from jax.experimental.pallas import tpu as pltpu
from jax.sharding import PartitionSpec as P


ITERS = 2
STEP = 0.4
THRESHOLD = 0.4
VMEM_LIMIT = 24 << 20
PIECES = 4

f32 = jnp.float32
bf16 = jnp.bfloat16


def dot(a, b, dims=((1,), (0,))):
    return lax.dot_general(a, b, (dims, ((), ())), preferred_element_type=f32)


def swap_halves(a):
    return pltpu.roll(a, a.shape[1] // 2, 1)


def left_half(a):
    return lax.broadcasted_iota(jnp.int32, a.shape, 1) < a.shape[1] // 2


def times_i(a):
    s = swap_halves(a)
    return jnp.where(left_half(a), -s, s)


def interleave(re, im):
    low = left_half(re)
    return (
        jnp.where(low, re, swap_halves(im)),
        jnp.where(low, swap_halves(re), im),
    )


def slices_of(re, im, width):
    out = []
    for k in range(re.shape[1] // (2 * width)):
        cut = slice(2 * width * k, 2 * width * (k + 1))
        out.extend(interleave(re[:, cut], im[:, cut]))
    return out


def group_index(group):
    return lax.rem(lax.axis_index("tile"), group)


def split(block):
    high = block.astype(bf16)
    low = (block - high.astype(f32)).astype(bf16)
    return high, low


def send_coeffs(vcat, xr, xi, out, *, group, width):
    half = vcat.shape[0] // 2
    t1 = dot(vcat, xr)
    t2 = dot(vcat, xi)
    cr = t1[:half] + t2[half:]
    ci = t2[:half] - t1[half:]
    rank = out.shape[1]
    blocks = slices_of(cr, ci, width)
    for i in range(half // rank):
        for q in range(group):
            out[i * group + q] = blocks[q][i * rank:(i + 1) * rank].astype(bf16)


def flat_factors(vfac, cut=slice(None)):
    parts, rows, rank, _ = vfac.shape
    return vfac[:, :, :, cut].reshape(parts * rows * rank, -1)


def first_kernel(data, x, ufac, vfac, to_far, to_near, own, u_own, x_own, v_own, out, *, group, width):
    rows = data.shape[1]
    folds = ufac.shape[2] // (4 * width)
    step = rows // folds
    q = group_index(group)

    def run(waves, scratch, sems):
        wave_copy = pltpu.make_async_copy(data, waves, sems.at[0])
        v_copy = pltpu.make_async_copy(vfac, v_own, sems.at[1])
        u_copy = pltpu.make_async_copy(ufac, u_own, sems.at[2])
        x_copy = pltpu.make_async_copy(x, x_own, sems.at[3])
        for copy in (wave_copy, u_copy, v_copy, x_copy):
            copy.start()
        wave_copy.wait()
        for s, block in enumerate(slices_of(waves[0], waves[1], width)):
            scratch[jnp.bitwise_xor(q, s)] = block
        own[...] = scratch[0]
        for ref, base, b in ((to_near, 0, 1), (to_far, 0, 2), (to_far, step, 3)):
            high, low = split(scratch[b])
            for g in range(folds):
                cut = slice(g * step, (g + 1) * step)
                lane = 4 * width * g
                ref[base:base + step, lane:lane + 2 * width] = high[cut]
                ref[base:base + step, lane + 2 * width:lane + 4 * width] = low[cut]
        u_copy.wait()
        for part in range(2):
            to_near[step + rows * part:step + rows * (part + 1)] = u_own[part]
            to_far[2 * step + rows * part:2 * step + rows * (part + 1)] = u_own[part]
        v_copy.wait()
        x_copy.wait()
        send_coeffs(
            flat_factors(v_own), x_own[0].astype(bf16), x_own[1].astype(bf16), out, group=group, width=width
        )

    pl.run_scoped(
        run,
        pltpu.VMEM(data.shape, f32),
        pltpu.VMEM((group, rows, 2 * width), f32),
        pltpu.SemaphoreType.DMA((4,)),
    )


def row_kernel(coeffs, own, ufac, near, far, far_near, adjoint, *maybe_misfit, width):
    lanes = 2 * width
    rows = own.shape[0]
    c = coeffs[...].reshape(-1, lanes)
    ci = times_i(c.astype(f32)).astype(bf16)

    folds = ufac.shape[2] // (2 * lanes)
    step = rows // folds

    def joined(ref, base):
        cuts = [ref[base:base + step, 2 * lanes * g:2 * lanes * (g + 1)].astype(f32) for g in range(folds)]
        pair = jnp.concatenate(cuts, axis=0)
        return pair[:, :lanes] + pair[:, lanes:]

    def factors(ref, base):
        return ref[base:base + rows], ref[base + rows:base + 2 * rows]

    blocks = (
        (own[...], (ufac[0], ufac[1])),
        (joined(near, 0), factors(near, step)),
        (joined(far, 0), factors(far, 2 * step)),
        (joined(far_near, step), factors(far_near, 2 * step)),
    )
    total = None
    for b, (wave, (ur, ui)) in enumerate(blocks):
        misfit = wave - (dot(ur, c) + dot(ui, ci))
        if maybe_misfit:
            if b < 2:
                maybe_misfit[b][...] = misfit
            else:
                maybe_misfit[2][b - 2] = misfit
        mt = misfit.T.astype(bf16)
        mr, mi = mt[:width], mt[width:]
        turned = jnp.concatenate([mi, -mr], axis=0)
        term = dot(mt, ur) + dot(turned, ui)
        total = term if total is None else total + term
    flat = total.T.astype(bf16)
    rank = adjoint.shape[1]
    for j in range(adjoint.shape[0]):
        adjoint[j] = flat[j * rank:(j + 1) * rank]


def adjoint_sides(adjoint, *, group):
    count, rank, lanes = adjoint.shape
    rows = count // group
    a = adjoint[...].astype(f32).reshape(rows, group, rank, lanes)
    re, im = [], []
    for k in range(group // 2):
        even = a[:, 2 * k].reshape(rows * rank, lanes)
        odd = a[:, 2 * k + 1].reshape(rows * rank, lanes)
        r, i = interleave(even, odd)
        re.append(r)
        im.append(i)
    re = jnp.concatenate(re, axis=1)
    im = jnp.concatenate(im, axis=1)
    real_side = jnp.concatenate([re, -im], axis=0).astype(bf16)
    imag_side = jnp.concatenate([im, re], axis=0).astype(bf16)
    return real_side, imag_side


def shrink(sr, si):
    magnitude = jnp.sqrt(sr * sr + si * si)
    factor = jnp.maximum(magnitude - THRESHOLD, 0.0) / jnp.maximum(magnitude, THRESHOLD)
    return sr * factor, si * factor


def updated(sides, xr, xi, vcat):
    gr, gi = (dot(vcat, side, ((0,), (0,))) for side in sides)
    return shrink(xr + STEP * gr, xi + STEP * gi)


def middle_kernel(adjoint, x, vfac, x_new, out, *, group, width):
    vcat = flat_factors(vfac)
    xr, xi = updated(adjoint_sides(adjoint, group=group), x[0], x[1], vcat)
    x_new[0] = xr
    x_new[1] = xi
    send_coeffs(vcat, xr.astype(bf16), xi.astype(bf16), out, group=group, width=width)


def last_kernel(adjoint, x, vfac, x_new, *, group, width):
    sources = x.shape[1]
    piece = sources // PIECES

    def run(stage, sems):
        sides = adjoint_sides(adjoint, group=group)
        copies = []
        for k in range(PIECES):
            cut = slice(k * piece, (k + 1) * piece)
            stage[0, cut], stage[1, cut] = updated(sides, x[0, cut], x[1, cut], flat_factors(vfac, cut))
            copies.append(pltpu.make_async_copy(stage.at[:, cut], x_new.at[:, cut], sems.at[k]))
            copies[-1].start()
        for copy in copies:
            copy.wait()

    pl.run_scoped(run, pltpu.VMEM(x.shape, f32), pltpu.SemaphoreType.DMA((PIECES,)))


def residual_kernel(misfit, near, far, far_near, out, *, group, width):
    q = group_index(group)

    def place(scratch, stage, sem):
        scratch[0] = misfit[...]
        scratch[1] = near[...]
        scratch[2] = far[0]
        scratch[3] = far_near[1]
        pieces = [scratch[jnp.bitwise_xor(q, s)] for s in range(group)]
        for k in range(group // 2):
            re, im = interleave(pieces[2 * k], pieces[2 * k + 1])
            stage[0, :, 2 * width * k:2 * width * (k + 1)] = re
            stage[1, :, 2 * width * k:2 * width * (k + 1)] = im
        copy = pltpu.make_async_copy(stage, out, sem)
        copy.start()
        copy.wait()

    pl.run_scoped(
        place,
        pltpu.VMEM((group,) + misfit.shape, f32),
        pltpu.VMEM(out.shape, f32),
        pltpu.SemaphoreType.DMA(()),
    )


def call(kernel, out_shape, *args, from_hbm=False, **static):
    on_chip = pl.BlockSpec(memory_space=pltpu.VMEM)
    off_chip = pl.BlockSpec(memory_space=pltpu.HBM)
    space = pltpu.HBM if from_hbm else pltpu.VMEM
    many = isinstance(out_shape, tuple)

    def spec(out):
        return off_chip if isinstance(out, jax.ShapeDtypeStruct) else on_chip

    return pl.pallas_call(
        functools.partial(kernel, **static),
        out_shape=out_shape,
        in_specs=[off_chip if from_hbm else on_chip] * len(args),
        out_specs=tuple(map(spec, out_shape)) if many else spec(out_shape),
        compiler_params=pltpu.CompilerParams(vmem_limit_bytes=VMEM_LIMIT),
    )(*(pltpu.with_memory_space_constraint(arg, space) for arg in args))


def body(data, x_init, ufac, vfac):
    tiles = lax.axis_size("tile")
    tile_rows, rank, _ = vfac.shape[1:]
    rows = data.shape[1]
    points = data.shape[2]
    group = tiles // tile_rows
    assert group == 4
    width = points // group
    lanes = 2 * width
    static = dict(group=group, width=width)
    shape = pltpu.VMEM
    result = jax.ShapeDtypeStruct

    def exchange(value, bit):
        return lax.ppermute(value, "tile", [(s, s ^ bit) for s in range(tiles)])

    def spread(value):
        return lax.all_to_all(value, "tile", split_axis=0, concat_axis=0, tiled=True)

    wide = ufac.shape[2]
    step = rows * 2 * lanes // wide
    assert wide % (2 * lanes) == 0 and step % 16 == 0
    chunks = shape((tiles, rank, lanes), bf16)
    to_far, to_near, own, ufac, estimate, vfac, coeffs = call(
        first_kernel,
        (
            shape((2 * rows + 2 * step, wide), bf16),
            shape((2 * rows + step, wide), bf16),
            shape((rows, lanes), f32),
            shape(ufac.shape, bf16),
            shape(x_init.shape, f32),
            shape(vfac.shape, bf16),
            chunks,
        ),
        data, x_init, ufac, vfac, from_hbm=True, **static,
    )
    far = exchange(to_far, 2)
    near = exchange(to_near, 1)
    far_near = exchange(far, 1)
    for iteration in range(ITERS):
        last = iteration == ITERS - 1
        block = shape((rows, lanes), f32)
        outs = (chunks, block, block, shape((2, rows, lanes), f32)) if last else (chunks,)
        row = call(row_kernel, outs, spread(coeffs), own, ufac, near, far, far_near, width=width)
        if last:
            _, misfit, to_near, to_far = row
            misfit_far = exchange(to_far, 2)
            misfit_near = exchange(to_near, 1)
            misfit_far_near = exchange(misfit_far, 1)
        adjoint = spread(row[0])
        if last:
            estimate = call(last_kernel, result(x_init.shape, f32), adjoint, estimate, vfac, **static)
        else:
            estimate, coeffs = call(
                middle_kernel, (shape(x_init.shape, f32), chunks), adjoint, estimate, vfac, **static
            )
    residual = call(
        residual_kernel, result(data.shape, f32), misfit, misfit_near, misfit_far, misfit_far_near, **static
    )
    return (estimate, residual)


def solution(mesh):
    in_specs = (
        P("freq", "tile", None),
        P("freq", "tile", None),
        P("freq", "tile", None),
        P("freq", None, None, "tile"),
    )
    out_specs = (P("freq", "tile", None), P("freq", "tile", None))
    return jax.shard_map(body, mesh=mesh, in_specs=in_specs, out_specs=out_specs, check_vma=False)
```

```python
import functools

import jax
import jax.numpy as jnp
from jax import lax
from jax.experimental import pallas as pl
from jax.experimental.pallas import tpu as pltpu
from jax.sharding import PartitionSpec as P


STEP = 0.4
THRESHOLD = 0.4
VMEM_LIMIT = 24 << 20
PIECES = 4

f32 = jnp.float32
bf16 = jnp.bfloat16


def dot(a, b, dims=((1,), (0,))):
    return lax.dot_general(a, b, (dims, ((), ())), preferred_element_type=f32)


def swap_halves(a):
    return pltpu.roll(a, a.shape[1] // 2, 1)


def left_half(a):
    return lax.broadcasted_iota(jnp.int32, a.shape, 1) < a.shape[1] // 2


def times_i(a):
    s = swap_halves(a)
    return jnp.where(left_half(a), -s, s)


def interleave(re, im):
    low = left_half(re)
    return (
        jnp.where(low, re, swap_halves(im)),
        jnp.where(low, swap_halves(re), im),
    )


def slices_of(re, im, width):
    out = []
    for k in range(re.shape[1] // (2 * width)):
        cut = slice(2 * width * k, 2 * width * (k + 1))
        out.extend(interleave(re[:, cut], im[:, cut]))
    return out


def group_index(group):
    return lax.rem(lax.axis_index("tile"), group)


def row_index(group):
    return lax.div(lax.axis_index("tile"), group)


def split(block):
    high = block.astype(bf16)
    low = (block - high.astype(f32)).astype(bf16)
    return high, low


def send_coeffs(vcat, xr, xi, out, *, group, width):
    half = vcat.shape[0] // 2
    t1 = dot(vcat, xr)
    t2 = dot(vcat, xi)
    cr = t1[:half] + t2[half:]
    ci = t2[:half] - t1[half:]
    rank = out.shape[1]
    blocks = slices_of(cr, ci, width)
    for i in range(half // rank):
        for q in range(group):
            out[i * group + q] = blocks[q][i * rank:(i + 1) * rank].astype(bf16)


def flat_factors(vfac, cut=slice(None)):
    parts, rows, rank, _ = vfac.shape
    return vfac[:, :, :, cut].reshape(parts * rows * rank, -1)


def first_kernel(data, x, ufac, vfac, to_far, to_near, own, u_own, x_own, v_own, out, *, group, width):
    rows = data.shape[1]
    folds = ufac.shape[2] // (4 * width)
    step = rows // folds
    q = group_index(group)

    def run(waves, scratch, sems):
        wave_copy = pltpu.make_async_copy(data, waves, sems.at[0])
        v_copy = pltpu.make_async_copy(vfac, v_own, sems.at[1])
        u_copy = pltpu.make_async_copy(ufac, u_own, sems.at[2])
        x_copy = pltpu.make_async_copy(x, x_own, sems.at[3])
        for copy in (wave_copy, u_copy, v_copy, x_copy):
            copy.start()
        wave_copy.wait()
        for s, block in enumerate(slices_of(waves[0], waves[1], width)):
            scratch[jnp.bitwise_xor(q, s)] = block
        own[...] = scratch[0]
        for ref, base, b in ((to_near, 0, 1), (to_far, 0, 2), (to_far, step, 3)):
            high, low = split(scratch[b])
            for g in range(folds):
                cut = slice(g * step, (g + 1) * step)
                lane = 4 * width * g
                ref[base:base + step, lane:lane + 2 * width] = high[cut]
                ref[base:base + step, lane + 2 * width:lane + 4 * width] = low[cut]
        u_copy.wait()
        for part in range(2):
            to_near[step + rows * part:step + rows * (part + 1)] = u_own[part]
            to_far[2 * step + rows * part:2 * step + rows * (part + 1)] = u_own[part]
        v_copy.wait()
        x_copy.wait()
        send_coeffs(
            flat_factors(v_own), x_own[0].astype(bf16), x_own[1].astype(bf16), out, group=group, width=width
        )

    pl.run_scoped(
        run,
        pltpu.VMEM(data.shape, f32),
        pltpu.VMEM((group, rows, 2 * width), f32),
        pltpu.SemaphoreType.DMA((4,)),
    )


def row_core(c, own, ufac, near, far, corner, misfits, width):
    lanes = 2 * width
    rows = own.shape[0]
    ci = times_i(c.astype(f32)).astype(bf16)
    folds = ufac.shape[2] // (2 * lanes)
    step = rows // folds

    def joined(ref, base):
        cuts = [ref[base:base + step, 2 * lanes * g:2 * lanes * (g + 1)].astype(f32) for g in range(folds)]
        pair = jnp.concatenate(cuts, axis=0)
        return pair[:, :lanes] + pair[:, lanes:]

    def factors(ref, base):
        return ref[base:base + rows], ref[base + rows:base + 2 * rows]

    blocks = (
        (own[...], (ufac[0], ufac[1])),
        (joined(near, 0), factors(near, step)),
        (joined(far, 0), factors(far, 2 * step)),
        (joined(corner, step), factors(corner, 2 * step)),
    )
    total = None
    for b, (wave, (ur, ui)) in enumerate(blocks):
        misfit = wave - (dot(ur, c) + dot(ui, ci))
        if misfits and b < 2:
            misfits[b][...] = misfit
        elif misfits:
            misfits[2][b - 2] = misfit
        mt = misfit.T.astype(bf16)
        mr, mi = mt[:width], mt[width:]
        turned = jnp.concatenate([mi, -mr], axis=0)
        term = dot(mt, ur) + dot(turned, ui)
        total = term if total is None else total + term
    return total.T.astype(bf16)


def to_chunks(flat, adjoint):
    rank = adjoint.shape[1]
    for j in range(adjoint.shape[0]):
        adjoint[j] = flat[j * rank:(j + 1) * rank]


def row_kernel(coeffs, own, ufac, near, far, corner, adjoint, *misfits, width):
    c = coeffs[...].reshape(-1, 2 * width)
    to_chunks(row_core(c, own, ufac, near, far, corner, misfits, width), adjoint)


def row_first_kernel(coeffs, own, ufac, near, far, corner, *pieces, group, width):
    z = row_index(group)
    rank = coeffs.shape[1]
    c = coeffs[...].reshape(-1, 2 * width)
    flat = row_core(c, own, ufac, near, far, corner, (), width)

    def place(scratch):
        for j in range(flat.shape[0] // rank):
            scratch[jnp.bitwise_xor(z, j // group), j % group] = flat[j * rank:(j + 1) * rank]
        for b, piece in enumerate(pieces):
            piece[...] = scratch[b]

    pl.run_scoped(place, pltpu.VMEM((len(pieces),) + pieces[0].shape, bf16))


def row_last_kernel(*refs, group, width, count):
    pieces, (own, ufac, near, far, corner, adjoint), misfits = refs[:count], refs[count:count + 6], refs[count + 6:]
    z = row_index(group)

    def run(scratch):
        for b, piece in enumerate(pieces):
            scratch[jnp.bitwise_xor(z, b)] = piece[...]
        c = scratch[...].reshape(-1, 2 * width)
        to_chunks(row_core(c, own, ufac, near, far, corner, misfits, width), adjoint)

    pl.run_scoped(run, pltpu.VMEM((count,) + pieces[0].shape, bf16))


def pack_kernel(x, vfac, to_far, to_near, own, *, group, width):
    q = group_index(group)
    sources = x.shape[1]
    lanes = 2 * width
    vcat = flat_factors(vfac)
    tall = vcat.shape[0]

    def place(scratch):
        for s, block in enumerate(slices_of(x[0], x[1], width)):
            scratch[jnp.bitwise_xor(q, s)] = block.astype(bf16)
        own[...] = scratch[0]
        to_near[:sources] = scratch[1]
        to_far[:sources, :lanes] = scratch[2]
        to_far[:sources, lanes:] = scratch[3]

    pl.run_scoped(place, pltpu.VMEM((group, sources, lanes), bf16))
    for ref in (to_near, to_far):
        wide = ref.shape[1]
        for h in range(sources // wide):
            ref[sources + h * tall:sources + (h + 1) * tall] = flat_factors(vfac, slice(h * wide, (h + 1) * wide))


def middle_columns_kernel(*refs, group, width, count):
    pieces, refs = refs[:count], refs[count:]
    (x_own, v_own, near, far, corner), refs = refs[:5], refs[5:]
    outs, (adj_own, adj_near, adj_far) = refs[:count], refs[count:]
    q = group_index(group)
    z = row_index(group)
    sources, lanes = x_own.shape
    rank = pieces[0].shape[1]
    side = count * rank
    tall = 2 * side

    def factors(ref):
        wide = ref.shape[1]
        cuts = [ref[sources + h * tall:sources + (h + 1) * tall] for h in range(sources // wide)]
        return jnp.concatenate(cuts, axis=1)

    def run(adj, coeffs):
        for b, piece in enumerate(pieces):
            for k in range(group):
                adj[k, jnp.bitwise_xor(z, b)] = piece[jnp.bitwise_xor(q, k)]
        columns = (
            (x_own[...], flat_factors(v_own)),
            (near[:sources], factors(near)),
            (far[:sources, :lanes], factors(far)),
            (corner[:sources, lanes:], factors(corner)),
        )
        for k, (x, vcat) in enumerate(columns):
            a = adj[k].reshape(side, lanes)
            if k == 0:
                adj_own[...] = a
            elif k == 1:
                adj_near[...] = a
            else:
                adj_far[k - 2] = a
            turned = times_i(a.astype(f32)).astype(bf16)
            s = x.astype(f32) + STEP * dot(vcat, jnp.concatenate([a, turned], axis=0), ((0,), (0,)))
            square = s * s
            magnitude = jnp.sqrt(square + swap_halves(square))
            factor = jnp.maximum(magnitude - THRESHOLD, 0.0) / jnp.maximum(magnitude, THRESHOLD)
            t = dot(vcat, (s * factor).astype(bf16))
            c = (t[:side] - times_i(t[side:])).astype(bf16)
            for i in range(count):
                coeffs[i, jnp.bitwise_xor(q, k)] = c[i * rank:(i + 1) * rank]
        for b, out in enumerate(outs):
            out[...] = coeffs[jnp.bitwise_xor(z, b)]

    pl.run_scoped(
        run,
        pltpu.VMEM((group, count, rank, lanes), bf16),
        pltpu.VMEM((count, group, rank, lanes), bf16),
    )


def own_column_kernel(adj_own, adj_near, adj_far, adj_corner, x, vfac, x_new, *, group, width):
    q = group_index(group)

    def run(scratch):
        scratch[0] = adj_own[...]
        scratch[1] = adj_near[...]
        scratch[2] = adj_far[0]
        scratch[3] = adj_corner[1]
        sides = sides_of([scratch[jnp.bitwise_xor(q, s)].astype(f32) for s in range(group)])
        x_new[0], x_new[1] = updated(sides, x[0], x[1], flat_factors(vfac))

    pl.run_scoped(run, pltpu.VMEM((group,) + adj_own.shape, bf16))


def sides_of(quarters):
    pairs = [interleave(*quarters[k:k + 2]) for k in range(0, len(quarters), 2)]
    re = jnp.concatenate([r for r, _ in pairs], axis=1)
    im = jnp.concatenate([i for _, i in pairs], axis=1)
    real_side = jnp.concatenate([re, -im], axis=0).astype(bf16)
    imag_side = jnp.concatenate([im, re], axis=0).astype(bf16)
    return real_side, imag_side


def adjoint_sides(adjoint, *, group):
    count, rank, lanes = adjoint.shape
    rows = count // group
    a = adjoint[...].astype(f32).reshape(rows, group, rank, lanes)
    return sides_of([a[:, s].reshape(rows * rank, lanes) for s in range(group)])


def shrink(sr, si):
    magnitude = jnp.sqrt(sr * sr + si * si)
    factor = jnp.maximum(magnitude - THRESHOLD, 0.0) / jnp.maximum(magnitude, THRESHOLD)
    return sr * factor, si * factor


def updated(sides, xr, xi, vcat):
    gr, gi = (dot(vcat, side, ((0,), (0,))) for side in sides)
    return shrink(xr + STEP * gr, xi + STEP * gi)


def middle_kernel(adjoint, x, vfac, x_new, out, *, group, width):
    vcat = flat_factors(vfac)
    xr, xi = updated(adjoint_sides(adjoint, group=group), x[0], x[1], vcat)
    x_new[0] = xr
    x_new[1] = xi
    send_coeffs(vcat, xr.astype(bf16), xi.astype(bf16), out, group=group, width=width)


def last_kernel(adjoint, x, vfac, x_new, *, group, width):
    sources = x.shape[1]
    piece = sources // PIECES

    def run(stage, sems):
        sides = adjoint_sides(adjoint, group=group)
        copies = []
        for k in range(PIECES):
            cut = slice(k * piece, (k + 1) * piece)
            stage[0, cut], stage[1, cut] = updated(sides, x[0, cut], x[1, cut], flat_factors(vfac, cut))
            copies.append(pltpu.make_async_copy(stage.at[:, cut], x_new.at[:, cut], sems.at[k]))
            copies[-1].start()
        for copy in copies:
            copy.wait()

    pl.run_scoped(run, pltpu.VMEM(x.shape, f32), pltpu.SemaphoreType.DMA((PIECES,)))


def residual_kernel(misfit, near, far, far_near, out, *, group, width):
    q = group_index(group)

    def place(scratch, stage, sem):
        scratch[0] = misfit[...]
        scratch[1] = near[...]
        scratch[2] = far[0]
        scratch[3] = far_near[1]
        pieces = [scratch[jnp.bitwise_xor(q, s)] for s in range(group)]
        for k in range(group // 2):
            re, im = interleave(pieces[2 * k], pieces[2 * k + 1])
            stage[0, :, 2 * width * k:2 * width * (k + 1)] = re
            stage[1, :, 2 * width * k:2 * width * (k + 1)] = im
        copy = pltpu.make_async_copy(stage, out, sem)
        copy.start()
        copy.wait()

    pl.run_scoped(
        place,
        pltpu.VMEM((group,) + misfit.shape, f32),
        pltpu.VMEM(out.shape, f32),
        pltpu.SemaphoreType.DMA(()),
    )


def call(kernel, out_shape, *args, from_hbm=False, **static):
    on_chip = pl.BlockSpec(memory_space=pltpu.VMEM)
    off_chip = pl.BlockSpec(memory_space=pltpu.HBM)
    space = pltpu.HBM if from_hbm else pltpu.VMEM
    many = isinstance(out_shape, tuple)

    def spec(out):
        return off_chip if isinstance(out, jax.ShapeDtypeStruct) else on_chip

    return pl.pallas_call(
        functools.partial(kernel, **static),
        out_shape=out_shape,
        in_specs=[off_chip if from_hbm else on_chip] * len(args),
        out_specs=tuple(map(spec, out_shape)) if many else spec(out_shape),
        compiler_params=pltpu.CompilerParams(vmem_limit_bytes=VMEM_LIMIT),
    )(*(pltpu.with_memory_space_constraint(arg, space) for arg in args))


def body(data, x_init, ufac, vfac):
    tiles = lax.axis_size("tile")
    tile_rows, rank, _ = vfac.shape[1:]
    rows = data.shape[1]
    points = data.shape[2]
    group = tiles // tile_rows
    assert group == 4
    width = points // group
    lanes = 2 * width
    static = dict(group=group, width=width)
    shape = pltpu.VMEM
    result = jax.ShapeDtypeStruct

    def exchange(value, bit):
        return lax.ppermute(value, "tile", [(s, s ^ bit) for s in range(tiles)])

    def spread(value):
        return lax.all_to_all(value, "tile", split_axis=0, concat_axis=0, tiled=True)

    wide = ufac.shape[2]
    step = rows * 2 * lanes // wide
    assert wide % (2 * lanes) == 0 and step % 16 == 0
    chunks = shape((tiles, rank, lanes), bf16)
    to_far, to_near, own, ufac, estimate, vfac, coeffs = call(
        first_kernel,
        (
            shape((2 * rows + 2 * step, wide), bf16),
            shape((2 * rows + step, wide), bf16),
            shape((rows, lanes), f32),
            shape(ufac.shape, bf16),
            shape(x_init.shape, f32),
            shape(vfac.shape, bf16),
            chunks,
        ),
        data, x_init, ufac, vfac, from_hbm=True, **static,
    )
    far = exchange(to_far, 2)
    near = exchange(to_near, 1)
    corner = exchange(far, 1)
    gathered = (own, ufac, near, far, corner)
    block = shape((rows, lanes), f32)
    row_outs = (chunks, block, block, shape((2, rows, lanes), f32))
    received = spread(coeffs)
    if tile_rows == 4:
        sources = x_init.shape[1]
        tall = 2 * tile_rows * rank
        piece = shape((group, rank, lanes), bf16)
        side = (tile_rows * rank, lanes)
        counted = dict(count=tile_rows, **static)

        def along_rows(pieces):
            order = {b: exchange(pieces[b], b * group) for b in range(tile_rows - 1, 0, -1)}
            return [pieces[0]] + [order[b] for b in range(1, tile_rows)]

        x_far, x_near, x_own = call(
            pack_kernel,
            (
                shape((sources + tall * sources // (2 * lanes), 2 * lanes), bf16),
                shape((sources + tall * sources // lanes, lanes), bf16),
                shape((sources, lanes), bf16),
            ),
            estimate, vfac, **static,
        )
        x_far = exchange(x_far, 2)
        x_near = exchange(x_near, 1)
        x_corner = exchange(x_far, 1)
        pieces = call(row_first_kernel, (piece,) * tile_rows, received, *gathered, **static)
        pieces = along_rows(pieces)
        *pieces, adj_own, adj_near, adj_far = call(
            middle_columns_kernel,
            (piece,) * tile_rows + (shape(side, bf16), shape(side, bf16), shape((2,) + side, bf16)),
            *pieces, x_own, vfac, x_near, x_far, x_corner, **counted,
        )
        pieces = along_rows(pieces)
        adj_far = exchange(adj_far, 2)
        adj_near = exchange(adj_near, 1)
        adj_corner = exchange(adj_far, 1)
        row = call(row_last_kernel, row_outs, *pieces, *gathered, **counted)
        estimate = call(
            own_column_kernel, shape(x_init.shape, f32),
            adj_own, adj_near, adj_far, adj_corner, estimate, vfac, **static,
        )
    else:
        (pieces,) = call(row_kernel, (chunks,), received, *gathered, width=width)
        estimate, coeffs = call(
            middle_kernel, (shape(x_init.shape, f32), chunks), spread(pieces), estimate, vfac, **static
        )
        row = call(row_kernel, row_outs, spread(coeffs), *gathered, width=width)
    adjoint, misfit, to_near, to_far = row
    misfit_far = exchange(to_far, 2)
    misfit_near = exchange(to_near, 1)
    misfit_corner = exchange(misfit_far, 1)
    adjoint = spread(adjoint)
    solved = call(last_kernel, result(x_init.shape, f32), adjoint, estimate, vfac, **static)
    residual = call(
        residual_kernel, result(data.shape, f32), misfit, misfit_near, misfit_far, misfit_corner, **static
    )
    return (solved, residual)


def solution(mesh):
    in_specs = (
        P("freq", "tile", None),
        P("freq", "tile", None),
        P("freq", "tile", None),
        P("freq", None, None, "tile"),
    )
    out_specs = (P("freq", "tile", None), P("freq", "tile", None))
    return jax.shard_map(body, mesh=mesh, in_specs=in_specs, out_specs=out_specs, check_vma=False)
```

```python
import functools

import jax
import jax.numpy as jnp
from jax import lax
from jax.experimental import pallas as pl
from jax.experimental.pallas import tpu as pltpu
from jax.sharding import PartitionSpec as P


STEP = 0.4
THRESHOLD = 0.4
VMEM_LIMIT = 24 << 20
PIECES = 4
GATHERED = 8

f32 = jnp.float32
bf16 = jnp.bfloat16


def dot(a, b, dims=((1,), (0,))):
    return lax.dot_general(a, b, (dims, ((), ())), preferred_element_type=f32)


def swap_halves(a):
    return pltpu.roll(a, a.shape[1] // 2, 1)


def left_half(a):
    return lax.broadcasted_iota(jnp.int32, a.shape, 1) < a.shape[1] // 2


def times_i(a):
    s = swap_halves(a)
    return jnp.where(left_half(a), -s, s)


def interleave(re, im):
    low = left_half(re)
    return (
        jnp.where(low, re, swap_halves(im)),
        jnp.where(low, swap_halves(re), im),
    )


def slices_of(re, im, width):
    out = []
    for k in range(re.shape[1] // (2 * width)):
        cut = slice(2 * width * k, 2 * width * (k + 1))
        out.extend(interleave(re[:, cut], im[:, cut]))
    return out


def group_index(group):
    return lax.rem(lax.axis_index("tile"), group)


def row_index(group):
    return lax.div(lax.axis_index("tile"), group)


def split(block):
    high = block.astype(bf16)
    low = (block - high.astype(f32)).astype(bf16)
    return high, low


def send_coeffs(vcat, xr, xi, out, *, group, width):
    half = vcat.shape[0] // 2
    t1 = dot(vcat, xr)
    t2 = dot(vcat, xi)
    cr = t1[:half] + t2[half:]
    ci = t2[:half] - t1[half:]
    rank = out.shape[1]
    blocks = slices_of(cr, ci, width)
    for i in range(half // rank):
        for q in range(group):
            out[i * group + q] = blocks[q][i * rank:(i + 1) * rank].astype(bf16)


def flat_factors(vfac, cut=slice(None)):
    parts, rows, rank, _ = vfac.shape
    return vfac[:, :, :, cut].reshape(parts * rows * rank, -1)


def first_kernel(data, x, ufac, vfac, to_far, to_near, own, u_own, x_own, v_own, out, *, group, width):
    rows = data.shape[1]
    lanes = 2 * width
    q = group_index(group)

    def run(waves, scratch, sems):
        wave_copy = pltpu.make_async_copy(data, waves, sems.at[0])
        v_copy = pltpu.make_async_copy(vfac, v_own, sems.at[1])
        u_copy = pltpu.make_async_copy(ufac, u_own, sems.at[2])
        x_copy = pltpu.make_async_copy(x, x_own, sems.at[3])
        for copy in (wave_copy, x_copy, v_copy, u_copy):
            copy.start()
        wave_copy.wait()
        for s, block in enumerate(slices_of(waves[0], waves[1], width)):
            scratch[jnp.bitwise_xor(q, s)] = block
        own[...] = scratch[0]
        for ref, base, b in ((to_near, 0, 1), (to_far, 0, 2), (to_far, rows, 3)):
            high, low = split(scratch[b])
            ref[base:base + rows, :lanes] = high
            ref[base:base + rows, lanes:] = low
        v_copy.wait()
        x_copy.wait()
        send_coeffs(
            flat_factors(v_own), x_own[0].astype(bf16), x_own[1].astype(bf16), out, group=group, width=width
        )
        u_copy.wait()

    pl.run_scoped(
        run,
        pltpu.VMEM(data.shape, f32),
        pltpu.VMEM((group, rows, lanes), f32),
        pltpu.SemaphoreType.DMA((4,)),
    )


def row_core(c, gathered, misfits, width):
    own, *pieces = gathered
    lanes = 2 * width
    rows = own.shape[0]
    ci = times_i(c.astype(f32)).astype(bf16)

    def joined(ref, base):
        pair = ref[base:base + rows].astype(f32)
        return pair[:, :lanes] + pair[:, lanes:]

    u_own, near, u_near, far, u_far, corner, u_corner = pieces
    blocks = (
        (own[...], u_own[...]),
        (joined(near, 0), u_near[...]),
        (joined(far, 0), u_far[...]),
        (joined(corner, rows), u_corner[...]),
    )
    total = None
    for b, (wave, (ur, ui)) in enumerate(blocks):
        misfit = wave - (dot(ur, c) + dot(ui, ci))
        if misfits and b < 2:
            misfits[b][...] = misfit
        elif misfits:
            misfits[2][b - 2] = misfit
        mt = misfit.T.astype(bf16)
        mr, mi = mt[:width], mt[width:]
        turned = jnp.concatenate([mi, -mr], axis=0)
        term = dot(mt, ur) + dot(turned, ui)
        total = term if total is None else total + term
    return total.T.astype(bf16)


def to_chunks(flat, adjoint):
    rank = adjoint.shape[1]
    for j in range(adjoint.shape[0]):
        adjoint[j] = flat[j * rank:(j + 1) * rank]


def row_kernel(coeffs, *refs, width):
    gathered, adjoint, misfits = refs[:GATHERED], refs[GATHERED], refs[GATHERED + 1:]
    c = coeffs[...].reshape(-1, 2 * width)
    to_chunks(row_core(c, gathered, misfits, width), adjoint)


def row_first_kernel(coeffs, *refs, group, width):
    gathered, pieces = refs[:GATHERED], refs[GATHERED:]
    z = row_index(group)
    rank = coeffs.shape[1]
    c = coeffs[...].reshape(-1, 2 * width)
    flat = row_core(c, gathered, (), width)

    def place(scratch):
        for j in range(flat.shape[0] // rank):
            scratch[jnp.bitwise_xor(z, j // group), j % group] = flat[j * rank:(j + 1) * rank]
        for b, piece in enumerate(pieces):
            piece[...] = scratch[b]

    pl.run_scoped(place, pltpu.VMEM((len(pieces),) + pieces[0].shape, bf16))


def row_last_kernel(*refs, group, width, count):
    pieces, refs = refs[:count], refs[count:]
    gathered, adjoint, misfits = refs[:GATHERED], refs[GATHERED], refs[GATHERED + 1:]
    z = row_index(group)

    def run(scratch):
        for b, piece in enumerate(pieces):
            scratch[jnp.bitwise_xor(z, b)] = piece[...]
        c = scratch[...].reshape(-1, 2 * width)
        to_chunks(row_core(c, gathered, misfits, width), adjoint)

    pl.run_scoped(run, pltpu.VMEM((count,) + pieces[0].shape, bf16))


def pack_kernel(x, to_far, to_near, own, *, group, width):
    q = group_index(group)
    lanes = 2 * width

    def place(scratch):
        for s, block in enumerate(slices_of(x[0], x[1], width)):
            scratch[jnp.bitwise_xor(q, s)] = block
        own[...] = scratch[0]
        to_far[0] = scratch[2].astype(bf16)
        to_far[1] = scratch[3].astype(bf16)
        high, low = split(scratch[1])
        to_near[:, :lanes] = high
        to_near[:, lanes:] = low

    pl.run_scoped(place, pltpu.VMEM((group, x.shape[1], lanes), f32))


def middle_columns_kernel(*refs, group, width, count):
    pieces, refs = refs[:count], refs[count:]
    (x_own, near, far, corner, v_own, v_near, v_far, v_corner), refs = refs[:8], refs[8:]
    outs, (adj_own, adj_near, adj_far) = refs[:count], refs[count:]
    q = group_index(group)
    z = row_index(group)
    lanes = 2 * width
    rank = pieces[0].shape[1]
    side = count * rank

    def run(adj, coeffs):
        for b, piece in enumerate(pieces):
            for k in range(group):
                adj[k, jnp.bitwise_xor(z, b)] = piece[jnp.bitwise_xor(q, k)]
        exact = near[...].astype(f32)
        columns = (
            (x_own[...], v_own),
            (exact[:, :lanes] + exact[:, lanes:], v_near),
            (far[0].astype(f32), v_far),
            (corner[1].astype(f32), v_corner),
        )
        for k, (x, v) in enumerate(columns):
            vcat = flat_factors(v)
            a = adj[k].reshape(side, lanes)
            if k == 0:
                adj_own[...] = a
            elif k == 1:
                adj_near[...] = a
            else:
                adj_far[k - 2] = a
            turned = times_i(a.astype(f32)).astype(bf16)
            s = x + STEP * dot(vcat, jnp.concatenate([a, turned], axis=0), ((0,), (0,)))
            square = s * s
            magnitude = jnp.sqrt(square + swap_halves(square))
            factor = jnp.maximum(magnitude - THRESHOLD, 0.0) / jnp.maximum(magnitude, THRESHOLD)
            t = dot(vcat, (s * factor).astype(bf16))
            c = (t[:side] - times_i(t[side:])).astype(bf16)
            for i in range(count):
                coeffs[i, jnp.bitwise_xor(q, k)] = c[i * rank:(i + 1) * rank]
        for b, out in enumerate(outs):
            out[...] = coeffs[jnp.bitwise_xor(z, b)]

    pl.run_scoped(
        run,
        pltpu.VMEM((group, count, rank, lanes), bf16),
        pltpu.VMEM((count, group, rank, lanes), bf16),
    )


def own_column_kernel(adj_own, adj_near, adj_far, adj_corner, x, vfac, x_new, *, group, width):
    q = group_index(group)

    def run(scratch):
        scratch[0] = adj_own[...]
        scratch[1] = adj_near[...]
        scratch[2] = adj_far[0]
        scratch[3] = adj_corner[1]
        sides = sides_of([scratch[jnp.bitwise_xor(q, s)].astype(f32) for s in range(group)])
        x_new[0], x_new[1] = updated(sides, x[0], x[1], flat_factors(vfac))

    pl.run_scoped(run, pltpu.VMEM((group,) + adj_own.shape, bf16))


def sides_of(quarters):
    pairs = [interleave(*quarters[k:k + 2]) for k in range(0, len(quarters), 2)]
    re = jnp.concatenate([r for r, _ in pairs], axis=1)
    im = jnp.concatenate([i for _, i in pairs], axis=1)
    real_side = jnp.concatenate([re, -im], axis=0).astype(bf16)
    imag_side = jnp.concatenate([im, re], axis=0).astype(bf16)
    return real_side, imag_side


def adjoint_sides(adjoint, *, group):
    count, rank, lanes = adjoint.shape
    rows = count // group
    a = adjoint[...].astype(f32).reshape(rows, group, rank, lanes)
    return sides_of([a[:, s].reshape(rows * rank, lanes) for s in range(group)])


def shrink(sr, si):
    magnitude = jnp.sqrt(sr * sr + si * si)
    factor = jnp.maximum(magnitude - THRESHOLD, 0.0) / jnp.maximum(magnitude, THRESHOLD)
    return sr * factor, si * factor


def updated(sides, xr, xi, vcat):
    gr, gi = (dot(vcat, side, ((0,), (0,))) for side in sides)
    return shrink(xr + STEP * gr, xi + STEP * gi)


def middle_kernel(adjoint, x, vfac, x_new, out, *, group, width):
    vcat = flat_factors(vfac)
    xr, xi = updated(adjoint_sides(adjoint, group=group), x[0], x[1], vcat)
    x_new[0] = xr
    x_new[1] = xi
    send_coeffs(vcat, xr.astype(bf16), xi.astype(bf16), out, group=group, width=width)


def last_kernel(adjoint, x, vfac, x_new, *, group, width):
    sources = x.shape[1]
    piece = sources // PIECES

    def run(stage, sems):
        sides = adjoint_sides(adjoint, group=group)
        copies = []
        for k in range(PIECES):
            cut = slice(k * piece, (k + 1) * piece)
            stage[0, cut], stage[1, cut] = updated(sides, x[0, cut], x[1, cut], flat_factors(vfac, cut))
            copies.append(pltpu.make_async_copy(stage.at[:, cut], x_new.at[:, cut], sems.at[k]))
            copies[-1].start()
        for copy in copies:
            copy.wait()

    pl.run_scoped(run, pltpu.VMEM(x.shape, f32), pltpu.SemaphoreType.DMA((PIECES,)))


def residual_kernel(misfit, near, far, far_near, out, *, group, width):
    q = group_index(group)

    def place(scratch, stage, sem):
        scratch[0] = misfit[...]
        scratch[1] = near[...]
        scratch[2] = far[0]
        scratch[3] = far_near[1]
        pieces = [scratch[jnp.bitwise_xor(q, s)] for s in range(group)]
        for k in range(group // 2):
            re, im = interleave(pieces[2 * k], pieces[2 * k + 1])
            stage[0, :, 2 * width * k:2 * width * (k + 1)] = re
            stage[1, :, 2 * width * k:2 * width * (k + 1)] = im
        copy = pltpu.make_async_copy(stage, out, sem)
        copy.start()
        copy.wait()

    pl.run_scoped(
        place,
        pltpu.VMEM((group,) + misfit.shape, f32),
        pltpu.VMEM(out.shape, f32),
        pltpu.SemaphoreType.DMA(()),
    )


def call(kernel, out_shape, *args, from_hbm=False, **static):
    on_chip = pl.BlockSpec(memory_space=pltpu.VMEM)
    off_chip = pl.BlockSpec(memory_space=pltpu.HBM)
    space = pltpu.HBM if from_hbm else pltpu.VMEM
    many = isinstance(out_shape, tuple)

    def spec(out):
        return off_chip if isinstance(out, jax.ShapeDtypeStruct) else on_chip

    return pl.pallas_call(
        functools.partial(kernel, **static),
        out_shape=out_shape,
        in_specs=[off_chip if from_hbm else on_chip] * len(args),
        out_specs=tuple(map(spec, out_shape)) if many else spec(out_shape),
        compiler_params=pltpu.CompilerParams(vmem_limit_bytes=VMEM_LIMIT),
    )(*(pltpu.with_memory_space_constraint(arg, space) for arg in args))


def body(data, x_init, ufac, vfac):
    tiles = lax.axis_size("tile")
    tile_rows, rank, _ = vfac.shape[1:]
    rows = data.shape[1]
    points = data.shape[2]
    group = tiles // tile_rows
    assert group == 4
    width = points // group
    lanes = 2 * width
    static = dict(group=group, width=width)
    shape = pltpu.VMEM
    result = jax.ShapeDtypeStruct

    def exchange(value, bit):
        return lax.ppermute(value, "tile", [(s, s ^ bit) for s in range(tiles)])

    def spread(value):
        return lax.all_to_all(value, "tile", split_axis=0, concat_axis=0, tiled=True)

    chunks = shape((tiles, rank, lanes), bf16)
    u_far = exchange(ufac, 2)
    u_near = exchange(ufac, 1)
    u_corner = exchange(u_far, 1)
    to_far, to_near, own, u_own, estimate, v_own, coeffs = call(
        first_kernel,
        (
            shape((2 * rows, 2 * lanes), bf16),
            shape((rows, 2 * lanes), bf16),
            shape((rows, lanes), f32),
            shape(ufac.shape, bf16),
            shape(x_init.shape, f32),
            shape(vfac.shape, bf16),
            chunks,
        ),
        data, x_init, ufac, vfac, from_hbm=True, **static,
    )
    far = exchange(to_far, 2)
    near = exchange(to_near, 1)
    corner = exchange(far, 1)
    gathered = (own, u_own, near, u_near, far, u_far, corner, u_corner)
    block = shape((rows, lanes), f32)
    row_outs = (chunks, block, block, shape((2, rows, lanes), f32))
    received = spread(coeffs)
    if tile_rows == 4:
        sources = x_init.shape[1]
        piece = shape((group, rank, lanes), bf16)
        side = (tile_rows * rank, lanes)
        counted = dict(count=tile_rows, **static)

        def along_rows(pieces):
            order = {b: exchange(pieces[b], b * group) for b in range(tile_rows - 1, 0, -1)}
            return [pieces[0]] + [order[b] for b in range(1, tile_rows)]

        v_far = exchange(vfac, 2)
        v_near = exchange(vfac, 1)
        v_corner = exchange(v_far, 1)
        x_far, x_near, x_own = call(
            pack_kernel,
            (
                shape((2, sources, lanes), bf16),
                shape((sources, 2 * lanes), bf16),
                shape((sources, lanes), f32),
            ),
            estimate, **static,
        )
        x_far = exchange(x_far, 2)
        x_near = exchange(x_near, 1)
        x_corner = exchange(x_far, 1)
        pieces = call(row_first_kernel, (piece,) * tile_rows, received, *gathered, **static)
        pieces = along_rows(pieces)
        *pieces, adj_own, adj_near, adj_far = call(
            middle_columns_kernel,
            (piece,) * tile_rows + (shape(side, bf16), shape(side, bf16), shape((2,) + side, bf16)),
            *pieces, x_own, x_near, x_far, x_corner, v_own, v_near, v_far, v_corner, **counted,
        )
        pieces = along_rows(pieces)
        adj_far = exchange(adj_far, 2)
        adj_near = exchange(adj_near, 1)
        adj_corner = exchange(adj_far, 1)
        row = call(row_last_kernel, row_outs, *pieces, *gathered, **counted)
        estimate = call(
            own_column_kernel, shape(x_init.shape, f32),
            adj_own, adj_near, adj_far, adj_corner, estimate, v_own, **static,
        )
    else:
        (pieces,) = call(row_kernel, (chunks,), received, *gathered, width=width)
        estimate, coeffs = call(
            middle_kernel, (shape(x_init.shape, f32), chunks), spread(pieces), estimate, v_own, **static
        )
        row = call(row_kernel, row_outs, spread(coeffs), *gathered, width=width)
    adjoint, misfit, to_near, to_far = row
    misfit_far = exchange(to_far, 2)
    misfit_near = exchange(to_near, 1)
    misfit_corner = exchange(misfit_far, 1)
    adjoint = spread(adjoint)
    solved = call(last_kernel, result(x_init.shape, f32), adjoint, estimate, v_own, **static)
    residual = call(
        residual_kernel, result(data.shape, f32), misfit, misfit_near, misfit_far, misfit_corner, **static
    )
    return (solved, residual)


def solution(mesh):
    in_specs = (
        P("freq", "tile", None),
        P("freq", "tile", None),
        P("freq", "tile", None),
        P("freq", None, None, "tile"),
    )
    out_specs = (P("freq", "tile", None), P("freq", "tile", None))
    return jax.shard_map(body, mesh=mesh, in_specs=in_specs, out_specs=out_specs, check_vma=False)
```

```python
import functools

import jax
import jax.numpy as jnp
from jax import lax
from jax.experimental import pallas as pl
from jax.experimental.pallas import tpu as pltpu
from jax.sharding import PartitionSpec as P


STEP = 0.4
THRESHOLD = 0.4
VMEM_LIMIT = 24 << 20
PIECES = 4

f32 = jnp.float32
bf16 = jnp.bfloat16


def dot(a, b, dims=((1,), (0,))):
    return lax.dot_general(a, b, (dims, ((), ())), preferred_element_type=f32)


def swap_halves(a):
    return pltpu.roll(a, a.shape[1] // 2, 1)


def left_half(a):
    return lax.broadcasted_iota(jnp.int32, a.shape, 1) < a.shape[1] // 2


def times_i(a):
    s = swap_halves(a)
    return jnp.where(left_half(a), -s, s)


def interleave(re, im):
    low = left_half(re)
    return (
        jnp.where(low, re, swap_halves(im)),
        jnp.where(low, swap_halves(re), im),
    )


def slices_of(re, im, width):
    out = []
    for k in range(re.shape[1] // (2 * width)):
        cut = slice(2 * width * k, 2 * width * (k + 1))
        out.extend(interleave(re[:, cut], im[:, cut]))
    return out


def group_index(group):
    return lax.rem(lax.axis_index("tile"), group)


def row_index(group):
    return lax.div(lax.axis_index("tile"), group)


def split(block):
    high = block.astype(bf16)
    low = (block - high.astype(f32)).astype(bf16)
    return high, low


def send_coeffs(vcat, xr, xi, out, *, group, width):
    half = vcat.shape[0] // 2
    t1 = dot(vcat, xr)
    t2 = dot(vcat, xi)
    cr = t1[:half] + t2[half:]
    ci = t2[:half] - t1[half:]
    rank = out.shape[1]
    blocks = slices_of(cr, ci, width)
    for i in range(half // rank):
        for q in range(group):
            out[i * group + q] = blocks[q][i * rank:(i + 1) * rank].astype(bf16)


def flat_factors(vfac, cut=slice(None)):
    parts, rows, rank, _ = vfac.shape
    return vfac[:, :, :, cut].reshape(parts * rows * rank, -1)


def first_kernel(data, x, ufac, vfac, to_far, to_near, own, u_own, x_own, v_own, out, *columns, group, width):
    rows = data.shape[1]
    sources = x.shape[1]
    lanes = 2 * width
    folds = ufac.shape[2] // (4 * width)
    step = rows // folds
    q = group_index(group)

    def run(waves, scratch, quarters, sems):
        wave_copy = pltpu.make_async_copy(data, waves, sems.at[0])
        v_copy = pltpu.make_async_copy(vfac, v_own, sems.at[1])
        u_copy = pltpu.make_async_copy(ufac, u_own, sems.at[2])
        x_copy = pltpu.make_async_copy(x, x_own, sems.at[3])
        for copy in (wave_copy, u_copy, v_copy, x_copy):
            copy.start()
        wave_copy.wait()
        for s, block in enumerate(slices_of(waves[0], waves[1], width)):
            scratch[jnp.bitwise_xor(q, s)] = block
        own[...] = scratch[0]
        for ref, base, b in ((to_near, 0, 1), (to_far, 0, 2), (to_far, step, 3)):
            high, low = split(scratch[b])
            for g in range(folds):
                cut = slice(g * step, (g + 1) * step)
                lane = 4 * width * g
                ref[base:base + step, lane:lane + 2 * width] = high[cut]
                ref[base:base + step, lane + 2 * width:lane + 4 * width] = low[cut]
        u_copy.wait()
        for part in range(2):
            to_near[step + rows * part:step + rows * (part + 1)] = u_own[part]
            to_far[2 * step + rows * part:2 * step + rows * (part + 1)] = u_own[part]
        v_copy.wait()
        if columns:
            far_x, near_x, block_x = columns
            tall = 2 * v_own.shape[1] * v_own.shape[2]
            wide = far_x.shape[1]
            for h in range(sources // wide):
                cut = slice(h * wide, (h + 1) * wide)
                far_x[sources + h * tall:sources + (h + 1) * tall] = flat_factors(v_own, cut)
        x_copy.wait()
        if columns:
            for s, block in enumerate(slices_of(x_own[0], x_own[1], width)):
                quarters[jnp.bitwise_xor(q, s)] = block
            block_x[...] = quarters[0]
            high, low = split(quarters[1])
            near_x[:, :lanes] = high
            near_x[:, lanes:] = low
            far_x[:sources, :lanes] = quarters[2].astype(bf16)
            far_x[:sources, lanes:] = quarters[3].astype(bf16)
        send_coeffs(
            flat_factors(v_own), x_own[0].astype(bf16), x_own[1].astype(bf16), out, group=group, width=width
        )

    pl.run_scoped(
        run,
        pltpu.VMEM(data.shape, f32),
        pltpu.VMEM((group, rows, 2 * width), f32),
        pltpu.VMEM((group, sources, lanes), f32),
        pltpu.SemaphoreType.DMA((4,)),
    )


def row_core(c, own, ufac, near, far, corner, misfits, width):
    lanes = 2 * width
    rows = own.shape[0]
    ci = times_i(c.astype(f32)).astype(bf16)
    folds = ufac.shape[2] // (2 * lanes)
    step = rows // folds

    def joined(ref, base):
        cuts = [ref[base:base + step, 2 * lanes * g:2 * lanes * (g + 1)].astype(f32) for g in range(folds)]
        pair = jnp.concatenate(cuts, axis=0)
        return pair[:, :lanes] + pair[:, lanes:]

    def factors(ref, base):
        return ref[base:base + rows], ref[base + rows:base + 2 * rows]

    blocks = (
        (own[...], (ufac[0], ufac[1])),
        (joined(near, 0), factors(near, step)),
        (joined(far, 0), factors(far, 2 * step)),
        (joined(corner, step), factors(corner, 2 * step)),
    )
    total = None
    for b, (wave, (ur, ui)) in enumerate(blocks):
        misfit = wave - (dot(ur, c) + dot(ui, ci))
        if misfits and b < 2:
            misfits[b][...] = misfit
        elif misfits:
            misfits[2][b - 2] = misfit
        mt = misfit.T.astype(bf16)
        mr, mi = mt[:width], mt[width:]
        turned = jnp.concatenate([mi, -mr], axis=0)
        term = dot(mt, ur) + dot(turned, ui)
        total = term if total is None else total + term
    return total.T.astype(bf16)


def to_chunks(flat, adjoint):
    rank = adjoint.shape[1]
    for j in range(adjoint.shape[0]):
        adjoint[j] = flat[j * rank:(j + 1) * rank]


def row_kernel(coeffs, own, ufac, near, far, corner, adjoint, *misfits, width):
    c = coeffs[...].reshape(-1, 2 * width)
    to_chunks(row_core(c, own, ufac, near, far, corner, misfits, width), adjoint)


def row_first_kernel(coeffs, own, ufac, near, far, corner, *pieces, group, width):
    z = row_index(group)
    rank = coeffs.shape[1]
    c = coeffs[...].reshape(-1, 2 * width)
    flat = row_core(c, own, ufac, near, far, corner, (), width)

    def place(scratch):
        for j in range(flat.shape[0] // rank):
            scratch[jnp.bitwise_xor(z, j // group), j % group] = flat[j * rank:(j + 1) * rank]
        for b, piece in enumerate(pieces):
            piece[...] = scratch[b]

    pl.run_scoped(place, pltpu.VMEM((len(pieces),) + pieces[0].shape, bf16))


def row_last_kernel(*refs, group, width, count):
    pieces, (own, ufac, near, far, corner, adjoint), misfits = refs[:count], refs[count:count + 6], refs[count + 6:]
    z = row_index(group)

    def run(scratch):
        for b, piece in enumerate(pieces):
            scratch[jnp.bitwise_xor(z, b)] = piece[...]
        c = scratch[...].reshape(-1, 2 * width)
        to_chunks(row_core(c, own, ufac, near, far, corner, misfits, width), adjoint)

    pl.run_scoped(run, pltpu.VMEM((count,) + pieces[0].shape, bf16))


def middle_columns_kernel(*refs, group, width, count):
    pieces, refs = refs[:count], refs[count:]
    (x_own, v_own, near, v_near, far, corner), refs = refs[:6], refs[6:]
    outs, (adj_own, adj_near, adj_far) = refs[:count], refs[count:]
    q = group_index(group)
    z = row_index(group)
    sources, lanes = x_own.shape
    rank = pieces[0].shape[1]
    side = count * rank
    tall = 2 * side

    def factors(ref):
        wide = ref.shape[1]
        cuts = [ref[sources + h * tall:sources + (h + 1) * tall] for h in range(sources // wide)]
        return jnp.concatenate(cuts, axis=1)

    def run(adj, coeffs):
        for b, piece in enumerate(pieces):
            for k in range(group):
                adj[k, jnp.bitwise_xor(z, b)] = piece[jnp.bitwise_xor(q, k)]
        exact = near[...].astype(f32)
        columns = (
            (x_own[...], flat_factors(v_own)),
            (exact[:, :lanes] + exact[:, lanes:], flat_factors(v_near)),
            (far[:sources, :lanes].astype(f32), factors(far)),
            (corner[:sources, lanes:].astype(f32), factors(corner)),
        )
        for k, (x, vcat) in enumerate(columns):
            a = adj[k].reshape(side, lanes)
            if k == 0:
                adj_own[...] = a
            elif k == 1:
                adj_near[...] = a
            else:
                adj_far[k - 2] = a
            turned = times_i(a.astype(f32)).astype(bf16)
            s = x + STEP * dot(vcat, jnp.concatenate([a, turned], axis=0), ((0,), (0,)))
            square = s * s
            magnitude = jnp.sqrt(square + swap_halves(square))
            factor = jnp.maximum(magnitude - THRESHOLD, 0.0) / jnp.maximum(magnitude, THRESHOLD)
            t = dot(vcat, (s * factor).astype(bf16))
            c = (t[:side] - times_i(t[side:])).astype(bf16)
            for i in range(count):
                coeffs[i, jnp.bitwise_xor(q, k)] = c[i * rank:(i + 1) * rank]
        for b, out in enumerate(outs):
            out[...] = coeffs[jnp.bitwise_xor(z, b)]

    pl.run_scoped(
        run,
        pltpu.VMEM((group, count, rank, lanes), bf16),
        pltpu.VMEM((count, group, rank, lanes), bf16),
    )


def own_column_kernel(adj_own, adj_near, adj_far, adj_corner, x, vfac, x_new, *, group, width):
    q = group_index(group)

    def run(scratch):
        scratch[0] = adj_own[...]
        scratch[1] = adj_near[...]
        scratch[2] = adj_far[0]
        scratch[3] = adj_corner[1]
        sides = sides_of([scratch[jnp.bitwise_xor(q, s)].astype(f32) for s in range(group)])
        x_new[0], x_new[1] = updated(sides, x[0], x[1], flat_factors(vfac))

    pl.run_scoped(run, pltpu.VMEM((group,) + adj_own.shape, bf16))


def sides_of(quarters):
    pairs = [interleave(*quarters[k:k + 2]) for k in range(0, len(quarters), 2)]
    re = jnp.concatenate([r for r, _ in pairs], axis=1)
    im = jnp.concatenate([i for _, i in pairs], axis=1)
    real_side = jnp.concatenate([re, -im], axis=0).astype(bf16)
    imag_side = jnp.concatenate([im, re], axis=0).astype(bf16)
    return real_side, imag_side


def adjoint_sides(adjoint, *, group):
    count, rank, lanes = adjoint.shape
    rows = count // group
    a = adjoint[...].astype(f32).reshape(rows, group, rank, lanes)
    return sides_of([a[:, s].reshape(rows * rank, lanes) for s in range(group)])


def shrink(sr, si):
    magnitude = jnp.sqrt(sr * sr + si * si)
    factor = jnp.maximum(magnitude - THRESHOLD, 0.0) / jnp.maximum(magnitude, THRESHOLD)
    return sr * factor, si * factor


def updated(sides, xr, xi, vcat):
    gr, gi = (dot(vcat, side, ((0,), (0,))) for side in sides)
    return shrink(xr + STEP * gr, xi + STEP * gi)


def middle_kernel(adjoint, x, vfac, x_new, out, *, group, width):
    vcat = flat_factors(vfac)
    xr, xi = updated(adjoint_sides(adjoint, group=group), x[0], x[1], vcat)
    x_new[0] = xr
    x_new[1] = xi
    send_coeffs(vcat, xr.astype(bf16), xi.astype(bf16), out, group=group, width=width)


def last_kernel(adjoint, x, vfac, x_new, *, group, width):
    sources = x.shape[1]
    piece = sources // PIECES

    def run(stage, sems):
        sides = adjoint_sides(adjoint, group=group)
        copies = []
        for k in range(PIECES):
            cut = slice(k * piece, (k + 1) * piece)
            stage[0, cut], stage[1, cut] = updated(sides, x[0, cut], x[1, cut], flat_factors(vfac, cut))
            copies.append(pltpu.make_async_copy(stage.at[:, cut], x_new.at[:, cut], sems.at[k]))
            copies[-1].start()
        for copy in copies:
            copy.wait()

    pl.run_scoped(run, pltpu.VMEM(x.shape, f32), pltpu.SemaphoreType.DMA((PIECES,)))


def residual_kernel(misfit, near, far, far_near, out, *, group, width):
    q = group_index(group)

    def place(scratch, stage, sem):
        scratch[0] = misfit[...]
        scratch[1] = near[...]
        scratch[2] = far[0]
        scratch[3] = far_near[1]
        pieces = [scratch[jnp.bitwise_xor(q, s)] for s in range(group)]
        for k in range(group // 2):
            re, im = interleave(pieces[2 * k], pieces[2 * k + 1])
            stage[0, :, 2 * width * k:2 * width * (k + 1)] = re
            stage[1, :, 2 * width * k:2 * width * (k + 1)] = im
        copy = pltpu.make_async_copy(stage, out, sem)
        copy.start()
        copy.wait()

    pl.run_scoped(
        place,
        pltpu.VMEM((group,) + misfit.shape, f32),
        pltpu.VMEM(out.shape, f32),
        pltpu.SemaphoreType.DMA(()),
    )


def call(kernel, out_shape, *args, from_hbm=False, **static):
    on_chip = pl.BlockSpec(memory_space=pltpu.VMEM)
    off_chip = pl.BlockSpec(memory_space=pltpu.HBM)
    space = pltpu.HBM if from_hbm else pltpu.VMEM
    many = isinstance(out_shape, tuple)

    def spec(out):
        return off_chip if isinstance(out, jax.ShapeDtypeStruct) else on_chip

    return pl.pallas_call(
        functools.partial(kernel, **static),
        out_shape=out_shape,
        in_specs=[off_chip if from_hbm else on_chip] * len(args),
        out_specs=tuple(map(spec, out_shape)) if many else spec(out_shape),
        compiler_params=pltpu.CompilerParams(vmem_limit_bytes=VMEM_LIMIT),
    )(*(pltpu.with_memory_space_constraint(arg, space) for arg in args))


def body(data, x_init, ufac, vfac):
    tiles = lax.axis_size("tile")
    tile_rows, rank, _ = vfac.shape[1:]
    rows = data.shape[1]
    points = data.shape[2]
    group = tiles // tile_rows
    assert group == 4
    width = points // group
    lanes = 2 * width
    static = dict(group=group, width=width)
    shape = pltpu.VMEM
    result = jax.ShapeDtypeStruct

    def exchange(value, bit):
        return lax.ppermute(value, "tile", [(s, s ^ bit) for s in range(tiles)])

    def spread(value):
        return lax.all_to_all(value, "tile", split_axis=0, concat_axis=0, tiled=True)

    wide = ufac.shape[2]
    step = rows * 2 * lanes // wide
    assert wide % (2 * lanes) == 0 and step % 16 == 0
    chunks = shape((tiles, rank, lanes), bf16)
    sources = x_init.shape[1]
    tall = 2 * tile_rows * rank
    columns = (
        shape((sources + tall * sources // (2 * lanes), 2 * lanes), bf16),
        shape((sources, 2 * lanes), bf16),
        shape((sources, lanes), f32),
    )
    by_columns = tile_rows == 4
    to_far, to_near, own, ufac, estimate, vfac, coeffs, *columns = call(
        first_kernel,
        (
            shape((2 * rows + 2 * step, wide), bf16),
            shape((2 * rows + step, wide), bf16),
            shape((rows, lanes), f32),
            shape(ufac.shape, bf16),
            shape(x_init.shape, f32),
            shape(vfac.shape, bf16),
            chunks,
        ) + (columns if by_columns else ()),
        data, x_init, ufac, vfac, from_hbm=True, **static,
    )
    far = exchange(to_far, 2)
    near = exchange(to_near, 1)
    corner = exchange(far, 1)
    gathered = (own, ufac, near, far, corner)
    block = shape((rows, lanes), f32)
    row_outs = (chunks, block, block, shape((2, rows, lanes), f32))
    received = spread(coeffs)
    if by_columns:
        piece = shape((group, rank, lanes), bf16)
        side = (tile_rows * rank, lanes)
        counted = dict(count=tile_rows, **static)

        def along_rows(pieces):
            order = {b: exchange(pieces[b], b * group) for b in range(tile_rows - 1, 0, -1)}
            return [pieces[0]] + [order[b] for b in range(1, tile_rows)]

        x_far, x_near, x_own = columns
        x_far = exchange(x_far, 2)
        x_near = exchange(x_near, 1)
        v_near = exchange(vfac, 1)
        x_corner = exchange(x_far, 1)
        pieces = call(row_first_kernel, (piece,) * tile_rows, received, *gathered, **static)
        pieces = along_rows(pieces)
        *pieces, adj_own, adj_near, adj_far = call(
            middle_columns_kernel,
            (piece,) * tile_rows + (shape(side, bf16), shape(side, bf16), shape((2,) + side, bf16)),
            *pieces, x_own, vfac, x_near, v_near, x_far, x_corner, **counted,
        )
        pieces = along_rows(pieces)
        adj_far = exchange(adj_far, 2)
        adj_near = exchange(adj_near, 1)
        adj_corner = exchange(adj_far, 1)
        row = call(row_last_kernel, row_outs, *pieces, *gathered, **counted)
        estimate = call(
            own_column_kernel, shape(x_init.shape, f32),
            adj_own, adj_near, adj_far, adj_corner, estimate, vfac, **static,
        )
    else:
        (pieces,) = call(row_kernel, (chunks,), received, *gathered, width=width)
        estimate, coeffs = call(
            middle_kernel, (shape(x_init.shape, f32), chunks), spread(pieces), estimate, vfac, **static
        )
        row = call(row_kernel, row_outs, spread(coeffs), *gathered, width=width)
    adjoint, misfit, to_near, to_far = row
    misfit_far = exchange(to_far, 2)
    misfit_near = exchange(to_near, 1)
    misfit_corner = exchange(misfit_far, 1)
    adjoint = spread(adjoint)
    solved = call(last_kernel, result(x_init.shape, f32), adjoint, estimate, vfac, **static)
    residual = call(
        residual_kernel, result(data.shape, f32), misfit, misfit_near, misfit_far, misfit_corner, **static
    )
    return (solved, residual)


def solution(mesh):
    in_specs = (
        P("freq", "tile", None),
        P("freq", "tile", None),
        P("freq", "tile", None),
        P("freq", None, None, "tile"),
    )
    out_specs = (P("freq", "tile", None), P("freq", "tile", None))
    return jax.shard_map(body, mesh=mesh, in_specs=in_specs, out_specs=out_specs, check_vma=False)
```

```python
import functools

import jax
import jax.numpy as jnp
from jax import lax
from jax.experimental import pallas as pl
from jax.experimental.pallas import tpu as pltpu
from jax.sharding import PartitionSpec as P


STEP = 0.4
THRESHOLD = 0.4
VMEM_LIMIT = 24 << 20
PIECES = 4

f32 = jnp.float32
bf16 = jnp.bfloat16


def dot(a, b, dims=((1,), (0,))):
    return lax.dot_general(a, b, (dims, ((), ())), preferred_element_type=f32)


def swap_halves(a):
    return pltpu.roll(a, a.shape[1] // 2, 1)


def left_half(a):
    return lax.broadcasted_iota(jnp.int32, a.shape, 1) < a.shape[1] // 2


def times_i(a):
    s = swap_halves(a)
    return jnp.where(left_half(a), -s, s)


def interleave(re, im):
    low = left_half(re)
    return (
        jnp.where(low, re, swap_halves(im)),
        jnp.where(low, swap_halves(re), im),
    )


def slices_of(re, im, width):
    out = []
    for k in range(re.shape[1] // (2 * width)):
        cut = slice(2 * width * k, 2 * width * (k + 1))
        out.extend(interleave(re[:, cut], im[:, cut]))
    return out


def group_index(group):
    return lax.rem(lax.axis_index("tile"), group)


def row_index(group):
    return lax.div(lax.axis_index("tile"), group)


def split(block):
    high = block.astype(bf16)
    low = (block - high.astype(f32)).astype(bf16)
    return high, low


def send_coeffs(vcat, xr, xi, out, *, group, width):
    half = vcat.shape[0] // 2
    t1 = dot(vcat, xr)
    t2 = dot(vcat, xi)
    cr = t1[:half] + t2[half:]
    ci = t2[:half] - t1[half:]
    rank = out.shape[1]
    blocks = slices_of(cr, ci, width)
    for i in range(half // rank):
        for q in range(group):
            out[i * group + q] = blocks[q][i * rank:(i + 1) * rank].astype(bf16)


def flat_factors(vfac, cut=slice(None)):
    parts, rows, rank, _ = vfac.shape
    return vfac[:, :, :, cut].reshape(parts * rows * rank, -1)


def first_kernel(data, x, ufac, vfac, out, to_far, to_near, own, u_own, x_own, v_own, *columns, group, width):
    rows = data.shape[1]
    sources = x.shape[1]
    lanes = 2 * width
    folds = ufac.shape[2] // (2 * lanes)
    step = rows // folds
    q = group_index(group)

    def run(stage, waves, scratch, quarters, sems):
        x_copy = pltpu.make_async_copy(x, x_own, sems.at[0])
        v_copy = pltpu.make_async_copy(vfac, v_own, sems.at[1])
        wave_copy = pltpu.make_async_copy(data, waves, sems.at[2])
        u_copy = pltpu.make_async_copy(ufac, u_own, sems.at[3])
        out_copy = pltpu.make_async_copy(stage, out, sems.at[4])
        for copy in (x_copy, v_copy, wave_copy, u_copy):
            copy.start()
        v_copy.wait()
        x_copy.wait()
        send_coeffs(
            flat_factors(v_own), x_own[0].astype(bf16), x_own[1].astype(bf16), stage, group=group, width=width
        )
        out_copy.start()
        wave_copy.wait()
        for s, block in enumerate(slices_of(waves[0], waves[1], width)):
            scratch[jnp.bitwise_xor(q, s)] = block
        own[...] = scratch[0]
        for ref, base, b in ((to_near, 0, 1), (to_far, 0, 2), (to_far, step, 3)):
            high, low = split(scratch[b])
            for g in range(folds):
                cut = slice(g * step, (g + 1) * step)
                lane = 2 * lanes * g
                ref[base:base + step, lane:lane + lanes] = high[cut]
                ref[base:base + step, lane + lanes:lane + 2 * lanes] = low[cut]
        u_copy.wait()
        for part in range(2):
            to_near[step + rows * part:step + rows * (part + 1)] = u_own[part]
            to_far[2 * step + rows * part:2 * step + rows * (part + 1)] = u_own[part]
        if columns:
            shared_x, far_x, near_x, block_x = columns
            tall = 2 * v_own.shape[1] * v_own.shape[2]
            for s, block in enumerate(slices_of(x_own[0], x_own[1], width)):
                quarters[jnp.bitwise_xor(q, s)] = block
            block_x[...] = quarters[0]
            high, low = split(quarters[1])
            near_x[:, :lanes] = high
            near_x[:, lanes:] = low
            far_x[...] = quarters[2].astype(bf16)
            half = sources // 2
            shared_x[:half, :lanes] = quarters[3, :half].astype(bf16)
            shared_x[:half, lanes:] = quarters[3, half:].astype(bf16)
            for h in range(sources // (2 * lanes)):
                cut = slice(h * 2 * lanes, (h + 1) * 2 * lanes)
                shared_x[half + h * tall:half + (h + 1) * tall] = flat_factors(v_own, cut)
        out_copy.wait()

    pl.run_scoped(
        run,
        pltpu.VMEM(out.shape, bf16),
        pltpu.VMEM(data.shape, f32),
        pltpu.VMEM((group, rows, lanes), f32),
        pltpu.VMEM((group, sources, lanes), f32),
        pltpu.SemaphoreType.DMA((5,)),
    )


def row_core(c, own, ufac, near, far, corner, misfits, width):
    lanes = 2 * width
    rows = own.shape[0]
    ci = times_i(c.astype(f32)).astype(bf16)
    folds = ufac.shape[2] // (2 * lanes)
    step = rows // folds

    def joined(ref, base):
        cuts = [ref[base:base + step, 2 * lanes * g:2 * lanes * (g + 1)].astype(f32) for g in range(folds)]
        pair = jnp.concatenate(cuts, axis=0)
        return pair[:, :lanes] + pair[:, lanes:]

    def factors(ref, base):
        return ref[base:base + rows], ref[base + rows:base + 2 * rows]

    blocks = (
        (own[...], (ufac[0], ufac[1])),
        (joined(near, 0), factors(near, step)),
        (joined(far, 0), factors(far, 2 * step)),
        (joined(corner, step), factors(corner, 2 * step)),
    )
    total = None
    for b, (wave, (ur, ui)) in enumerate(blocks):
        misfit = wave - (dot(ur, c) + dot(ui, ci))
        if misfits and b < 2:
            misfits[b][...] = misfit
        elif misfits:
            misfits[2][b - 2] = misfit
        mt = misfit.T.astype(bf16)
        mr, mi = mt[:width], mt[width:]
        turned = jnp.concatenate([mi, -mr], axis=0)
        term = dot(mt, ur) + dot(turned, ui)
        total = term if total is None else total + term
    return total.T.astype(bf16)


def to_chunks(flat, adjoint):
    rank = adjoint.shape[1]
    for j in range(adjoint.shape[0]):
        adjoint[j] = flat[j * rank:(j + 1) * rank]


def row_kernel(coeffs, own, ufac, near, far, corner, adjoint, *misfits, width):
    c = coeffs[...].reshape(-1, 2 * width)
    to_chunks(row_core(c, own, ufac, near, far, corner, misfits, width), adjoint)


def row_first_kernel(coeffs, own, ufac, near, far, corner, *pieces, group, width):
    z = row_index(group)
    rank = coeffs.shape[1]
    c = coeffs[...].reshape(-1, 2 * width)
    flat = row_core(c, own, ufac, near, far, corner, (), width)

    def place(scratch):
        for j in range(flat.shape[0] // rank):
            scratch[jnp.bitwise_xor(z, j // group), j % group] = flat[j * rank:(j + 1) * rank]
        for b, piece in enumerate(pieces):
            piece[...] = scratch[b]

    pl.run_scoped(place, pltpu.VMEM((len(pieces),) + pieces[0].shape, bf16))


def row_last_kernel(*refs, group, width, count):
    pieces, (own, ufac, near, far, corner, adjoint), misfits = refs[:count], refs[count:count + 6], refs[count + 6:]
    z = row_index(group)

    def run(scratch):
        for b, piece in enumerate(pieces):
            scratch[jnp.bitwise_xor(z, b)] = piece[...]
        c = scratch[...].reshape(-1, 2 * width)
        to_chunks(row_core(c, own, ufac, near, far, corner, misfits, width), adjoint)

    pl.run_scoped(run, pltpu.VMEM((count,) + pieces[0].shape, bf16))


def middle_columns_kernel(*refs, group, width, count):
    pieces, refs = refs[:count], refs[count:]
    (x_own, v_own, near, v_near, far, shared, corner), refs = refs[:7], refs[7:]
    outs, (adj_own, adj_near, adj_far) = refs[:count], refs[count:]
    q = group_index(group)
    z = row_index(group)
    sources, lanes = x_own.shape
    rank = pieces[0].shape[1]
    side = count * rank
    tall = 2 * side

    half = sources // 2

    def factors(ref):
        wide = ref.shape[1]
        cuts = [ref[half + h * tall:half + (h + 1) * tall] for h in range(sources // wide)]
        return jnp.concatenate(cuts, axis=1)

    def run(adj, coeffs):
        for b, piece in enumerate(pieces):
            for k in range(group):
                adj[k, jnp.bitwise_xor(z, b)] = piece[jnp.bitwise_xor(q, k)]
        exact = near[...].astype(f32)
        columns = (
            (x_own[...], flat_factors(v_own)),
            (exact[:, :lanes] + exact[:, lanes:], flat_factors(v_near)),
            (far[...].astype(f32), factors(shared)),
            (
                jnp.concatenate([corner[:half, :lanes], corner[:half, lanes:]], axis=0).astype(f32),
                factors(corner),
            ),
        )
        for k, (x, vcat) in enumerate(columns):
            a = adj[k].reshape(side, lanes)
            if k == 0:
                adj_own[...] = a
            elif k == 1:
                adj_near[...] = a
            else:
                adj_far[k - 2] = a
            turned = times_i(a.astype(f32)).astype(bf16)
            s = x + STEP * dot(vcat, jnp.concatenate([a, turned], axis=0), ((0,), (0,)))
            square = s * s
            magnitude = jnp.sqrt(square + swap_halves(square))
            factor = jnp.maximum(magnitude - THRESHOLD, 0.0) / jnp.maximum(magnitude, THRESHOLD)
            t = dot(vcat, (s * factor).astype(bf16))
            c = (t[:side] - times_i(t[side:])).astype(bf16)
            for i in range(count):
                coeffs[i, jnp.bitwise_xor(q, k)] = c[i * rank:(i + 1) * rank]
        for b, out in enumerate(outs):
            out[...] = coeffs[jnp.bitwise_xor(z, b)]

    pl.run_scoped(
        run,
        pltpu.VMEM((group, count, rank, lanes), bf16),
        pltpu.VMEM((count, group, rank, lanes), bf16),
    )


def own_column_kernel(adj_own, adj_near, adj_far, adj_corner, x, vfac, x_new, *, group, width):
    q = group_index(group)

    def run(scratch):
        scratch[0] = adj_own[...]
        scratch[1] = adj_near[...]
        scratch[2] = adj_far[0]
        scratch[3] = adj_corner[1]
        sides = sides_of([scratch[jnp.bitwise_xor(q, s)].astype(f32) for s in range(group)])
        x_new[0], x_new[1] = updated(sides, x[0], x[1], flat_factors(vfac))

    pl.run_scoped(run, pltpu.VMEM((group,) + adj_own.shape, bf16))


def sides_of(quarters):
    pairs = [interleave(*quarters[k:k + 2]) for k in range(0, len(quarters), 2)]
    re = jnp.concatenate([r for r, _ in pairs], axis=1)
    im = jnp.concatenate([i for _, i in pairs], axis=1)
    real_side = jnp.concatenate([re, -im], axis=0).astype(bf16)
    imag_side = jnp.concatenate([im, re], axis=0).astype(bf16)
    return real_side, imag_side


def adjoint_sides(adjoint, *, group):
    count, rank, lanes = adjoint.shape
    rows = count // group
    a = adjoint[...].astype(f32).reshape(rows, group, rank, lanes)
    return sides_of([a[:, s].reshape(rows * rank, lanes) for s in range(group)])


def shrink(sr, si):
    magnitude = jnp.sqrt(sr * sr + si * si)
    factor = jnp.maximum(magnitude - THRESHOLD, 0.0) / jnp.maximum(magnitude, THRESHOLD)
    return sr * factor, si * factor


def updated(sides, xr, xi, vcat):
    gr, gi = (dot(vcat, side, ((0,), (0,))) for side in sides)
    return shrink(xr + STEP * gr, xi + STEP * gi)


def middle_kernel(adjoint, x, vfac, x_new, out, *, group, width):
    vcat = flat_factors(vfac)
    xr, xi = updated(adjoint_sides(adjoint, group=group), x[0], x[1], vcat)
    x_new[0] = xr
    x_new[1] = xi
    send_coeffs(vcat, xr.astype(bf16), xi.astype(bf16), out, group=group, width=width)


def last_kernel(adjoint, x, vfac, x_new, *, group, width):
    sources = x.shape[1]
    piece = sources // PIECES

    def run(stage, sems):
        sides = adjoint_sides(adjoint, group=group)
        copies = []
        for k in range(PIECES):
            cut = slice(k * piece, (k + 1) * piece)
            stage[0, cut], stage[1, cut] = updated(sides, x[0, cut], x[1, cut], flat_factors(vfac, cut))
            copies.append(pltpu.make_async_copy(stage.at[:, cut], x_new.at[:, cut], sems.at[k]))
            copies[-1].start()
        for copy in copies:
            copy.wait()

    pl.run_scoped(run, pltpu.VMEM(x.shape, f32), pltpu.SemaphoreType.DMA((PIECES,)))


def residual_kernel(misfit, near, far, far_near, out, *, group, width):
    q = group_index(group)

    def place(scratch, stage, sem):
        scratch[0] = misfit[...]
        scratch[1] = near[...]
        scratch[2] = far[0]
        scratch[3] = far_near[1]
        pieces = [scratch[jnp.bitwise_xor(q, s)] for s in range(group)]
        for k in range(group // 2):
            re, im = interleave(pieces[2 * k], pieces[2 * k + 1])
            stage[0, :, 2 * width * k:2 * width * (k + 1)] = re
            stage[1, :, 2 * width * k:2 * width * (k + 1)] = im
        copy = pltpu.make_async_copy(stage, out, sem)
        copy.start()
        copy.wait()

    pl.run_scoped(
        place,
        pltpu.VMEM((group,) + misfit.shape, f32),
        pltpu.VMEM(out.shape, f32),
        pltpu.SemaphoreType.DMA(()),
    )


def call(kernel, out_shape, *args, from_hbm=False, **static):
    on_chip = pl.BlockSpec(memory_space=pltpu.VMEM)
    off_chip = pl.BlockSpec(memory_space=pltpu.HBM)
    space = pltpu.HBM if from_hbm else pltpu.VMEM
    many = isinstance(out_shape, tuple)

    def spec(out):
        return off_chip if isinstance(out, jax.ShapeDtypeStruct) else on_chip

    return pl.pallas_call(
        functools.partial(kernel, **static),
        out_shape=out_shape,
        in_specs=[off_chip if from_hbm else on_chip] * len(args),
        out_specs=tuple(map(spec, out_shape)) if many else spec(out_shape),
        compiler_params=pltpu.CompilerParams(vmem_limit_bytes=VMEM_LIMIT),
    )(*(pltpu.with_memory_space_constraint(arg, space) for arg in args))


def body(data, x_init, ufac, vfac):
    tiles = lax.axis_size("tile")
    tile_rows, rank, _ = vfac.shape[1:]
    rows = data.shape[1]
    points = data.shape[2]
    group = tiles // tile_rows
    assert group == 4
    width = points // group
    lanes = 2 * width
    static = dict(group=group, width=width)
    shape = pltpu.VMEM
    result = jax.ShapeDtypeStruct

    def exchange(value, bit):
        return lax.ppermute(value, "tile", [(s, s ^ bit) for s in range(tiles)])

    def spread(value):
        return lax.all_to_all(value, "tile", split_axis=0, concat_axis=0, tiled=True)

    wide = ufac.shape[2]
    step = rows * 2 * lanes // wide
    assert wide % (2 * lanes) == 0 and step % 16 == 0
    chunks = shape((tiles, rank, lanes), bf16)
    sources = x_init.shape[1]
    tall = 2 * tile_rows * rank
    columns = (
        shape((sources // 2 + tall * sources // (2 * lanes), 2 * lanes), bf16),
        shape((sources, lanes), bf16),
        shape((sources, 2 * lanes), bf16),
        shape((sources, lanes), f32),
    )
    by_columns = tile_rows == 4
    coeffs, to_far, to_near, own, ufac, estimate, vfac, *columns = call(
        first_kernel,
        (
            result(chunks.shape, bf16),
            shape((2 * rows + 2 * step, wide), bf16),
            shape((2 * rows + step, wide), bf16),
            shape((rows, lanes), f32),
            shape(ufac.shape, bf16),
            shape(x_init.shape, f32),
            shape(vfac.shape, bf16),
        ) + (columns if by_columns else ()),
        data, x_init, ufac, vfac, from_hbm=True, **static,
    )
    far = exchange(to_far, 2)
    near = exchange(to_near, 1)
    corner = exchange(far, 1)
    gathered = (own, ufac, near, far, corner)
    block = shape((rows, lanes), f32)
    row_outs = (chunks, block, block, shape((2, rows, lanes), f32))
    received = spread(coeffs)
    if by_columns:
        piece = shape((group, rank, lanes), bf16)
        side = (tile_rows * rank, lanes)
        counted = dict(count=tile_rows, **static)

        def along_rows(pieces):
            order = {b: exchange(pieces[b], b * group) for b in range(tile_rows - 1, 0, -1)}
            return [pieces[0]] + [order[b] for b in range(1, tile_rows)]

        x_shared, x_far, x_near, x_own = columns
        x_shared = exchange(x_shared, 2)
        x_far = exchange(x_far, 2)
        x_near = exchange(x_near, 1)
        v_near = exchange(vfac, 1)
        x_corner = exchange(x_shared, 1)
        pieces = call(row_first_kernel, (piece,) * tile_rows, received, *gathered, **static)
        pieces = along_rows(pieces)
        *pieces, adj_own, adj_near, adj_far = call(
            middle_columns_kernel,
            (piece,) * tile_rows + (shape(side, bf16), shape(side, bf16), shape((2,) + side, bf16)),
            *pieces, x_own, vfac, x_near, v_near, x_far, x_shared, x_corner, **counted,
        )
        pieces = along_rows(pieces)
        adj_far = exchange(adj_far, 2)
        adj_near = exchange(adj_near, 1)
        adj_corner = exchange(adj_far, 1)
        row = call(row_last_kernel, row_outs, *pieces, *gathered, **counted)
        estimate = call(
            own_column_kernel, shape(x_init.shape, f32),
            adj_own, adj_near, adj_far, adj_corner, estimate, vfac, **static,
        )
    else:
        (pieces,) = call(row_kernel, (chunks,), received, *gathered, width=width)
        estimate, coeffs = call(
            middle_kernel, (shape(x_init.shape, f32), chunks), spread(pieces), estimate, vfac, **static
        )
        row = call(row_kernel, row_outs, spread(coeffs), *gathered, width=width)
    adjoint, misfit, to_near, to_far = row
    misfit_far = exchange(to_far, 2)
    misfit_near = exchange(to_near, 1)
    misfit_corner = exchange(misfit_far, 1)
    adjoint = spread(adjoint)
    solved = call(last_kernel, result(x_init.shape, f32), adjoint, estimate, vfac, **static)
    residual = call(
        residual_kernel, result(data.shape, f32), misfit, misfit_near, misfit_far, misfit_corner, **static
    )
    return (solved, residual)


def solution(mesh):
    in_specs = (
        P("freq", "tile", None),
        P("freq", "tile", None),
        P("freq", "tile", None),
        P("freq", None, None, "tile"),
    )
    out_specs = (P("freq", "tile", None), P("freq", "tile", None))
    return jax.shard_map(body, mesh=mesh, in_specs=in_specs, out_specs=out_specs, check_vma=False)
```

```python
import functools

import jax
import jax.numpy as jnp
from jax import lax
from jax.experimental import pallas as pl
from jax.experimental.pallas import tpu as pltpu
from jax.sharding import PartitionSpec as P


STEP = 0.4
THRESHOLD = 0.4
VMEM_LIMIT = 24 << 20
PIECES = 4

f32 = jnp.float32
bf16 = jnp.bfloat16


def dot(a, b, dims=((1,), (0,))):
    return lax.dot_general(a, b, (dims, ((), ())), preferred_element_type=f32)


def swap_halves(a):
    return pltpu.roll(a, a.shape[1] // 2, 1)


def left_half(a):
    return lax.broadcasted_iota(jnp.int32, a.shape, 1) < a.shape[1] // 2


def times_i(a):
    s = swap_halves(a)
    return jnp.where(left_half(a), -s, s)


def interleave(re, im):
    low = left_half(re)
    return (
        jnp.where(low, re, swap_halves(im)),
        jnp.where(low, swap_halves(re), im),
    )


def slices_of(re, im, width):
    out = []
    for k in range(re.shape[1] // (2 * width)):
        cut = slice(2 * width * k, 2 * width * (k + 1))
        out.extend(interleave(re[:, cut], im[:, cut]))
    return out


def group_index(group):
    return lax.rem(lax.axis_index("tile"), group)


def row_index(group):
    return lax.div(lax.axis_index("tile"), group)


def split(block):
    high = block.astype(bf16)
    low = (block - high.astype(f32)).astype(bf16)
    return high, low


def send_coeffs(vcat, xr, xi, out, *, group, width):
    half = vcat.shape[0] // 2
    t1 = dot(vcat, xr)
    t2 = dot(vcat, xi)
    cr = t1[:half] + t2[half:]
    ci = t2[:half] - t1[half:]
    rank = out.shape[1]
    blocks = slices_of(cr, ci, width)
    for i in range(half // rank):
        for q in range(group):
            out[i * group + q] = blocks[q][i * rank:(i + 1) * rank].astype(bf16)


def flat_factors(vfac, cut=slice(None)):
    parts, rows, rank, _ = vfac.shape
    return vfac[:, :, :, cut].reshape(parts * rows * rank, -1)


def half_blocks(x, which, parity, lanes):
    cut = pl.ds(pl.multiple_of(which * lanes, lanes), lanes)
    even, odd = interleave(x[0, :, cut], x[1, :, cut])
    first = jnp.broadcast_to(parity, even.shape) == 0
    return jnp.where(first, even, odd), jnp.where(first, odd, even)


def blocks_kernel(x_own, x_near, own, near, *, group, width):
    q = group_index(group)
    for x, out in ((x_own, own), (x_near, near)):
        out[...], _ = half_blocks(x, lax.div(q, 2), lax.rem(q, 2), 2 * width)


def first_kernel(data, x, ufac, vfac, out, to_far, to_near, own, u_own, x_own, v_own, *columns, group, width):
    rows = data.shape[1]
    sources = x.shape[1]
    lanes = 2 * width
    folds = ufac.shape[2] // (2 * lanes)
    step = rows // folds
    q = group_index(group)

    def run(stage, waves, scratch, sems):
        x_copy = pltpu.make_async_copy(x, x_own, sems.at[0])
        v_copy = pltpu.make_async_copy(vfac, v_own, sems.at[1])
        wave_copy = pltpu.make_async_copy(data, waves, sems.at[2])
        u_copy = pltpu.make_async_copy(ufac, u_own, sems.at[3])
        out_copy = pltpu.make_async_copy(stage, out, sems.at[4])
        for copy in (x_copy, v_copy, wave_copy, u_copy):
            copy.start()
        v_copy.wait()
        x_copy.wait()
        send_coeffs(
            flat_factors(v_own), x_own[0].astype(bf16), x_own[1].astype(bf16), stage, group=group, width=width
        )
        out_copy.start()
        wave_copy.wait()
        for s, block in enumerate(slices_of(waves[0], waves[1], width)):
            scratch[jnp.bitwise_xor(q, s)] = block
        own[...] = scratch[0]
        for ref, base, b in ((to_near, 0, 1), (to_far, 0, 2), (to_far, step, 3)):
            high, low = split(scratch[b])
            for g in range(folds):
                cut = slice(g * step, (g + 1) * step)
                lane = 2 * lanes * g
                ref[base:base + step, lane:lane + lanes] = high[cut]
                ref[base:base + step, lane + lanes:lane + 2 * lanes] = low[cut]
        u_copy.wait()
        for part in range(2):
            to_near[step + rows * part:step + rows * (part + 1)] = u_own[part]
            to_far[2 * step + rows * part:2 * step + rows * (part + 1)] = u_own[part]
        if columns:
            shared_x, far_x = columns
            tall = 2 * v_own.shape[1] * v_own.shape[2]
            same, other = half_blocks(x_own, 1 - lax.div(q, 2), lax.rem(q, 2), lanes)
            far_x[...] = same.astype(bf16)
            half = sources // 2
            shared_x[:half, :lanes] = other[:half].astype(bf16)
            shared_x[:half, lanes:] = other[half:].astype(bf16)
            for h in range(sources // (2 * lanes)):
                cut = slice(h * 2 * lanes, (h + 1) * 2 * lanes)
                shared_x[half + h * tall:half + (h + 1) * tall] = flat_factors(v_own, cut)
        out_copy.wait()

    pl.run_scoped(
        run,
        pltpu.VMEM(out.shape, bf16),
        pltpu.VMEM(data.shape, f32),
        pltpu.VMEM((group, rows, lanes), f32),
        pltpu.SemaphoreType.DMA((5,)),
    )


def row_core(c, own, ufac, near, far, corner, misfits, width):
    lanes = 2 * width
    rows = own.shape[0]
    ci = times_i(c.astype(f32)).astype(bf16)
    folds = ufac.shape[2] // (2 * lanes)
    step = rows // folds

    def joined(ref, base):
        cuts = [ref[base:base + step, 2 * lanes * g:2 * lanes * (g + 1)].astype(f32) for g in range(folds)]
        pair = jnp.concatenate(cuts, axis=0)
        return pair[:, :lanes] + pair[:, lanes:]

    def factors(ref, base):
        return ref[base:base + rows], ref[base + rows:base + 2 * rows]

    blocks = (
        (own[...], (ufac[0], ufac[1])),
        (joined(near, 0), factors(near, step)),
        (joined(far, 0), factors(far, 2 * step)),
        (joined(corner, step), factors(corner, 2 * step)),
    )
    total = None
    for b, (wave, (ur, ui)) in enumerate(blocks):
        misfit = wave - (dot(ur, c) + dot(ui, ci))
        if misfits and b < 2:
            misfits[b][...] = misfit
        elif misfits:
            misfits[2][b - 2] = misfit
        mt = misfit.T.astype(bf16)
        mr, mi = mt[:width], mt[width:]
        turned = jnp.concatenate([mi, -mr], axis=0)
        term = dot(mt, ur) + dot(turned, ui)
        total = term if total is None else total + term
    return total.T.astype(bf16)


def to_chunks(flat, adjoint):
    rank = adjoint.shape[1]
    for j in range(adjoint.shape[0]):
        adjoint[j] = flat[j * rank:(j + 1) * rank]


def row_kernel(coeffs, own, ufac, near, far, corner, adjoint, *misfits, width):
    c = coeffs[...].reshape(-1, 2 * width)
    to_chunks(row_core(c, own, ufac, near, far, corner, misfits, width), adjoint)


def row_first_kernel(coeffs, own, ufac, near, far, corner, *pieces, group, width):
    z = row_index(group)
    rank = coeffs.shape[1]
    c = coeffs[...].reshape(-1, 2 * width)
    flat = row_core(c, own, ufac, near, far, corner, (), width)

    def place(scratch):
        for j in range(flat.shape[0] // rank):
            scratch[jnp.bitwise_xor(z, j // group), j % group] = flat[j * rank:(j + 1) * rank]
        for b, piece in enumerate(pieces):
            piece[...] = scratch[b]

    pl.run_scoped(place, pltpu.VMEM((len(pieces),) + pieces[0].shape, bf16))


def row_last_kernel(*refs, group, width, count):
    pieces, (own, ufac, near, far, corner, adjoint), misfits = refs[:count], refs[count:count + 6], refs[count + 6:]
    z = row_index(group)

    def run(scratch):
        for b, piece in enumerate(pieces):
            scratch[jnp.bitwise_xor(z, b)] = piece[...]
        c = scratch[...].reshape(-1, 2 * width)
        to_chunks(row_core(c, own, ufac, near, far, corner, misfits, width), adjoint)

    pl.run_scoped(run, pltpu.VMEM((count,) + pieces[0].shape, bf16))


def middle_columns_kernel(*refs, group, width, count):
    pieces, refs = refs[:count], refs[count:]
    (x_own, v_own, near, v_near, far, shared, corner), refs = refs[:7], refs[7:]
    outs, (adj_own, adj_near, adj_far) = refs[:count], refs[count:]
    q = group_index(group)
    z = row_index(group)
    sources, lanes = x_own.shape
    rank = pieces[0].shape[1]
    side = count * rank
    tall = 2 * side

    half = sources // 2

    def factors(ref):
        wide = ref.shape[1]
        cuts = [ref[half + h * tall:half + (h + 1) * tall] for h in range(sources // wide)]
        return jnp.concatenate(cuts, axis=1)

    def run(adj, coeffs):
        for b, piece in enumerate(pieces):
            for k in range(group):
                adj[k, jnp.bitwise_xor(z, b)] = piece[jnp.bitwise_xor(q, k)]
        columns = (
            (x_own[...], flat_factors(v_own)),
            (near[...], flat_factors(v_near)),
            (far[...].astype(f32), factors(shared)),
            (
                jnp.concatenate([corner[:half, :lanes], corner[:half, lanes:]], axis=0).astype(f32),
                factors(corner),
            ),
        )
        for k, (x, vcat) in enumerate(columns):
            a = adj[k].reshape(side, lanes)
            if k == 0:
                adj_own[...] = a
            elif k == 1:
                adj_near[...] = a
            else:
                adj_far[k - 2] = a
            turned = times_i(a.astype(f32)).astype(bf16)
            s = x + STEP * dot(vcat, jnp.concatenate([a, turned], axis=0), ((0,), (0,)))
            square = s * s
            magnitude = jnp.sqrt(square + swap_halves(square))
            factor = jnp.maximum(magnitude - THRESHOLD, 0.0) / jnp.maximum(magnitude, THRESHOLD)
            t = dot(vcat, (s * factor).astype(bf16))
            c = (t[:side] - times_i(t[side:])).astype(bf16)
            for i in range(count):
                coeffs[i, jnp.bitwise_xor(q, k)] = c[i * rank:(i + 1) * rank]
        for b, out in enumerate(outs):
            out[...] = coeffs[jnp.bitwise_xor(z, b)]

    pl.run_scoped(
        run,
        pltpu.VMEM((group, count, rank, lanes), bf16),
        pltpu.VMEM((count, group, rank, lanes), bf16),
    )


def own_column_kernel(adj_own, adj_near, adj_far, adj_corner, x, vfac, x_new, *, group, width):
    q = group_index(group)

    def run(scratch):
        scratch[0] = adj_own[...]
        scratch[1] = adj_near[...]
        scratch[2] = adj_far[0]
        scratch[3] = adj_corner[1]
        sides = sides_of([scratch[jnp.bitwise_xor(q, s)].astype(f32) for s in range(group)])
        x_new[0], x_new[1] = updated(sides, x[0], x[1], flat_factors(vfac))

    pl.run_scoped(run, pltpu.VMEM((group,) + adj_own.shape, bf16))


def sides_of(quarters):
    pairs = [interleave(*quarters[k:k + 2]) for k in range(0, len(quarters), 2)]
    re = jnp.concatenate([r for r, _ in pairs], axis=1)
    im = jnp.concatenate([i for _, i in pairs], axis=1)
    real_side = jnp.concatenate([re, -im], axis=0).astype(bf16)
    imag_side = jnp.concatenate([im, re], axis=0).astype(bf16)
    return real_side, imag_side


def adjoint_sides(adjoint, *, group):
    count, rank, lanes = adjoint.shape
    rows = count // group
    a = adjoint[...].astype(f32).reshape(rows, group, rank, lanes)
    return sides_of([a[:, s].reshape(rows * rank, lanes) for s in range(group)])


def shrink(sr, si):
    magnitude = jnp.sqrt(sr * sr + si * si)
    factor = jnp.maximum(magnitude - THRESHOLD, 0.0) / jnp.maximum(magnitude, THRESHOLD)
    return sr * factor, si * factor


def updated(sides, xr, xi, vcat):
    gr, gi = (dot(vcat, side, ((0,), (0,))) for side in sides)
    return shrink(xr + STEP * gr, xi + STEP * gi)


def middle_kernel(adjoint, x, vfac, x_new, out, *, group, width):
    vcat = flat_factors(vfac)
    xr, xi = updated(adjoint_sides(adjoint, group=group), x[0], x[1], vcat)
    x_new[0] = xr
    x_new[1] = xi
    send_coeffs(vcat, xr.astype(bf16), xi.astype(bf16), out, group=group, width=width)


def last_kernel(adjoint, x, vfac, x_new, *, group, width):
    sources = x.shape[1]
    piece = sources // PIECES

    def run(stage, sems):
        sides = adjoint_sides(adjoint, group=group)
        copies = []
        for k in range(PIECES):
            cut = slice(k * piece, (k + 1) * piece)
            stage[0, cut], stage[1, cut] = updated(sides, x[0, cut], x[1, cut], flat_factors(vfac, cut))
            copies.append(pltpu.make_async_copy(stage.at[:, cut], x_new.at[:, cut], sems.at[k]))
            copies[-1].start()
        for copy in copies:
            copy.wait()

    pl.run_scoped(run, pltpu.VMEM(x.shape, f32), pltpu.SemaphoreType.DMA((PIECES,)))


def residual_kernel(misfit, near, far, far_near, out, *, group, width):
    q = group_index(group)

    def place(scratch, stage, sem):
        scratch[0] = misfit[...]
        scratch[1] = near[...]
        scratch[2] = far[0]
        scratch[3] = far_near[1]
        pieces = [scratch[jnp.bitwise_xor(q, s)] for s in range(group)]
        for k in range(group // 2):
            re, im = interleave(pieces[2 * k], pieces[2 * k + 1])
            stage[0, :, 2 * width * k:2 * width * (k + 1)] = re
            stage[1, :, 2 * width * k:2 * width * (k + 1)] = im
        copy = pltpu.make_async_copy(stage, out, sem)
        copy.start()
        copy.wait()

    pl.run_scoped(
        place,
        pltpu.VMEM((group,) + misfit.shape, f32),
        pltpu.VMEM(out.shape, f32),
        pltpu.SemaphoreType.DMA(()),
    )


def call(kernel, out_shape, *args, from_hbm=False, **static):
    on_chip = pl.BlockSpec(memory_space=pltpu.VMEM)
    off_chip = pl.BlockSpec(memory_space=pltpu.HBM)
    space = pltpu.HBM if from_hbm else pltpu.VMEM
    many = isinstance(out_shape, tuple)

    def spec(out):
        return off_chip if isinstance(out, jax.ShapeDtypeStruct) else on_chip

    return pl.pallas_call(
        functools.partial(kernel, **static),
        out_shape=out_shape,
        in_specs=[off_chip if from_hbm else on_chip] * len(args),
        out_specs=tuple(map(spec, out_shape)) if many else spec(out_shape),
        compiler_params=pltpu.CompilerParams(vmem_limit_bytes=VMEM_LIMIT),
    )(*(pltpu.with_memory_space_constraint(arg, space) for arg in args))


def body(data, x_init, ufac, vfac):
    tiles = lax.axis_size("tile")
    tile_rows, rank, _ = vfac.shape[1:]
    rows = data.shape[1]
    points = data.shape[2]
    group = tiles // tile_rows
    assert group == 4
    width = points // group
    lanes = 2 * width
    static = dict(group=group, width=width)
    shape = pltpu.VMEM
    result = jax.ShapeDtypeStruct

    def exchange(value, bit):
        return lax.ppermute(value, "tile", [(s, s ^ bit) for s in range(tiles)])

    def spread(value):
        return lax.all_to_all(value, "tile", split_axis=0, concat_axis=0, tiled=True)

    wide = ufac.shape[2]
    step = rows * 2 * lanes // wide
    assert wide % (2 * lanes) == 0 and step % 16 == 0
    chunks = shape((tiles, rank, lanes), bf16)
    sources = x_init.shape[1]
    tall = 2 * tile_rows * rank
    columns = (
        shape((sources // 2 + tall * sources // (2 * lanes), 2 * lanes), bf16),
        shape((sources, lanes), bf16),
    )
    by_columns = tile_rows == 4
    coeffs, to_far, to_near, own, ufac, estimate, vfac, *columns = call(
        first_kernel,
        (
            result(chunks.shape, bf16),
            shape((2 * rows + 2 * step, wide), bf16),
            shape((2 * rows + step, wide), bf16),
            shape((rows, lanes), f32),
            shape(ufac.shape, bf16),
            shape(x_init.shape, f32),
            shape(vfac.shape, bf16),
        ) + (columns if by_columns else ()),
        data, x_init, ufac, vfac, from_hbm=True, **static,
    )
    far = exchange(to_far, 2)
    near = exchange(to_near, 1)
    corner = exchange(far, 1)
    gathered = (own, ufac, near, far, corner)
    block = shape((rows, lanes), f32)
    row_outs = (chunks, block, block, shape((2, rows, lanes), f32))
    received = spread(coeffs)
    if by_columns:
        piece = shape((group, rank, lanes), bf16)
        side = (tile_rows * rank, lanes)
        counted = dict(count=tile_rows, **static)

        def along_rows(pieces):
            order = {b: exchange(pieces[b], b * group) for b in range(tile_rows - 1, 0, -1)}
            return [pieces[0]] + [order[b] for b in range(1, tile_rows)]

        x_shared, x_far = columns
        x_shared = exchange(x_shared, 2)
        x_far = exchange(x_far, 2)
        x_near = exchange(x_init, 1)
        x_own, x_near = call(blocks_kernel, (shape((sources, lanes), f32),) * 2, estimate, x_near, **static)
        v_near = exchange(vfac, 1)
        x_corner = exchange(x_shared, 1)
        pieces = call(row_first_kernel, (piece,) * tile_rows, received, *gathered, **static)
        pieces = along_rows(pieces)
        *pieces, adj_own, adj_near, adj_far = call(
            middle_columns_kernel,
            (piece,) * tile_rows + (shape(side, bf16), shape(side, bf16), shape((2,) + side, bf16)),
            *pieces, x_own, vfac, x_near, v_near, x_far, x_shared, x_corner, **counted,
        )
        pieces = along_rows(pieces)
        adj_far = exchange(adj_far, 2)
        adj_near = exchange(adj_near, 1)
        adj_corner = exchange(adj_far, 1)
        row = call(row_last_kernel, row_outs, *pieces, *gathered, **counted)
        estimate = call(
            own_column_kernel, shape(x_init.shape, f32),
            adj_own, adj_near, adj_far, adj_corner, estimate, vfac, **static,
        )
    else:
        (pieces,) = call(row_kernel, (chunks,), received, *gathered, width=width)
        estimate, coeffs = call(
            middle_kernel, (shape(x_init.shape, f32), chunks), spread(pieces), estimate, vfac, **static
        )
        row = call(row_kernel, row_outs, spread(coeffs), *gathered, width=width)
    adjoint, misfit, to_near, to_far = row
    misfit_far = exchange(to_far, 2)
    misfit_near = exchange(to_near, 1)
    misfit_corner = exchange(misfit_far, 1)
    adjoint = spread(adjoint)
    solved = call(last_kernel, result(x_init.shape, f32), adjoint, estimate, vfac, **static)
    residual = call(residual_kernel, result(data.shape, f32), misfit, misfit_near, misfit_far, misfit_corner, **static)
    return (solved, residual)


def solution(mesh):
    in_specs = (
        P("freq", "tile", None),
        P("freq", "tile", None),
        P("freq", "tile", None),
        P("freq", None, None, "tile"),
    )
    out_specs = (P("freq", "tile", None), P("freq", "tile", None))
    return jax.shard_map(body, mesh=mesh, in_specs=in_specs, out_specs=out_specs, check_vma=False)
```

```python
import functools

import jax
import jax.numpy as jnp
from jax import lax
from jax.experimental import pallas as pl
from jax.experimental.pallas import tpu as pltpu
from jax.sharding import PartitionSpec as P


STEP = 0.4
THRESHOLD = 0.4
VMEM_LIMIT = 24 << 20
PIECES = 4

f32 = jnp.float32
bf16 = jnp.bfloat16


def dot(a, b, dims=((1,), (0,))):
    return lax.dot_general(a, b, (dims, ((), ())), preferred_element_type=f32)


def swap_halves(a):
    return pltpu.roll(a, a.shape[1] // 2, 1)


def left_half(a):
    return lax.broadcasted_iota(jnp.int32, a.shape, 1) < a.shape[1] // 2


def times_i(a):
    s = swap_halves(a)
    return jnp.where(left_half(a), -s, s)


def interleave(re, im):
    low = left_half(re)
    return (
        jnp.where(low, re, swap_halves(im)),
        jnp.where(low, swap_halves(re), im),
    )


def slices_of(re, im, width):
    out = []
    for k in range(re.shape[1] // (2 * width)):
        cut = slice(2 * width * k, 2 * width * (k + 1))
        out.extend(interleave(re[:, cut], im[:, cut]))
    return out


def group_index(group):
    return lax.rem(lax.axis_index("tile"), group)


def row_index(group):
    return lax.div(lax.axis_index("tile"), group)


def split(block):
    high = block.astype(bf16)
    low = (block - high.astype(f32)).astype(bf16)
    return high, low


def send_coeffs(vcat, xr, xi, out, *, group, width):
    half = vcat.shape[0] // 2
    t1 = dot(vcat, xr)
    t2 = dot(vcat, xi)
    cr = t1[:half] + t2[half:]
    ci = t2[:half] - t1[half:]
    rank = out.shape[1]
    blocks = slices_of(cr, ci, width)
    for i in range(half // rank):
        for q in range(group):
            out[i * group + q] = blocks[q][i * rank:(i + 1) * rank].astype(bf16)


def flat_factors(vfac, cut=slice(None)):
    parts, rows, rank, _ = vfac.shape
    return vfac[:, :, :, cut].reshape(parts * rows * rank, -1)


def first_kernel(data, x, ufac, vfac, out, to_far, to_near, own, u_own, x_own, v_own, *columns, group, width):
    rows = data.shape[1]
    sources = x.shape[1]
    lanes = 2 * width
    folds = ufac.shape[2] // (2 * lanes)
    step = rows // folds
    q = group_index(group)

    def run(stage, waves, scratch, quarters, sems):
        x_copy = pltpu.make_async_copy(x, x_own, sems.at[0])
        v_copy = pltpu.make_async_copy(vfac, v_own, sems.at[1])
        wave_copy = pltpu.make_async_copy(data, waves, sems.at[2])
        u_copy = pltpu.make_async_copy(ufac, u_own, sems.at[3])
        out_copy = pltpu.make_async_copy(stage, out, sems.at[4])
        for copy in (x_copy, v_copy, wave_copy, u_copy):
            copy.start()
        v_copy.wait()
        x_copy.wait()
        send_coeffs(
            flat_factors(v_own), x_own[0].astype(bf16), x_own[1].astype(bf16), stage, group=group, width=width
        )
        out_copy.start()
        wave_copy.wait()
        for s, block in enumerate(slices_of(waves[0], waves[1], width)):
            scratch[jnp.bitwise_xor(q, s)] = block
        own[...] = scratch[0]
        for ref, base, b in ((to_near, 0, 1), (to_far, 0, 2), (to_far, step, 3)):
            high, low = split(scratch[b])
            for g in range(folds):
                cut = slice(g * step, (g + 1) * step)
                lane = 2 * lanes * g
                ref[base:base + step, lane:lane + lanes] = high[cut]
                ref[base:base + step, lane + lanes:lane + 2 * lanes] = low[cut]
        u_copy.wait()
        for part in range(2):
            to_near[step + rows * part:step + rows * (part + 1)] = u_own[part]
            to_far[2 * step + rows * part:2 * step + rows * (part + 1)] = u_own[part]
        if columns:
            shared_x, far_x, near_x, block_x = columns
            tall = 2 * v_own.shape[1] * v_own.shape[2]
            for s, block in enumerate(slices_of(x_own[0], x_own[1], width)):
                quarters[jnp.bitwise_xor(q, s)] = block
            block_x[...] = quarters[0]
            high, low = split(quarters[1])
            near_x[:, :lanes] = high
            near_x[:, lanes:] = low
            far_x[...] = quarters[2].astype(bf16)
            half = sources // 2
            shared_x[:half, :lanes] = quarters[3, :half].astype(bf16)
            shared_x[:half, lanes:] = quarters[3, half:].astype(bf16)
            for h in range(sources // (2 * lanes)):
                cut = slice(h * 2 * lanes, (h + 1) * 2 * lanes)
                shared_x[half + h * tall:half + (h + 1) * tall] = flat_factors(v_own, cut)
        out_copy.wait()

    pl.run_scoped(
        run,
        pltpu.VMEM(out.shape, bf16),
        pltpu.VMEM(data.shape, f32),
        pltpu.VMEM((group, rows, lanes), f32),
        pltpu.VMEM((group, sources, lanes), f32),
        pltpu.SemaphoreType.DMA((5,)),
    )


def row_core(c, own, ufac, near, far, corner, misfits, width):
    lanes = 2 * width
    rows = own.shape[0]
    ci = times_i(c.astype(f32)).astype(bf16)
    folds = ufac.shape[2] // (2 * lanes)
    step = rows // folds

    def joined(ref, base):
        cuts = [ref[base:base + step, 2 * lanes * g:2 * lanes * (g + 1)].astype(f32) for g in range(folds)]
        pair = jnp.concatenate(cuts, axis=0)
        return pair[:, :lanes] + pair[:, lanes:]

    def factors(ref, base):
        return ref[base:base + rows], ref[base + rows:base + 2 * rows]

    blocks = (
        (own[...], (ufac[0], ufac[1])),
        (joined(near, 0), factors(near, step)),
        (joined(far, 0), factors(far, 2 * step)),
        (joined(corner, step), factors(corner, 2 * step)),
    )
    total = None
    for b, (wave, (ur, ui)) in enumerate(blocks):
        misfit = wave - (dot(ur, c) + dot(ui, ci))
        if misfits and b < 2:
            misfits[b][...] = misfit
        elif misfits:
            misfits[2][b - 2] = misfit
        mt = misfit.T.astype(bf16)
        mr, mi = mt[:width], mt[width:]
        turned = jnp.concatenate([mi, -mr], axis=0)
        term = dot(mt, ur) + dot(turned, ui)
        total = term if total is None else total + term
    return total.T.astype(bf16)


def to_chunks(flat, adjoint):
    rank = adjoint.shape[1]
    for j in range(adjoint.shape[0]):
        adjoint[j] = flat[j * rank:(j + 1) * rank]


def row_kernel(coeffs, own, ufac, near, far, corner, adjoint, *misfits, width):
    c = coeffs[...].reshape(-1, 2 * width)
    to_chunks(row_core(c, own, ufac, near, far, corner, misfits, width), adjoint)


def row_first_kernel(coeffs, own, ufac, near, far, corner, *pieces, group, width):
    z = row_index(group)
    rank = coeffs.shape[1]
    c = coeffs[...].reshape(-1, 2 * width)
    flat = row_core(c, own, ufac, near, far, corner, (), width)

    def place(scratch):
        for j in range(flat.shape[0] // rank):
            scratch[jnp.bitwise_xor(z, j // group), j % group] = flat[j * rank:(j + 1) * rank]
        for b, piece in enumerate(pieces):
            piece[...] = scratch[b]

    pl.run_scoped(place, pltpu.VMEM((len(pieces),) + pieces[0].shape, bf16))


def row_last_kernel(*refs, group, width, count):
    pieces, (own, ufac, near, far, corner, adjoint), misfits = refs[:count], refs[count:count + 6], refs[count + 6:]
    z = row_index(group)

    def run(scratch):
        for b, piece in enumerate(pieces):
            scratch[jnp.bitwise_xor(z, b)] = piece[...]
        c = scratch[...].reshape(-1, 2 * width)
        to_chunks(row_core(c, own, ufac, near, far, corner, misfits, width), adjoint)

    pl.run_scoped(run, pltpu.VMEM((count,) + pieces[0].shape, bf16))


def middle_columns_kernel(*refs, group, width, count):
    pieces, refs = refs[:count], refs[count:]
    (x_own, v_own, near, v_near, far, shared, corner), refs = refs[:7], refs[7:]
    outs, (adj_own, adj_near, adj_far) = refs[:count], refs[count:]
    q = group_index(group)
    z = row_index(group)
    sources, lanes = x_own.shape
    rank = pieces[0].shape[1]
    side = count * rank
    tall = 2 * side

    half = sources // 2

    def factors(ref):
        wide = ref.shape[1]
        cuts = [ref[half + h * tall:half + (h + 1) * tall] for h in range(sources // wide)]
        return jnp.concatenate(cuts, axis=1)

    def run(adj, coeffs):
        for b, piece in enumerate(pieces):
            for k in range(group):
                adj[k, jnp.bitwise_xor(z, b)] = piece[jnp.bitwise_xor(q, k)]
        exact = near[...].astype(f32)
        columns = (
            (x_own[...], flat_factors(v_own)),
            (exact[:, :lanes] + exact[:, lanes:], flat_factors(v_near)),
            (far[...].astype(f32), factors(shared)),
            (
                jnp.concatenate([corner[:half, :lanes], corner[:half, lanes:]], axis=0).astype(f32),
                factors(corner),
            ),
        )
        for k, (x, vcat) in enumerate(columns):
            a = adj[k].reshape(side, lanes)
            if k == 0:
                adj_own[...] = a
            elif k == 1:
                adj_near[...] = a
            else:
                adj_far[k - 2] = a
            turned = times_i(a.astype(f32)).astype(bf16)
            s = x + STEP * dot(vcat, jnp.concatenate([a, turned], axis=0), ((0,), (0,)))
            square = s * s
            magnitude = jnp.sqrt(square + swap_halves(square))
            factor = jnp.maximum(magnitude - THRESHOLD, 0.0) / jnp.maximum(magnitude, THRESHOLD)
            t = dot(vcat, (s * factor).astype(bf16))
            c = (t[:side] - times_i(t[side:])).astype(bf16)
            for i in range(count):
                coeffs[i, jnp.bitwise_xor(q, k)] = c[i * rank:(i + 1) * rank]
        for b, out in enumerate(outs):
            out[...] = coeffs[jnp.bitwise_xor(z, b)]

    pl.run_scoped(
        run,
        pltpu.VMEM((group, count, rank, lanes), bf16),
        pltpu.VMEM((count, group, rank, lanes), bf16),
    )


def own_column_kernel(adj_own, adj_near, adj_far, adj_corner, x, vfac, x_new, *, group, width):
    q = group_index(group)

    def run(scratch):
        scratch[0] = adj_own[...]
        scratch[1] = adj_near[...]
        scratch[2] = adj_far[0]
        scratch[3] = adj_corner[1]
        sides = sides_of([scratch[jnp.bitwise_xor(q, s)].astype(f32) for s in range(group)])
        x_new[0], x_new[1] = updated(sides, x[0], x[1], flat_factors(vfac))

    pl.run_scoped(run, pltpu.VMEM((group,) + adj_own.shape, bf16))


def sides_of(quarters):
    pairs = [interleave(*quarters[k:k + 2]) for k in range(0, len(quarters), 2)]
    re = jnp.concatenate([r for r, _ in pairs], axis=1)
    im = jnp.concatenate([i for _, i in pairs], axis=1)
    real_side = jnp.concatenate([re, -im], axis=0).astype(bf16)
    imag_side = jnp.concatenate([im, re], axis=0).astype(bf16)
    return real_side, imag_side


def adjoint_sides(adjoint, *, group):
    count, rank, lanes = adjoint.shape
    rows = count // group
    a = adjoint[...].astype(f32).reshape(rows, group, rank, lanes)
    return sides_of([a[:, s].reshape(rows * rank, lanes) for s in range(group)])


def shrink(sr, si):
    magnitude = jnp.sqrt(sr * sr + si * si)
    factor = jnp.maximum(magnitude - THRESHOLD, 0.0) / jnp.maximum(magnitude, THRESHOLD)
    return sr * factor, si * factor


def updated(sides, xr, xi, vcat):
    gr, gi = (dot(vcat, side, ((0,), (0,))) for side in sides)
    return shrink(xr + STEP * gr, xi + STEP * gi)


def middle_kernel(adjoint, x, vfac, x_new, out, *, group, width):
    vcat = flat_factors(vfac)
    xr, xi = updated(adjoint_sides(adjoint, group=group), x[0], x[1], vcat)
    x_new[0] = xr
    x_new[1] = xi
    send_coeffs(vcat, xr.astype(bf16), xi.astype(bf16), out, group=group, width=width)


def last_kernel(adjoint, x, vfac, x_new, *, group, width):
    sources = x.shape[1]
    piece = sources // PIECES

    def run(stage, sems):
        sides = adjoint_sides(adjoint, group=group)
        copies = []
        for k in range(PIECES):
            cut = slice(k * piece, (k + 1) * piece)
            stage[0, cut], stage[1, cut] = updated(sides, x[0, cut], x[1, cut], flat_factors(vfac, cut))
            copies.append(pltpu.make_async_copy(stage.at[:, cut], x_new.at[:, cut], sems.at[k]))
            copies[-1].start()
        for copy in copies:
            copy.wait()

    pl.run_scoped(run, pltpu.VMEM(x.shape, f32), pltpu.SemaphoreType.DMA((PIECES,)))


def residual_kernel(misfit, near, far, far_near, out, *, group, width):
    q = group_index(group)

    def place(scratch, stage, sem):
        scratch[0] = misfit[...]
        scratch[1] = near[...]
        scratch[2] = far[0]
        scratch[3] = far_near[1]
        pieces = [scratch[jnp.bitwise_xor(q, s)] for s in range(group)]
        for k in range(group // 2):
            re, im = interleave(pieces[2 * k], pieces[2 * k + 1])
            stage[0, :, 2 * width * k:2 * width * (k + 1)] = re
            stage[1, :, 2 * width * k:2 * width * (k + 1)] = im
        copy = pltpu.make_async_copy(stage, out, sem)
        copy.start()
        copy.wait()

    pl.run_scoped(
        place,
        pltpu.VMEM((group,) + misfit.shape, f32),
        pltpu.VMEM(out.shape, f32),
        pltpu.SemaphoreType.DMA(()),
    )


def call(kernel, out_shape, *args, from_hbm=False, aliases=None, **static):
    on_chip = pl.BlockSpec(memory_space=pltpu.VMEM)
    off_chip = pl.BlockSpec(memory_space=pltpu.HBM)
    space = pltpu.HBM if from_hbm else pltpu.VMEM
    many = isinstance(out_shape, tuple)

    def spec(out):
        return off_chip if isinstance(out, jax.ShapeDtypeStruct) else on_chip

    return pl.pallas_call(
        functools.partial(kernel, **static),
        out_shape=out_shape,
        in_specs=[off_chip if from_hbm else on_chip] * len(args),
        out_specs=tuple(map(spec, out_shape)) if many else spec(out_shape),
        input_output_aliases=aliases or {},
        compiler_params=pltpu.CompilerParams(vmem_limit_bytes=VMEM_LIMIT),
    )(*(pltpu.with_memory_space_constraint(arg, space) for arg in args))


def body(data, x_init, ufac, vfac):
    tiles = lax.axis_size("tile")
    tile_rows, rank, _ = vfac.shape[1:]
    rows = data.shape[1]
    points = data.shape[2]
    group = tiles // tile_rows
    assert group == 4
    width = points // group
    lanes = 2 * width
    static = dict(group=group, width=width)
    shape = pltpu.VMEM
    result = jax.ShapeDtypeStruct

    def exchange(value, bit):
        return lax.ppermute(value, "tile", [(s, s ^ bit) for s in range(tiles)])

    def spread(value):
        return lax.all_to_all(value, "tile", split_axis=0, concat_axis=0, tiled=True)

    wide = ufac.shape[2]
    step = rows * 2 * lanes // wide
    assert wide % (2 * lanes) == 0 and step % 16 == 0
    chunks = shape((tiles, rank, lanes), bf16)
    sources = x_init.shape[1]
    tall = 2 * tile_rows * rank
    columns = (
        shape((sources // 2 + tall * sources // (2 * lanes), 2 * lanes), bf16),
        shape((sources, lanes), bf16),
        shape((sources, 2 * lanes), bf16),
        shape((sources, lanes), f32),
    )
    by_columns = tile_rows == 4
    coeffs, to_far, to_near, own, ufac, estimate, vfac, *columns = call(
        first_kernel,
        (
            result(chunks.shape, bf16),
            shape((2 * rows + 2 * step, wide), bf16),
            shape((2 * rows + step, wide), bf16),
            shape((rows, lanes), f32),
            shape(ufac.shape, bf16),
            shape(x_init.shape, f32),
            shape(vfac.shape, bf16),
        ) + (columns if by_columns else ()),
        data, x_init, ufac, vfac, from_hbm=True, **static,
    )
    far = exchange(to_far, 2)
    near = exchange(to_near, 1)
    corner = exchange(far, 1)
    gathered = (own, ufac, near, far, corner)
    block = shape((rows, lanes), f32)
    row_outs = (chunks, block, block, shape((2, rows, lanes), f32))
    received = spread(coeffs)
    if by_columns:
        piece = shape((group, rank, lanes), bf16)
        side = (tile_rows * rank, lanes)
        counted = dict(count=tile_rows, **static)

        def along_rows(pieces):
            order = {b: exchange(pieces[b], b * group) for b in range(tile_rows - 1, 0, -1)}
            return [pieces[0]] + [order[b] for b in range(1, tile_rows)]

        x_shared, x_far, x_near, x_own = columns
        x_shared = exchange(x_shared, 2)
        x_far = exchange(x_far, 2)
        x_near = exchange(x_near, 1)
        v_near = exchange(vfac, 1)
        x_corner = exchange(x_shared, 1)
        pieces = call(row_first_kernel, (piece,) * tile_rows, received, *gathered, **static)
        pieces = along_rows(pieces)
        *pieces, adj_own, adj_near, adj_far = call(
            middle_columns_kernel,
            (piece,) * tile_rows + (shape(side, bf16), shape(side, bf16), shape((2,) + side, bf16)),
            *pieces, x_own, vfac, x_near, v_near, x_far, x_shared, x_corner, **counted,
        )
        pieces = along_rows(pieces)
        adj_far = exchange(adj_far, 2)
        adj_near = exchange(adj_near, 1)
        adj_corner = exchange(adj_far, 1)
        row = call(row_last_kernel, row_outs, *pieces, *gathered, **counted)
        estimate = call(
            own_column_kernel, shape(x_init.shape, f32),
            adj_own, adj_near, adj_far, adj_corner, estimate, vfac, aliases={4: 0}, **static,
        )
    else:
        (pieces,) = call(row_kernel, (chunks,), received, *gathered, width=width)
        estimate, coeffs = call(
            middle_kernel, (shape(x_init.shape, f32), chunks), spread(pieces), estimate, vfac, **static
        )
        row = call(row_kernel, row_outs, spread(coeffs), *gathered, width=width)
    adjoint, misfit, to_near, to_far = row
    misfit_far = exchange(to_far, 2)
    misfit_near = exchange(to_near, 1)
    misfit_corner = exchange(misfit_far, 1)
    adjoint = spread(adjoint)
    solved = call(last_kernel, result(x_init.shape, f32), adjoint, estimate, vfac, **static)
    residual = call(
        residual_kernel, result(data.shape, f32), misfit, misfit_near, misfit_far, misfit_corner, **static
    )
    return (solved, residual)


def solution(mesh):
    in_specs = (
        P("freq", "tile", None),
        P("freq", "tile", None),
        P("freq", "tile", None),
        P("freq", None, None, "tile"),
    )
    out_specs = (P("freq", "tile", None), P("freq", "tile", None))
    return jax.shard_map(body, mesh=mesh, in_specs=in_specs, out_specs=out_specs, check_vma=False)
```

```python
import functools

import jax
import jax.numpy as jnp
from jax import lax
from jax.experimental import pallas as pl
from jax.experimental.pallas import tpu as pltpu
from jax.sharding import PartitionSpec as P


STEP = 0.4
THRESHOLD = 0.4
VMEM_LIMIT = 24 << 20
PIECES = 4

f32 = jnp.float32
bf16 = jnp.bfloat16


def dot(a, b, dims=((1,), (0,))):
    return lax.dot_general(a, b, (dims, ((), ())), preferred_element_type=f32)


def swap_halves(a):
    return pltpu.roll(a, a.shape[1] // 2, 1)


def left_half(a):
    return lax.broadcasted_iota(jnp.int32, a.shape, 1) < a.shape[1] // 2


def times_i(a):
    s = swap_halves(a)
    return jnp.where(left_half(a), -s, s)


def interleave(re, im):
    low = left_half(re)
    return (
        jnp.where(low, re, swap_halves(im)),
        jnp.where(low, swap_halves(re), im),
    )


def slices_of(re, im, width):
    out = []
    for k in range(re.shape[1] // (2 * width)):
        cut = slice(2 * width * k, 2 * width * (k + 1))
        out.extend(interleave(re[:, cut], im[:, cut]))
    return out


def group_index(group):
    return lax.rem(lax.axis_index("tile"), group)


def row_index(group):
    return lax.div(lax.axis_index("tile"), group)


def split(block):
    high = block.astype(bf16)
    low = (block - high.astype(f32)).astype(bf16)
    return high, low


def send_coeffs(vcat, xr, xi, out, *, group, width):
    half = vcat.shape[0] // 2
    t1 = dot(vcat, xr)
    t2 = dot(vcat, xi)
    cr = t1[:half] + t2[half:]
    ci = t2[:half] - t1[half:]
    rank = out.shape[1]
    blocks = slices_of(cr, ci, width)
    for i in range(half // rank):
        for q in range(group):
            out[i * group + q] = blocks[q][i * rank:(i + 1) * rank].astype(bf16)


def flat_factors(vfac, cut=slice(None)):
    parts, rows, rank, _ = vfac.shape
    return vfac[:, :, :, cut].reshape(parts * rows * rank, -1)


def first_kernel(data, x, ufac, vfac, out, waves, to_far, to_near, own, u_own, x_own, v_own, *columns, group, width):
    rows = data.shape[1]
    sources = x.shape[1]
    lanes = 2 * width
    folds = ufac.shape[2] // (2 * lanes)
    step = rows // folds
    q = group_index(group)

    def run(stage, scratch, quarters, sems):
        x_copy = pltpu.make_async_copy(x, x_own, sems.at[0])
        v_copy = pltpu.make_async_copy(vfac, v_own, sems.at[1])
        wave_copy = pltpu.make_async_copy(data, waves, sems.at[2])
        u_copy = pltpu.make_async_copy(ufac, u_own, sems.at[3])
        out_copy = pltpu.make_async_copy(stage, out, sems.at[4])
        for copy in (x_copy, v_copy, wave_copy, u_copy):
            copy.start()
        v_copy.wait()
        x_copy.wait()
        send_coeffs(
            flat_factors(v_own), x_own[0].astype(bf16), x_own[1].astype(bf16), stage, group=group, width=width
        )
        out_copy.start()
        wave_copy.wait()
        for s, block in enumerate(slices_of(waves[0], waves[1], width)):
            scratch[jnp.bitwise_xor(q, s)] = block
        own[...] = scratch[0]
        for ref, base, b in ((to_near, 0, 1), (to_far, 0, 2), (to_far, step, 3)):
            high, low = split(scratch[b])
            for g in range(folds):
                cut = slice(g * step, (g + 1) * step)
                lane = 2 * lanes * g
                ref[base:base + step, lane:lane + lanes] = high[cut]
                ref[base:base + step, lane + lanes:lane + 2 * lanes] = low[cut]
        u_copy.wait()
        for part in range(2):
            to_near[step + rows * part:step + rows * (part + 1)] = u_own[part]
            to_far[2 * step + rows * part:2 * step + rows * (part + 1)] = u_own[part]
        if columns:
            shared_x, far_x, near_x, block_x = columns
            tall = 2 * v_own.shape[1] * v_own.shape[2]
            for s, block in enumerate(slices_of(x_own[0], x_own[1], width)):
                quarters[jnp.bitwise_xor(q, s)] = block
            block_x[...] = quarters[0]
            high, low = split(quarters[1])
            near_x[:, :lanes] = high
            near_x[:, lanes:] = low
            far_x[...] = quarters[2].astype(bf16)
            half = sources // 2
            shared_x[:half, :lanes] = quarters[3, :half].astype(bf16)
            shared_x[:half, lanes:] = quarters[3, half:].astype(bf16)
            for h in range(sources // (2 * lanes)):
                cut = slice(h * 2 * lanes, (h + 1) * 2 * lanes)
                shared_x[half + h * tall:half + (h + 1) * tall] = flat_factors(v_own, cut)
        out_copy.wait()

    pl.run_scoped(
        run,
        pltpu.VMEM(out.shape, bf16),
        pltpu.VMEM((group, rows, lanes), f32),
        pltpu.VMEM((group, sources, lanes), f32),
        pltpu.SemaphoreType.DMA((5,)),
    )


def row_core(c, own, ufac, near, far, corner, width):
    lanes = 2 * width
    rows = own.shape[0]
    ci = times_i(c.astype(f32)).astype(bf16)
    folds = ufac.shape[2] // (2 * lanes)
    step = rows // folds

    def joined(ref, base):
        cuts = [ref[base:base + step, 2 * lanes * g:2 * lanes * (g + 1)].astype(f32) for g in range(folds)]
        pair = jnp.concatenate(cuts, axis=0)
        return pair[:, :lanes] + pair[:, lanes:]

    def factors(ref, base):
        return ref[base:base + rows], ref[base + rows:base + 2 * rows]

    blocks = (
        (own[...], (ufac[0], ufac[1])),
        (joined(near, 0), factors(near, step)),
        (joined(far, 0), factors(far, 2 * step)),
        (joined(corner, step), factors(corner, 2 * step)),
    )
    total = None
    for wave, (ur, ui) in blocks:
        misfit = wave - (dot(ur, c) + dot(ui, ci))
        mt = misfit.T.astype(bf16)
        mr, mi = mt[:width], mt[width:]
        turned = jnp.concatenate([mi, -mr], axis=0)
        term = dot(mt, ur) + dot(turned, ui)
        total = term if total is None else total + term
    return total.T.astype(bf16)


def to_chunks(flat, adjoint):
    rank = adjoint.shape[1]
    for j in range(adjoint.shape[0]):
        adjoint[j] = flat[j * rank:(j + 1) * rank]


def row_kernel(coeffs, own, ufac, near, far, corner, adjoint, *, width):
    c = coeffs[...].reshape(-1, 2 * width)
    to_chunks(row_core(c, own, ufac, near, far, corner, width), adjoint)


def row_first_kernel(coeffs, own, ufac, near, far, corner, *pieces, group, width):
    z = row_index(group)
    rank = coeffs.shape[1]
    c = coeffs[...].reshape(-1, 2 * width)
    flat = row_core(c, own, ufac, near, far, corner, width)

    def place(scratch):
        for j in range(flat.shape[0] // rank):
            scratch[jnp.bitwise_xor(z, j // group), j % group] = flat[j * rank:(j + 1) * rank]
        for b, piece in enumerate(pieces):
            piece[...] = scratch[b]

    pl.run_scoped(place, pltpu.VMEM((len(pieces),) + pieces[0].shape, bf16))


def row_last_kernel(*refs, group, width, count):
    pieces, (own, ufac, near, far, corner, adjoint, coeffs) = refs[:count], refs[count:]
    z = row_index(group)

    def run(scratch):
        for b, piece in enumerate(pieces):
            scratch[jnp.bitwise_xor(z, b)] = piece[...]
        c = scratch[...].reshape(-1, 2 * width)
        coeffs[...] = c
        to_chunks(row_core(c, own, ufac, near, far, corner, width), adjoint)

    pl.run_scoped(run, pltpu.VMEM((count,) + pieces[0].shape, bf16))


def middle_columns_kernel(*refs, group, width, count):
    pieces, refs = refs[:count], refs[count:]
    (x_own, v_own, near, v_near, far, shared, corner), refs = refs[:7], refs[7:]
    outs, (adj_own, adj_near, adj_far) = refs[:count], refs[count:]
    q = group_index(group)
    z = row_index(group)
    sources, lanes = x_own.shape
    rank = pieces[0].shape[1]
    side = count * rank
    tall = 2 * side

    half = sources // 2

    def factors(ref):
        wide = ref.shape[1]
        cuts = [ref[half + h * tall:half + (h + 1) * tall] for h in range(sources // wide)]
        return jnp.concatenate(cuts, axis=1)

    def run(adj, coeffs):
        for b, piece in enumerate(pieces):
            for k in range(group):
                adj[k, jnp.bitwise_xor(z, b)] = piece[jnp.bitwise_xor(q, k)]
        exact = near[...].astype(f32)
        columns = (
            (x_own[...], flat_factors(v_own)),
            (exact[:, :lanes] + exact[:, lanes:], flat_factors(v_near)),
            (far[...].astype(f32), factors(shared)),
            (
                jnp.concatenate([corner[:half, :lanes], corner[:half, lanes:]], axis=0).astype(f32),
                factors(corner),
            ),
        )
        for k, (x, vcat) in enumerate(columns):
            a = adj[k].reshape(side, lanes)
            if k == 0:
                adj_own[...] = a
            elif k == 1:
                adj_near[...] = a
            else:
                adj_far[k - 2] = a
            turned = times_i(a.astype(f32)).astype(bf16)
            s = x + STEP * dot(vcat, jnp.concatenate([a, turned], axis=0), ((0,), (0,)))
            square = s * s
            magnitude = jnp.sqrt(square + swap_halves(square))
            factor = jnp.maximum(magnitude - THRESHOLD, 0.0) / jnp.maximum(magnitude, THRESHOLD)
            t = dot(vcat, (s * factor).astype(bf16))
            c = (t[:side] - times_i(t[side:])).astype(bf16)
            for i in range(count):
                coeffs[i, jnp.bitwise_xor(q, k)] = c[i * rank:(i + 1) * rank]
        for b, out in enumerate(outs):
            out[...] = coeffs[jnp.bitwise_xor(z, b)]

    pl.run_scoped(
        run,
        pltpu.VMEM((group, count, rank, lanes), bf16),
        pltpu.VMEM((count, group, rank, lanes), bf16),
    )


def own_column_kernel(adj_own, adj_near, adj_far, adj_corner, x, vfac, x_new, *, group, width):
    q = group_index(group)

    def run(scratch):
        scratch[0] = adj_own[...]
        scratch[1] = adj_near[...]
        scratch[2] = adj_far[0]
        scratch[3] = adj_corner[1]
        sides = sides_of([scratch[jnp.bitwise_xor(q, s)].astype(f32) for s in range(group)])
        x_new[0], x_new[1] = updated(sides, x[0], x[1], flat_factors(vfac))

    pl.run_scoped(run, pltpu.VMEM((group,) + adj_own.shape, bf16))


def sides_of(quarters):
    pairs = [interleave(*quarters[k:k + 2]) for k in range(0, len(quarters), 2)]
    re = jnp.concatenate([r for r, _ in pairs], axis=1)
    im = jnp.concatenate([i for _, i in pairs], axis=1)
    real_side = jnp.concatenate([re, -im], axis=0).astype(bf16)
    imag_side = jnp.concatenate([im, re], axis=0).astype(bf16)
    return real_side, imag_side


def adjoint_sides(adjoint, *, group):
    count, rank, lanes = adjoint.shape
    rows = count // group
    a = adjoint[...].astype(f32).reshape(rows, group, rank, lanes)
    return sides_of([a[:, s].reshape(rows * rank, lanes) for s in range(group)])


def shrink(sr, si):
    magnitude = jnp.sqrt(sr * sr + si * si)
    factor = jnp.maximum(magnitude - THRESHOLD, 0.0) / jnp.maximum(magnitude, THRESHOLD)
    return sr * factor, si * factor


def updated(sides, xr, xi, vcat):
    gr, gi = (dot(vcat, side, ((0,), (0,))) for side in sides)
    return shrink(xr + STEP * gr, xi + STEP * gi)


def middle_kernel(adjoint, x, vfac, x_new, out, *, group, width):
    vcat = flat_factors(vfac)
    xr, xi = updated(adjoint_sides(adjoint, group=group), x[0], x[1], vcat)
    x_new[0] = xr
    x_new[1] = xi
    send_coeffs(vcat, xr.astype(bf16), xi.astype(bf16), out, group=group, width=width)


def last_kernel(adjoint, x, vfac, x_new, *, group, width):
    sources = x.shape[1]
    piece = sources // PIECES

    def run(stage, sems):
        sides = adjoint_sides(adjoint, group=group)
        copies = []
        for k in range(PIECES):
            cut = slice(k * piece, (k + 1) * piece)
            stage[0, cut], stage[1, cut] = updated(sides, x[0, cut], x[1, cut], flat_factors(vfac, cut))
            copies.append(pltpu.make_async_copy(stage.at[:, cut], x_new.at[:, cut], sems.at[k]))
            copies[-1].start()
        for copy in copies:
            copy.wait()

    pl.run_scoped(run, pltpu.VMEM(x.shape, f32), pltpu.SemaphoreType.DMA((PIECES,)))


def residual_kernel(own, near, far, corner, ufac, data, out, *, group, width):
    q = group_index(group)
    lanes = 2 * width
    ur, ui = ufac[0], ufac[1]

    def place(scratch, stage, sem):
        for b, ref in enumerate((own, near, far, corner)):
            c = ref[...]
            scratch[b] = dot(ur, c) + dot(ui, times_i(c.astype(f32)).astype(bf16))
        for k in range(group // 2):
            cut = slice(lanes * k, lanes * (k + 1))
            pair = (scratch[jnp.bitwise_xor(q, s)] for s in (2 * k, 2 * k + 1))
            for part, predicted in enumerate(interleave(*pair)):
                stage[part, :, cut] = data[part, :, cut] - predicted
        copy = pltpu.make_async_copy(stage, out, sem)
        copy.start()
        copy.wait()

    pl.run_scoped(
        place,
        pltpu.VMEM((group, data.shape[1], lanes), f32),
        pltpu.VMEM(out.shape, f32),
        pltpu.SemaphoreType.DMA(()),
    )


def call(kernel, out_shape, *args, from_hbm=False, aliases=None, **static):
    on_chip = pl.BlockSpec(memory_space=pltpu.VMEM)
    off_chip = pl.BlockSpec(memory_space=pltpu.HBM)
    space = pltpu.HBM if from_hbm else pltpu.VMEM
    many = isinstance(out_shape, tuple)

    def spec(out):
        return off_chip if isinstance(out, jax.ShapeDtypeStruct) else on_chip

    return pl.pallas_call(
        functools.partial(kernel, **static),
        out_shape=out_shape,
        in_specs=[off_chip if from_hbm else on_chip] * len(args),
        out_specs=tuple(map(spec, out_shape)) if many else spec(out_shape),
        input_output_aliases=aliases or {},
        compiler_params=pltpu.CompilerParams(vmem_limit_bytes=VMEM_LIMIT),
    )(*(pltpu.with_memory_space_constraint(arg, space) for arg in args))


def body(data, x_init, ufac, vfac):
    tiles = lax.axis_size("tile")
    tile_rows, rank, _ = vfac.shape[1:]
    rows = data.shape[1]
    points = data.shape[2]
    group = tiles // tile_rows
    assert group == 4
    width = points // group
    lanes = 2 * width
    static = dict(group=group, width=width)
    shape = pltpu.VMEM
    result = jax.ShapeDtypeStruct

    def exchange(value, bit):
        return lax.ppermute(value, "tile", [(s, s ^ bit) for s in range(tiles)])

    def spread(value):
        return lax.all_to_all(value, "tile", split_axis=0, concat_axis=0, tiled=True)

    wide = ufac.shape[2]
    step = rows * 2 * lanes // wide
    assert wide % (2 * lanes) == 0 and step % 16 == 0
    chunks = shape((tiles, rank, lanes), bf16)
    sources = x_init.shape[1]
    tall = 2 * tile_rows * rank
    columns = (
        shape((sources // 2 + tall * sources // (2 * lanes), 2 * lanes), bf16),
        shape((sources, lanes), bf16),
        shape((sources, 2 * lanes), bf16),
        shape((sources, lanes), f32),
    )
    by_columns = tile_rows == 4
    coeffs, data, to_far, to_near, own, ufac, estimate, vfac, *columns = call(
        first_kernel,
        (
            result(chunks.shape, bf16),
            shape(data.shape, f32),
            shape((2 * rows + 2 * step, wide), bf16),
            shape((2 * rows + step, wide), bf16),
            shape((rows, lanes), f32),
            shape(ufac.shape, bf16),
            shape(x_init.shape, f32),
            shape(vfac.shape, bf16),
        ) + (columns if by_columns else ()),
        data, x_init, ufac, vfac, from_hbm=True, **static,
    )
    far = exchange(to_far, 2)
    near = exchange(to_near, 1)
    corner = exchange(far, 1)
    gathered = (own, ufac, near, far, corner)
    flat = (tiles * rank, lanes)
    received = spread(coeffs)
    if by_columns:
        piece = shape((group, rank, lanes), bf16)
        side = (tile_rows * rank, lanes)
        counted = dict(count=tile_rows, **static)

        def along_rows(pieces):
            order = {b: exchange(pieces[b], b * group) for b in range(tile_rows - 1, 0, -1)}
            return [pieces[0]] + [order[b] for b in range(1, tile_rows)]

        x_shared, x_far, x_near, x_own = columns
        x_shared = exchange(x_shared, 2)
        x_far = exchange(x_far, 2)
        x_near = exchange(x_near, 1)
        v_near = exchange(vfac, 1)
        x_corner = exchange(x_shared, 1)
        pieces = call(row_first_kernel, (piece,) * tile_rows, received, *gathered, **static)
        pieces = along_rows(pieces)
        *pieces, adj_own, adj_near, adj_far = call(
            middle_columns_kernel,
            (piece,) * tile_rows + (shape(side, bf16), shape(side, bf16), shape((2,) + side, bf16)),
            *pieces, x_own, vfac, x_near, v_near, x_far, x_shared, x_corner, **counted,
        )
        pieces = along_rows(pieces)
        adj_far = exchange(adj_far, 2)
        adj_near = exchange(adj_near, 1)
        adj_corner = exchange(adj_far, 1)
        adjoint, coeffs = call(row_last_kernel, (chunks, shape(flat, bf16)), *pieces, *gathered, **counted)
        estimate = call(
            own_column_kernel, shape(x_init.shape, f32),
            adj_own, adj_near, adj_far, adj_corner, estimate, vfac, aliases={4: 0}, **static,
        )
    else:
        pieces = call(row_kernel, chunks, received, *gathered, width=width)
        estimate, coeffs = call(
            middle_kernel, (shape(x_init.shape, f32), chunks), spread(pieces), estimate, vfac, **static
        )
        received = spread(coeffs)
        adjoint = call(row_kernel, chunks, received, *gathered, width=width)
        coeffs = received.reshape(flat)
    coeffs_far = exchange(coeffs, 2)
    coeffs_near = exchange(coeffs, 1)
    coeffs_corner = exchange(coeffs_far, 1)
    adjoint = spread(adjoint)
    solved = call(last_kernel, result(x_init.shape, f32), adjoint, estimate, vfac, **static)
    residual = call(
        residual_kernel, result(data.shape, f32),
        coeffs, coeffs_near, coeffs_far, coeffs_corner, ufac, data, **static,
    )
    return (solved, residual)


def solution(mesh):
    in_specs = (
        P("freq", "tile", None),
        P("freq", "tile", None),
        P("freq", "tile", None),
        P("freq", None, None, "tile"),
    )
    out_specs = (P("freq", "tile", None), P("freq", "tile", None))
    return jax.shard_map(body, mesh=mesh, in_specs=in_specs, out_specs=out_specs, check_vma=False)
```

```python
import functools

import jax
import jax.numpy as jnp
from jax import lax
from jax.experimental import pallas as pl
from jax.experimental.pallas import tpu as pltpu
from jax.sharding import PartitionSpec as P


STEP = 0.4
THRESHOLD = 0.4
VMEM_LIMIT = 24 << 20
PIECES = 4

f32 = jnp.float32
bf16 = jnp.bfloat16


def dot(a, b, dims=((1,), (0,))):
    return lax.dot_general(a, b, (dims, ((), ())), preferred_element_type=f32)


def swap_halves(a):
    return pltpu.roll(a, a.shape[1] // 2, 1)


def left_half(a):
    return lax.broadcasted_iota(jnp.int32, a.shape, 1) < a.shape[1] // 2


def times_i(a):
    s = swap_halves(a)
    return jnp.where(left_half(a), -s, s)


def interleave(re, im):
    low = left_half(re)
    return (
        jnp.where(low, re, swap_halves(im)),
        jnp.where(low, swap_halves(re), im),
    )


def slices_of(re, im, width):
    out = []
    for k in range(re.shape[1] // (2 * width)):
        cut = slice(2 * width * k, 2 * width * (k + 1))
        out.extend(interleave(re[:, cut], im[:, cut]))
    return out


def group_index(group):
    return lax.rem(lax.axis_index("tile"), group)


def row_index(group):
    return lax.div(lax.axis_index("tile"), group)


def split(block):
    high = block.astype(bf16)
    low = (block - high.astype(f32)).astype(bf16)
    return high, low


def send_coeffs(vcat, xr, xi, out, *, group, width):
    half = vcat.shape[0] // 2
    t1 = dot(vcat, xr)
    t2 = dot(vcat, xi)
    cr = t1[:half] + t2[half:]
    ci = t2[:half] - t1[half:]
    rank = out.shape[1]
    blocks = slices_of(cr, ci, width)
    for i in range(half // rank):
        for q in range(group):
            out[i * group + q] = blocks[q][i * rank:(i + 1) * rank].astype(bf16)


def flat_factors(vfac, cut=slice(None)):
    parts, rows, rank, _ = vfac.shape
    return vfac[:, :, :, cut].reshape(parts * rows * rank, -1)


def first_kernel(data, x, ufac, vfac, out, kept, to_far, to_near, own, u_own, x_own, v_own, *columns, group, width):
    rows = data.shape[1]
    sources = x.shape[1]
    lanes = 2 * width
    folds = ufac.shape[2] // (2 * lanes)
    step = rows // folds
    q = group_index(group)

    def run(stage, waves, scratch, quarters, sems):
        x_copy = pltpu.make_async_copy(x, x_own, sems.at[0])
        v_copy = pltpu.make_async_copy(vfac, v_own, sems.at[1])
        wave_copy = pltpu.make_async_copy(data, waves, sems.at[2])
        u_copy = pltpu.make_async_copy(ufac, u_own, sems.at[3])
        out_copy = pltpu.make_async_copy(stage, out, sems.at[4])
        for copy in (x_copy, v_copy, wave_copy, u_copy):
            copy.start()
        v_copy.wait()
        x_copy.wait()
        send_coeffs(
            flat_factors(v_own), x_own[0].astype(bf16), x_own[1].astype(bf16), stage, group=group, width=width
        )
        out_copy.start()
        wave_copy.wait()
        for s, block in enumerate(slices_of(waves[0], waves[1], width)):
            scratch[jnp.bitwise_xor(q, s)] = block
        own[...] = scratch[0]
        kept[...] = waves[...]
        for ref, base, b in ((to_near, 0, 1), (to_far, 0, 2), (to_far, step, 3)):
            high, low = split(scratch[b])
            for g in range(folds):
                cut = slice(g * step, (g + 1) * step)
                lane = 2 * lanes * g
                ref[base:base + step, lane:lane + lanes] = high[cut]
                ref[base:base + step, lane + lanes:lane + 2 * lanes] = low[cut]
        u_copy.wait()
        for part in range(2):
            to_near[step + rows * part:step + rows * (part + 1)] = u_own[part]
            to_far[2 * step + rows * part:2 * step + rows * (part + 1)] = u_own[part]
        if columns:
            shared_x, far_x, near_x, block_x = columns
            tall = 2 * v_own.shape[1] * v_own.shape[2]
            for s, block in enumerate(slices_of(x_own[0], x_own[1], width)):
                quarters[jnp.bitwise_xor(q, s)] = block
            block_x[...] = quarters[0]
            high, low = split(quarters[1])
            near_x[:, :lanes] = high
            near_x[:, lanes:] = low
            far_x[...] = quarters[2].astype(bf16)
            half = sources // 2
            shared_x[:half, :lanes] = quarters[3, :half].astype(bf16)
            shared_x[:half, lanes:] = quarters[3, half:].astype(bf16)
            for h in range(sources // (2 * lanes)):
                cut = slice(h * 2 * lanes, (h + 1) * 2 * lanes)
                shared_x[half + h * tall:half + (h + 1) * tall] = flat_factors(v_own, cut)
        out_copy.wait()

    pl.run_scoped(
        run,
        pltpu.VMEM(out.shape, bf16),
        pltpu.VMEM(data.shape, f32),
        pltpu.VMEM((group, rows, lanes), f32),
        pltpu.VMEM((group, sources, lanes), f32),
        pltpu.SemaphoreType.DMA((5,)),
    )


def row_core(c, own, ufac, near, far, corner, width):
    lanes = 2 * width
    rows = own.shape[0]
    ci = times_i(c.astype(f32)).astype(bf16)
    folds = ufac.shape[2] // (2 * lanes)
    step = rows // folds

    def joined(ref, base):
        cuts = [ref[base:base + step, 2 * lanes * g:2 * lanes * (g + 1)].astype(f32) for g in range(folds)]
        pair = jnp.concatenate(cuts, axis=0)
        return pair[:, :lanes] + pair[:, lanes:]

    def factors(ref, base):
        return ref[base:base + rows], ref[base + rows:base + 2 * rows]

    blocks = (
        (own[...], (ufac[0], ufac[1])),
        (joined(near, 0), factors(near, step)),
        (joined(far, 0), factors(far, 2 * step)),
        (joined(corner, step), factors(corner, 2 * step)),
    )
    total = None
    for wave, (ur, ui) in blocks:
        misfit = wave - (dot(ur, c) + dot(ui, ci))
        mt = misfit.T.astype(bf16)
        mr, mi = mt[:width], mt[width:]
        turned = jnp.concatenate([mi, -mr], axis=0)
        term = dot(mt, ur) + dot(turned, ui)
        total = term if total is None else total + term
    return total.T.astype(bf16)


def to_chunks(flat, adjoint):
    rank = adjoint.shape[1]
    for j in range(adjoint.shape[0]):
        adjoint[j] = flat[j * rank:(j + 1) * rank]


def row_kernel(coeffs, own, ufac, near, far, corner, adjoint, *, width):
    c = coeffs[...].reshape(-1, 2 * width)
    to_chunks(row_core(c, own, ufac, near, far, corner, width), adjoint)


def row_first_kernel(coeffs, own, ufac, near, far, corner, *pieces, group, width):
    z = row_index(group)
    rank = coeffs.shape[1]
    c = coeffs[...].reshape(-1, 2 * width)
    flat = row_core(c, own, ufac, near, far, corner, width)

    def place(scratch):
        for j in range(flat.shape[0] // rank):
            scratch[jnp.bitwise_xor(z, j // group), j % group] = flat[j * rank:(j + 1) * rank]
        for b, piece in enumerate(pieces):
            piece[...] = scratch[b]

    pl.run_scoped(place, pltpu.VMEM((len(pieces),) + pieces[0].shape, bf16))


def row_last_kernel(*refs, group, width, count):
    pieces, (own, ufac, near, far, corner, adjoint, coeffs) = refs[:count], refs[count:]
    z = row_index(group)

    def run(scratch):
        for b, piece in enumerate(pieces):
            scratch[jnp.bitwise_xor(z, b)] = piece[...]
        c = scratch[...].reshape(-1, 2 * width)
        coeffs[...] = c
        to_chunks(row_core(c, own, ufac, near, far, corner, width), adjoint)

    pl.run_scoped(run, pltpu.VMEM((count,) + pieces[0].shape, bf16))


def middle_columns_kernel(*refs, group, width, count):
    pieces, refs = refs[:count], refs[count:]
    (x_own, v_own, near, v_near, far, shared, corner), refs = refs[:7], refs[7:]
    outs, (adj_own, adj_near, adj_far) = refs[:count], refs[count:]
    q = group_index(group)
    z = row_index(group)
    sources, lanes = x_own.shape
    rank = pieces[0].shape[1]
    side = count * rank
    tall = 2 * side

    half = sources // 2

    def factors(ref):
        wide = ref.shape[1]
        cuts = [ref[half + h * tall:half + (h + 1) * tall] for h in range(sources // wide)]
        return jnp.concatenate(cuts, axis=1)

    def run(adj, coeffs):
        for b, piece in enumerate(pieces):
            for k in range(group):
                adj[k, jnp.bitwise_xor(z, b)] = piece[jnp.bitwise_xor(q, k)]
        exact = near[...].astype(f32)
        columns = (
            (x_own[...], flat_factors(v_own)),
            (exact[:, :lanes] + exact[:, lanes:], flat_factors(v_near)),
            (far[...].astype(f32), factors(shared)),
            (
                jnp.concatenate([corner[:half, :lanes], corner[:half, lanes:]], axis=0).astype(f32),
                factors(corner),
            ),
        )
        for k, (x, vcat) in enumerate(columns):
            a = adj[k].reshape(side, lanes)
            if k == 0:
                adj_own[...] = a
            elif k == 1:
                adj_near[...] = a
            else:
                adj_far[k - 2] = a
            turned = times_i(a.astype(f32)).astype(bf16)
            s = x + STEP * dot(vcat, jnp.concatenate([a, turned], axis=0), ((0,), (0,)))
            square = s * s
            magnitude = jnp.sqrt(square + swap_halves(square))
            factor = jnp.maximum(magnitude - THRESHOLD, 0.0) / jnp.maximum(magnitude, THRESHOLD)
            t = dot(vcat, (s * factor).astype(bf16))
            c = (t[:side] - times_i(t[side:])).astype(bf16)
            for i in range(count):
                coeffs[i, jnp.bitwise_xor(q, k)] = c[i * rank:(i + 1) * rank]
        for b, out in enumerate(outs):
            out[...] = coeffs[jnp.bitwise_xor(z, b)]

    pl.run_scoped(
        run,
        pltpu.VMEM((group, count, rank, lanes), bf16),
        pltpu.VMEM((count, group, rank, lanes), bf16),
    )


def own_column_kernel(adj_own, adj_near, adj_far, adj_corner, x, vfac, x_new, *, group, width):
    q = group_index(group)

    def run(scratch):
        scratch[0] = adj_own[...]
        scratch[1] = adj_near[...]
        scratch[2] = adj_far[0]
        scratch[3] = adj_corner[1]
        sides = sides_of([scratch[jnp.bitwise_xor(q, s)].astype(f32) for s in range(group)])
        x_new[0], x_new[1] = updated(sides, x[0], x[1], flat_factors(vfac))

    pl.run_scoped(run, pltpu.VMEM((group,) + adj_own.shape, bf16))


def sides_of(quarters):
    pairs = [interleave(*quarters[k:k + 2]) for k in range(0, len(quarters), 2)]
    re = jnp.concatenate([r for r, _ in pairs], axis=1)
    im = jnp.concatenate([i for _, i in pairs], axis=1)
    real_side = jnp.concatenate([re, -im], axis=0).astype(bf16)
    imag_side = jnp.concatenate([im, re], axis=0).astype(bf16)
    return real_side, imag_side


def adjoint_sides(adjoint, *, group):
    count, rank, lanes = adjoint.shape
    rows = count // group
    a = adjoint[...].astype(f32).reshape(rows, group, rank, lanes)
    return sides_of([a[:, s].reshape(rows * rank, lanes) for s in range(group)])


def shrink(sr, si):
    magnitude = jnp.sqrt(sr * sr + si * si)
    factor = jnp.maximum(magnitude - THRESHOLD, 0.0) / jnp.maximum(magnitude, THRESHOLD)
    return sr * factor, si * factor


def updated(sides, xr, xi, vcat):
    gr, gi = (dot(vcat, side, ((0,), (0,))) for side in sides)
    return shrink(xr + STEP * gr, xi + STEP * gi)


def middle_kernel(adjoint, x, vfac, x_new, out, *, group, width):
    vcat = flat_factors(vfac)
    xr, xi = updated(adjoint_sides(adjoint, group=group), x[0], x[1], vcat)
    x_new[0] = xr
    x_new[1] = xi
    send_coeffs(vcat, xr.astype(bf16), xi.astype(bf16), out, group=group, width=width)


def last_kernel(adjoint, x, vfac, misfit, x_new, residual, *, group, width):
    sources = x.shape[1]
    piece = sources // PIECES

    def run(stage, sems):
        copies = [pltpu.make_async_copy(misfit, residual, sems.at[PIECES])]
        copies[0].start()
        sides = adjoint_sides(adjoint, group=group)
        for k in range(PIECES):
            cut = slice(k * piece, (k + 1) * piece)
            stage[0, cut], stage[1, cut] = updated(sides, x[0, cut], x[1, cut], flat_factors(vfac, cut))
            copies.append(pltpu.make_async_copy(stage.at[:, cut], x_new.at[:, cut], sems.at[k]))
            copies[-1].start()
        for copy in copies:
            copy.wait()

    pl.run_scoped(run, pltpu.VMEM(x.shape, f32), pltpu.SemaphoreType.DMA((PIECES + 1,)))


def residual_kernel(own, near, far, corner, ufac, data, out, *, group, width):
    q = group_index(group)
    lanes = 2 * width
    ur, ui = ufac[0], ufac[1]

    def place(scratch):
        for b, ref in enumerate((own, near, far, corner)):
            c = ref[...]
            scratch[b] = dot(ur, c) + dot(ui, times_i(c.astype(f32)).astype(bf16))
        for k in range(group // 2):
            cut = slice(lanes * k, lanes * (k + 1))
            pair = (scratch[jnp.bitwise_xor(q, s)] for s in (2 * k, 2 * k + 1))
            for part, predicted in enumerate(interleave(*pair)):
                out[part, :, cut] = data[part, :, cut] - predicted

    pl.run_scoped(place, pltpu.VMEM((group, data.shape[1], lanes), f32))


def call(kernel, out_shape, *args, from_hbm=False, aliases=None, **static):
    on_chip = pl.BlockSpec(memory_space=pltpu.VMEM)
    off_chip = pl.BlockSpec(memory_space=pltpu.HBM)
    space = pltpu.HBM if from_hbm else pltpu.VMEM
    many = isinstance(out_shape, tuple)

    def spec(out):
        return off_chip if isinstance(out, jax.ShapeDtypeStruct) else on_chip

    return pl.pallas_call(
        functools.partial(kernel, **static),
        out_shape=out_shape,
        in_specs=[off_chip if from_hbm else on_chip] * len(args),
        out_specs=tuple(map(spec, out_shape)) if many else spec(out_shape),
        input_output_aliases=aliases or {},
        compiler_params=pltpu.CompilerParams(vmem_limit_bytes=VMEM_LIMIT),
    )(*(pltpu.with_memory_space_constraint(arg, space) for arg in args))


def body(data, x_init, ufac, vfac):
    tiles = lax.axis_size("tile")
    tile_rows, rank, _ = vfac.shape[1:]
    rows = data.shape[1]
    points = data.shape[2]
    group = tiles // tile_rows
    assert group == 4
    width = points // group
    lanes = 2 * width
    static = dict(group=group, width=width)
    shape = pltpu.VMEM
    result = jax.ShapeDtypeStruct

    def exchange(value, bit):
        return lax.ppermute(value, "tile", [(s, s ^ bit) for s in range(tiles)])

    def spread(value):
        return lax.all_to_all(value, "tile", split_axis=0, concat_axis=0, tiled=True)

    wide = ufac.shape[2]
    step = rows * 2 * lanes // wide
    assert wide % (2 * lanes) == 0 and step % 16 == 0
    chunks = shape((tiles, rank, lanes), bf16)
    sources = x_init.shape[1]
    tall = 2 * tile_rows * rank
    columns = (
        shape((sources // 2 + tall * sources // (2 * lanes), 2 * lanes), bf16),
        shape((sources, lanes), bf16),
        shape((sources, 2 * lanes), bf16),
        shape((sources, lanes), f32),
    )
    by_columns = tile_rows == 4
    coeffs, data, to_far, to_near, own, ufac, estimate, vfac, *columns = call(
        first_kernel,
        (
            result(chunks.shape, bf16),
            shape(data.shape, f32),
            shape((2 * rows + 2 * step, wide), bf16),
            shape((2 * rows + step, wide), bf16),
            shape((rows, lanes), f32),
            shape(ufac.shape, bf16),
            shape(x_init.shape, f32),
            shape(vfac.shape, bf16),
        ) + (columns if by_columns else ()),
        data, x_init, ufac, vfac, from_hbm=True, **static,
    )
    far = exchange(to_far, 2)
    near = exchange(to_near, 1)
    corner = exchange(far, 1)
    gathered = (own, ufac, near, far, corner)
    flat = (tiles * rank, lanes)
    received = spread(coeffs)
    if by_columns:
        piece = shape((group, rank, lanes), bf16)
        side = (tile_rows * rank, lanes)
        counted = dict(count=tile_rows, **static)

        def along_rows(pieces):
            order = {b: exchange(pieces[b], b * group) for b in range(tile_rows - 1, 0, -1)}
            return [pieces[0]] + [order[b] for b in range(1, tile_rows)]

        x_shared, x_far, x_near, x_own = columns
        x_shared = exchange(x_shared, 2)
        x_far = exchange(x_far, 2)
        x_near = exchange(x_near, 1)
        v_near = exchange(vfac, 1)
        x_corner = exchange(x_shared, 1)
        pieces = call(row_first_kernel, (piece,) * tile_rows, received, *gathered, **static)
        pieces = along_rows(pieces)
        *pieces, adj_own, adj_near, adj_far = call(
            middle_columns_kernel,
            (piece,) * tile_rows + (shape(side, bf16), shape(side, bf16), shape((2,) + side, bf16)),
            *pieces, x_own, vfac, x_near, v_near, x_far, x_shared, x_corner, **counted,
        )
        pieces = along_rows(pieces)
        adj_far = exchange(adj_far, 2)
        adj_near = exchange(adj_near, 1)
        adj_corner = exchange(adj_far, 1)
        adjoint, coeffs = call(row_last_kernel, (chunks, shape(flat, bf16)), *pieces, *gathered, **counted)
        estimate = call(
            own_column_kernel, shape(x_init.shape, f32),
            adj_own, adj_near, adj_far, adj_corner, estimate, vfac, aliases={4: 0}, **static,
        )
    else:
        pieces = call(row_kernel, chunks, received, *gathered, width=width)
        estimate, coeffs = call(
            middle_kernel, (shape(x_init.shape, f32), chunks), spread(pieces), estimate, vfac, **static
        )
        received = spread(coeffs)
        adjoint = call(row_kernel, chunks, received, *gathered, width=width)
        coeffs = received.reshape(flat)
    coeffs_far = exchange(coeffs, 2)
    coeffs_near = exchange(coeffs, 1)
    coeffs_corner = exchange(coeffs_far, 1)
    adjoint = spread(adjoint)
    misfit = call(
        residual_kernel, shape(data.shape, f32),
        coeffs, coeffs_near, coeffs_far, coeffs_corner, ufac, data, **static,
    )
    return call(
        last_kernel, (result(x_init.shape, f32), result(data.shape, f32)),
        adjoint, estimate, vfac, misfit, **static,
    )


def solution(mesh):
    in_specs = (
        P("freq", "tile", None),
        P("freq", "tile", None),
        P("freq", "tile", None),
        P("freq", None, None, "tile"),
    )
    out_specs = (P("freq", "tile", None), P("freq", "tile", None))
    return jax.shard_map(body, mesh=mesh, in_specs=in_specs, out_specs=out_specs, check_vma=False)
```

```python
import functools

import jax
import jax.numpy as jnp
from jax import lax
from jax.experimental import pallas as pl
from jax.experimental.pallas import tpu as pltpu
from jax.sharding import PartitionSpec as P


STEP = 0.4
THRESHOLD = 0.4
VMEM_LIMIT = 24 << 20
PIECES = 4

f32 = jnp.float32
bf16 = jnp.bfloat16


def dot(a, b, dims=((1,), (0,))):
    return lax.dot_general(a, b, (dims, ((), ())), preferred_element_type=f32)


def swap_halves(a):
    return pltpu.roll(a, a.shape[1] // 2, 1)


def left_half(a):
    return lax.broadcasted_iota(jnp.int32, a.shape, 1) < a.shape[1] // 2


def times_i(a):
    s = swap_halves(a)
    return jnp.where(left_half(a), -s, s)


def interleave(re, im):
    low = left_half(re)
    return (
        jnp.where(low, re, swap_halves(im)),
        jnp.where(low, swap_halves(re), im),
    )


def slices_of(re, im, width):
    out = []
    for k in range(re.shape[1] // (2 * width)):
        cut = slice(2 * width * k, 2 * width * (k + 1))
        out.extend(interleave(re[:, cut], im[:, cut]))
    return out


def group_index(group):
    return lax.rem(lax.axis_index("tile"), group)


def row_index(group):
    return lax.div(lax.axis_index("tile"), group)


def split(block):
    high = block.astype(bf16)
    low = (block - high.astype(f32)).astype(bf16)
    return high, low


def send_coeffs(vcat, xr, xi, out, *, group, width):
    half = vcat.shape[0] // 2
    t1 = dot(vcat, xr)
    t2 = dot(vcat, xi)
    cr = t1[:half] + t2[half:]
    ci = t2[:half] - t1[half:]
    rank = out.shape[1]
    blocks = slices_of(cr, ci, width)
    for i in range(half // rank):
        for q in range(group):
            out[i * group + q] = blocks[q][i * rank:(i + 1) * rank].astype(bf16)


def flat_factors(vfac, cut=slice(None)):
    parts, rows, rank, _ = vfac.shape
    return vfac[:, :, :, cut].reshape(parts * rows * rank, -1)


def first_kernel(data, x, ufac, vfac, out, to_far, to_near, own, u_own, x_own, v_own, *columns, group, width):
    rows = data.shape[1]
    sources = x.shape[1]
    lanes = 2 * width
    folds = ufac.shape[2] // (2 * lanes)
    step = rows // folds
    q = group_index(group)

    def run(stage, waves, scratch, quarters, sems):
        x_copy = pltpu.make_async_copy(x, x_own, sems.at[0])
        v_copy = pltpu.make_async_copy(vfac, v_own, sems.at[1])
        wave_copy = pltpu.make_async_copy(data, waves, sems.at[2])
        u_copy = pltpu.make_async_copy(ufac, u_own, sems.at[3])
        out_copy = pltpu.make_async_copy(stage, out, sems.at[4])
        for copy in (x_copy, v_copy, wave_copy, u_copy):
            copy.start()
        v_copy.wait()
        x_copy.wait()
        send_coeffs(
            flat_factors(v_own), x_own[0].astype(bf16), x_own[1].astype(bf16), stage, group=group, width=width
        )
        out_copy.start()
        wave_copy.wait()
        for s, block in enumerate(slices_of(waves[0], waves[1], width)):
            scratch[jnp.bitwise_xor(q, s)] = block
        own[...] = scratch[0]
        for ref, base, b in ((to_near, 0, 1), (to_far, 0, 2), (to_far, step, 3)):
            high, low = split(scratch[b])
            for g in range(folds):
                cut = slice(g * step, (g + 1) * step)
                lane = 2 * lanes * g
                ref[base:base + step, lane:lane + lanes] = high[cut]
                ref[base:base + step, lane + lanes:lane + 2 * lanes] = low[cut]
        u_copy.wait()
        for part in range(2):
            to_near[step + rows * part:step + rows * (part + 1)] = u_own[part]
            to_far[2 * step + rows * part:2 * step + rows * (part + 1)] = u_own[part]
        if columns:
            shared_x, far_x, near_x, block_x = columns
            tall = 2 * v_own.shape[1] * v_own.shape[2]
            for s, block in enumerate(slices_of(x_own[0], x_own[1], width)):
                quarters[jnp.bitwise_xor(q, s)] = block
            block_x[...] = quarters[0]
            high, low = split(quarters[1])
            near_x[:, :lanes] = high
            near_x[:, lanes:] = low
            far_x[...] = quarters[2].astype(bf16)
            half = sources // 2
            shared_x[:half, :lanes] = quarters[3, :half].astype(bf16)
            shared_x[:half, lanes:] = quarters[3, half:].astype(bf16)
            for h in range(sources // (2 * lanes)):
                cut = slice(h * 2 * lanes, (h + 1) * 2 * lanes)
                shared_x[half + h * tall:half + (h + 1) * tall] = flat_factors(v_own, cut)
        out_copy.wait()

    pl.run_scoped(
        run,
        pltpu.VMEM(out.shape, bf16),
        pltpu.VMEM(data.shape, f32),
        pltpu.VMEM((group, rows, lanes), f32),
        pltpu.VMEM((group, sources, lanes), f32),
        pltpu.SemaphoreType.DMA((5,)),
    )


def row_core(c, own, ufac, near, far, corner, width):
    lanes = 2 * width
    rows = own.shape[0]
    ci = times_i(c.astype(f32)).astype(bf16)
    folds = ufac.shape[2] // (2 * lanes)
    step = rows // folds

    def joined(ref, base):
        cuts = [ref[base:base + step, 2 * lanes * g:2 * lanes * (g + 1)].astype(f32) for g in range(folds)]
        pair = jnp.concatenate(cuts, axis=0)
        return pair[:, :lanes] + pair[:, lanes:]

    def factors(ref, base):
        return ref[base:base + rows], ref[base + rows:base + 2 * rows]

    blocks = (
        (own[...], (ufac[0], ufac[1])),
        (joined(near, 0), factors(near, step)),
        (joined(far, 0), factors(far, 2 * step)),
        (joined(corner, step), factors(corner, 2 * step)),
    )
    total = None
    for wave, (ur, ui) in blocks:
        misfit = wave - (dot(ur, c) + dot(ui, ci))
        mt = misfit.T.astype(bf16)
        mr, mi = mt[:width], mt[width:]
        turned = jnp.concatenate([mi, -mr], axis=0)
        term = dot(mt, ur) + dot(turned, ui)
        total = term if total is None else total + term
    return total.T.astype(bf16)


def to_chunks(flat, adjoint):
    rank = adjoint.shape[1]
    for j in range(adjoint.shape[0]):
        adjoint[j] = flat[j * rank:(j + 1) * rank]


def row_kernel(coeffs, own, ufac, near, far, corner, adjoint, *, width):
    c = coeffs[...].reshape(-1, 2 * width)
    to_chunks(row_core(c, own, ufac, near, far, corner, width), adjoint)


def row_first_kernel(coeffs, own, ufac, near, far, corner, *pieces, group, width):
    z = row_index(group)
    rank = coeffs.shape[1]
    c = coeffs[...].reshape(-1, 2 * width)
    flat = row_core(c, own, ufac, near, far, corner, width)

    def place(scratch):
        for j in range(flat.shape[0] // rank):
            scratch[jnp.bitwise_xor(z, j // group), j % group] = flat[j * rank:(j + 1) * rank]
        for b, piece in enumerate(pieces):
            piece[...] = scratch[b]

    pl.run_scoped(place, pltpu.VMEM((len(pieces),) + pieces[0].shape, bf16))


def row_last_kernel(*refs, group, width, count):
    pieces, (own, ufac, near, far, corner, adjoint, coeffs) = refs[:count], refs[count:]
    z = row_index(group)

    def run(scratch):
        for b, piece in enumerate(pieces):
            scratch[jnp.bitwise_xor(z, b)] = piece[...]
        c = scratch[...].reshape(-1, 2 * width)
        coeffs[...] = c
        to_chunks(row_core(c, own, ufac, near, far, corner, width), adjoint)

    pl.run_scoped(run, pltpu.VMEM((count,) + pieces[0].shape, bf16))


def middle_columns_kernel(*refs, group, width, count):
    pieces, refs = refs[:count], refs[count:]
    (x_own, v_own, near, v_near, far, shared, corner), refs = refs[:7], refs[7:]
    outs, (adj_own, adj_near, adj_far) = refs[:count], refs[count:]
    q = group_index(group)
    z = row_index(group)
    sources, lanes = x_own.shape
    rank = pieces[0].shape[1]
    side = count * rank
    tall = 2 * side

    half = sources // 2

    def factors(ref):
        wide = ref.shape[1]
        cuts = [ref[half + h * tall:half + (h + 1) * tall] for h in range(sources // wide)]
        return jnp.concatenate(cuts, axis=1)

    def run(adj, coeffs):
        for b, piece in enumerate(pieces):
            for k in range(group):
                adj[k, jnp.bitwise_xor(z, b)] = piece[jnp.bitwise_xor(q, k)]
        exact = near[...].astype(f32)
        columns = (
            (x_own[...], flat_factors(v_own)),
            (exact[:, :lanes] + exact[:, lanes:], flat_factors(v_near)),
            (far[...].astype(f32), factors(shared)),
            (
                jnp.concatenate([corner[:half, :lanes], corner[:half, lanes:]], axis=0).astype(f32),
                factors(corner),
            ),
        )
        for k, (x, vcat) in enumerate(columns):
            a = adj[k].reshape(side, lanes)
            if k == 0:
                adj_own[...] = a
            elif k == 1:
                adj_near[...] = a
            else:
                adj_far[k - 2] = a
            turned = times_i(a.astype(f32)).astype(bf16)
            s = x + STEP * dot(vcat, jnp.concatenate([a, turned], axis=0), ((0,), (0,)))
            square = s * s
            magnitude = jnp.sqrt(square + swap_halves(square))
            factor = jnp.maximum(magnitude - THRESHOLD, 0.0) / jnp.maximum(magnitude, THRESHOLD)
            t = dot(vcat, (s * factor).astype(bf16))
            c = (t[:side] - times_i(t[side:])).astype(bf16)
            for i in range(count):
                coeffs[i, jnp.bitwise_xor(q, k)] = c[i * rank:(i + 1) * rank]
        for b, out in enumerate(outs):
            out[...] = coeffs[jnp.bitwise_xor(z, b)]

    pl.run_scoped(
        run,
        pltpu.VMEM((group, count, rank, lanes), bf16),
        pltpu.VMEM((count, group, rank, lanes), bf16),
    )


def own_column_kernel(adj_own, adj_near, adj_far, adj_corner, x, vfac, x_new, *, group, width):
    q = group_index(group)

    def run(scratch):
        scratch[0] = adj_own[...]
        scratch[1] = adj_near[...]
        scratch[2] = adj_far[0]
        scratch[3] = adj_corner[1]
        sides = sides_of([scratch[jnp.bitwise_xor(q, s)].astype(f32) for s in range(group)])
        x_new[0], x_new[1] = updated(sides, x[0], x[1], flat_factors(vfac))

    pl.run_scoped(run, pltpu.VMEM((group,) + adj_own.shape, bf16))


def sides_of(quarters):
    pairs = [interleave(*quarters[k:k + 2]) for k in range(0, len(quarters), 2)]
    re = jnp.concatenate([r for r, _ in pairs], axis=1)
    im = jnp.concatenate([i for _, i in pairs], axis=1)
    real_side = jnp.concatenate([re, -im], axis=0).astype(bf16)
    imag_side = jnp.concatenate([im, re], axis=0).astype(bf16)
    return real_side, imag_side


def adjoint_sides(adjoint, *, group):
    count, rank, lanes = adjoint.shape
    rows = count // group
    a = adjoint[...].astype(f32).reshape(rows, group, rank, lanes)
    return sides_of([a[:, s].reshape(rows * rank, lanes) for s in range(group)])


def shrink(sr, si):
    magnitude = jnp.sqrt(sr * sr + si * si)
    factor = jnp.maximum(magnitude - THRESHOLD, 0.0) / jnp.maximum(magnitude, THRESHOLD)
    return sr * factor, si * factor


def updated(sides, xr, xi, vcat):
    gr, gi = (dot(vcat, side, ((0,), (0,))) for side in sides)
    return shrink(xr + STEP * gr, xi + STEP * gi)


def middle_kernel(adjoint, x, vfac, x_new, out, *, group, width):
    vcat = flat_factors(vfac)
    xr, xi = updated(adjoint_sides(adjoint, group=group), x[0], x[1], vcat)
    x_new[0] = xr
    x_new[1] = xi
    send_coeffs(vcat, xr.astype(bf16), xi.astype(bf16), out, group=group, width=width)


def last_kernel(adjoint, x, vfac, misfit, x_new, residual, *, group, width):
    sources = x.shape[1]
    piece = sources // PIECES

    def run(stage, sems):
        copies = [pltpu.make_async_copy(misfit, residual, sems.at[PIECES])]
        copies[0].start()
        sides = adjoint_sides(adjoint, group=group)
        for k in range(PIECES):
            cut = slice(k * piece, (k + 1) * piece)
            stage[0, cut], stage[1, cut] = updated(sides, x[0, cut], x[1, cut], flat_factors(vfac, cut))
            copies.append(pltpu.make_async_copy(stage.at[:, cut], x_new.at[:, cut], sems.at[k]))
            copies[-1].start()
        for copy in copies:
            copy.wait()

    pl.run_scoped(run, pltpu.VMEM(x.shape, f32), pltpu.SemaphoreType.DMA((PIECES + 1,)))


def residual_kernel(own, near, far, corner, ufac, data, out, *, group, width):
    q = group_index(group)
    lanes = 2 * width
    ur, ui = ufac[0], ufac[1]

    def place(scratch):
        for b, ref in enumerate((own, near, far, corner)):
            c = ref[...]
            scratch[b] = dot(ur, c) + dot(ui, times_i(c.astype(f32)).astype(bf16))
        for k in range(group // 2):
            cut = slice(lanes * k, lanes * (k + 1))
            pair = (scratch[jnp.bitwise_xor(q, s)] for s in (2 * k, 2 * k + 1))
            for part, predicted in enumerate(interleave(*pair)):
                out[part, :, cut] = data[part, :, cut] - predicted

    pl.run_scoped(place, pltpu.VMEM((group, data.shape[1], lanes), f32))


def call(kernel, out_shape, *args, from_hbm=False, aliases=None, **static):
    on_chip = pl.BlockSpec(memory_space=pltpu.VMEM)
    off_chip = pl.BlockSpec(memory_space=pltpu.HBM)
    space = pltpu.HBM if from_hbm else pltpu.VMEM
    many = isinstance(out_shape, tuple)

    def spec(out):
        return off_chip if isinstance(out, jax.ShapeDtypeStruct) else on_chip

    return pl.pallas_call(
        functools.partial(kernel, **static),
        out_shape=out_shape,
        in_specs=[off_chip if from_hbm else on_chip] * len(args),
        out_specs=tuple(map(spec, out_shape)) if many else spec(out_shape),
        input_output_aliases=aliases or {},
        compiler_params=pltpu.CompilerParams(vmem_limit_bytes=VMEM_LIMIT),
    )(*(pltpu.with_memory_space_constraint(arg, space) for arg in args))


def body(data, x_init, ufac, vfac):
    tiles = lax.axis_size("tile")
    tile_rows, rank, _ = vfac.shape[1:]
    rows = data.shape[1]
    points = data.shape[2]
    group = tiles // tile_rows
    assert group == 4
    width = points // group
    lanes = 2 * width
    static = dict(group=group, width=width)
    shape = pltpu.VMEM
    result = jax.ShapeDtypeStruct

    def exchange(value, bit):
        return lax.ppermute(value, "tile", [(s, s ^ bit) for s in range(tiles)])

    def spread(value):
        return lax.all_to_all(value, "tile", split_axis=0, concat_axis=0, tiled=True)

    wide = ufac.shape[2]
    step = rows * 2 * lanes // wide
    assert wide % (2 * lanes) == 0 and step % 16 == 0
    chunks = shape((tiles, rank, lanes), bf16)
    sources = x_init.shape[1]
    tall = 2 * tile_rows * rank
    columns = (
        shape((sources // 2 + tall * sources // (2 * lanes), 2 * lanes), bf16),
        shape((sources, lanes), bf16),
        shape((sources, 2 * lanes), bf16),
        shape((sources, lanes), f32),
    )
    by_columns = tile_rows == 4
    coeffs, to_far, to_near, own, ufac, estimate, vfac, *columns = call(
        first_kernel,
        (
            result(chunks.shape, bf16),
            shape((2 * rows + 2 * step, wide), bf16),
            shape((2 * rows + step, wide), bf16),
            shape((rows, lanes), f32),
            shape(ufac.shape, bf16),
            shape(x_init.shape, f32),
            shape(vfac.shape, bf16),
        ) + (columns if by_columns else ()),
        data, x_init, ufac, vfac, from_hbm=True, **static,
    )
    far = exchange(to_far, 2)
    near = exchange(to_near, 1)
    corner = exchange(far, 1)
    gathered = (own, ufac, near, far, corner)
    flat = (tiles * rank, lanes)
    received = spread(coeffs)
    if by_columns:
        piece = shape((group, rank, lanes), bf16)
        side = (tile_rows * rank, lanes)
        counted = dict(count=tile_rows, **static)

        def along_rows(pieces):
            order = {b: exchange(pieces[b], b * group) for b in range(tile_rows - 1, 0, -1)}
            return [pieces[0]] + [order[b] for b in range(1, tile_rows)]

        x_shared, x_far, x_near, x_own = columns
        x_shared = exchange(x_shared, 2)
        x_far = exchange(x_far, 2)
        x_near = exchange(x_near, 1)
        v_near = exchange(vfac, 1)
        x_corner = exchange(x_shared, 1)
        pieces = call(row_first_kernel, (piece,) * tile_rows, received, *gathered, **static)
        pieces = along_rows(pieces)
        *pieces, adj_own, adj_near, adj_far = call(
            middle_columns_kernel,
            (piece,) * tile_rows + (shape(side, bf16), shape(side, bf16), shape((2,) + side, bf16)),
            *pieces, x_own, vfac, x_near, v_near, x_far, x_shared, x_corner, **counted,
        )
        pieces = along_rows(pieces)
        adj_far = exchange(adj_far, 2)
        adj_near = exchange(adj_near, 1)
        adj_corner = exchange(adj_far, 1)
        adjoint, coeffs = call(row_last_kernel, (chunks, shape(flat, bf16)), *pieces, *gathered, **counted)
        estimate = call(
            own_column_kernel, shape(x_init.shape, f32),
            adj_own, adj_near, adj_far, adj_corner, estimate, vfac, aliases={4: 0}, **static,
        )
    else:
        pieces = call(row_kernel, chunks, received, *gathered, width=width)
        estimate, coeffs = call(
            middle_kernel, (shape(x_init.shape, f32), chunks), spread(pieces), estimate, vfac, **static
        )
        received = spread(coeffs)
        adjoint = call(row_kernel, chunks, received, *gathered, width=width)
        coeffs = received.reshape(flat)
    coeffs_far = exchange(coeffs, 2)
    coeffs_near = exchange(coeffs, 1)
    coeffs_corner = exchange(coeffs_far, 1)
    adjoint = spread(adjoint)
    misfit = call(
        residual_kernel, shape(data.shape, f32),
        coeffs, coeffs_near, coeffs_far, coeffs_corner, ufac, data, **static,
    )
    return call(
        last_kernel, (result(x_init.shape, f32), result(data.shape, f32)),
        adjoint, estimate, vfac, misfit, **static,
    )


def solution(mesh):
    in_specs = (
        P("freq", "tile", None),
        P("freq", "tile", None),
        P("freq", "tile", None),
        P("freq", None, None, "tile"),
    )
    out_specs = (P("freq", "tile", None), P("freq", "tile", None))
    return jax.shard_map(body, mesh=mesh, in_specs=in_specs, out_specs=out_specs, check_vma=False)
```

```python
import functools

import jax
import jax.numpy as jnp
from jax import lax
from jax.experimental import pallas as pl
from jax.experimental.pallas import tpu as pltpu
from jax.sharding import PartitionSpec as P


STEP = 0.4
THRESHOLD = 0.4
VMEM_LIMIT = 24 << 20
PIECES = 4

f32 = jnp.float32
bf16 = jnp.bfloat16


def dot(a, b, dims=((1,), (0,))):
    return lax.dot_general(a, b, (dims, ((), ())), preferred_element_type=f32)


def swap_halves(a):
    return pltpu.roll(a, a.shape[1] // 2, 1)


def left_half(a):
    return lax.broadcasted_iota(jnp.int32, a.shape, 1) < a.shape[1] // 2


def times_i(a):
    s = swap_halves(a)
    return jnp.where(left_half(a), -s, s)


def interleave(re, im):
    low = left_half(re)
    return (
        jnp.where(low, re, swap_halves(im)),
        jnp.where(low, swap_halves(re), im),
    )


def slices_of(re, im, width):
    out = []
    for k in range(re.shape[1] // (2 * width)):
        cut = slice(2 * width * k, 2 * width * (k + 1))
        out.extend(interleave(re[:, cut], im[:, cut]))
    return out


def group_index(group):
    return lax.rem(lax.axis_index("tile"), group)


def row_index(group):
    return lax.div(lax.axis_index("tile"), group)


def split(block):
    high = block.astype(bf16)
    low = (block - high.astype(f32)).astype(bf16)
    return high, low


def send_coeffs(vcat, xr, xi, out, *, group, width):
    half = vcat.shape[0] // 2
    t1 = dot(vcat, xr)
    t2 = dot(vcat, xi)
    cr = t1[:half] + t2[half:]
    ci = t2[:half] - t1[half:]
    rank = out.shape[1]
    blocks = slices_of(cr, ci, width)
    for i in range(half // rank):
        for q in range(group):
            out[i * group + q] = blocks[q][i * rank:(i + 1) * rank].astype(bf16)


def flat_factors(vfac, cut=slice(None)):
    parts, rows, rank, _ = vfac.shape
    return vfac[:, :, :, cut].reshape(parts * rows * rank, -1)


def half_blocks(x, which, parity, lanes):
    cut = pl.ds(pl.multiple_of(which * lanes, lanes), lanes)
    even, odd = interleave(x[0, :, cut], x[1, :, cut])
    first = jnp.broadcast_to(parity, even.shape) == 0
    return jnp.where(first, even, odd), jnp.where(first, odd, even)


def first_kernel(data, x, ufac, vfac, out, to_far, to_near, own, u_own, x_own, v_own, *columns, group, width):
    rows = data.shape[1]
    sources = x.shape[1]
    lanes = 2 * width
    folds = ufac.shape[2] // (2 * lanes)
    step = rows // folds
    q = group_index(group)

    def run(stage, waves, scratch, sems):
        x_copy = pltpu.make_async_copy(x, x_own, sems.at[0])
        v_copy = pltpu.make_async_copy(vfac, v_own, sems.at[1])
        wave_copy = pltpu.make_async_copy(data, waves, sems.at[2])
        u_copy = pltpu.make_async_copy(ufac, u_own, sems.at[3])
        out_copy = pltpu.make_async_copy(stage, out, sems.at[4])
        for copy in (x_copy, v_copy, wave_copy, u_copy):
            copy.start()
        v_copy.wait()
        x_copy.wait()
        send_coeffs(
            flat_factors(v_own), x_own[0].astype(bf16), x_own[1].astype(bf16), stage, group=group, width=width
        )
        out_copy.start()
        wave_copy.wait()
        for s, block in enumerate(slices_of(waves[0], waves[1], width)):
            scratch[jnp.bitwise_xor(q, s)] = block
        own[...] = scratch[0]
        for ref, base, b in ((to_near, 0, 1), (to_far, 0, 2), (to_far, step, 3)):
            high, low = split(scratch[b])
            for g in range(folds):
                cut = slice(g * step, (g + 1) * step)
                lane = 2 * lanes * g
                ref[base:base + step, lane:lane + lanes] = high[cut]
                ref[base:base + step, lane + lanes:lane + 2 * lanes] = low[cut]
        u_copy.wait()
        for part in range(2):
            to_near[step + rows * part:step + rows * (part + 1)] = u_own[part]
            to_far[2 * step + rows * part:2 * step + rows * (part + 1)] = u_own[part]
        if columns:
            shared_x, far_x, near_x = columns
            tall = 2 * v_own.shape[1] * v_own.shape[2]
            side, parity = lax.div(q, 2), lax.rem(q, 2)
            same, other = half_blocks(x_own, 1 - side, parity, lanes)
            far_x[...] = same.astype(bf16)
            half = sources // 2
            shared_x[:half, :lanes] = other[:half].astype(bf16)
            shared_x[:half, lanes:] = other[half:].astype(bf16)
            _, other = half_blocks(x_own, side, parity, lanes)
            high, low = split(other)
            near_x[:, :lanes] = high
            near_x[:, lanes:] = low
            for h in range(sources // (2 * lanes)):
                cut = slice(h * 2 * lanes, (h + 1) * 2 * lanes)
                shared_x[half + h * tall:half + (h + 1) * tall] = flat_factors(v_own, cut)
        out_copy.wait()

    pl.run_scoped(
        run,
        pltpu.VMEM(out.shape, bf16),
        pltpu.VMEM(data.shape, f32),
        pltpu.VMEM((group, rows, lanes), f32),
        pltpu.SemaphoreType.DMA((5,)),
    )


def row_core(c, own, ufac, near, far, corner, width):
    lanes = 2 * width
    rows = own.shape[0]
    ci = times_i(c.astype(f32)).astype(bf16)
    folds = ufac.shape[2] // (2 * lanes)
    step = rows // folds

    def joined(ref, base):
        cuts = [ref[base:base + step, 2 * lanes * g:2 * lanes * (g + 1)].astype(f32) for g in range(folds)]
        pair = jnp.concatenate(cuts, axis=0)
        return pair[:, :lanes] + pair[:, lanes:]

    def factors(ref, base):
        return ref[base:base + rows], ref[base + rows:base + 2 * rows]

    blocks = (
        (own[...], (ufac[0], ufac[1])),
        (joined(near, 0), factors(near, step)),
        (joined(far, 0), factors(far, 2 * step)),
        (joined(corner, step), factors(corner, 2 * step)),
    )
    total = None
    for wave, (ur, ui) in blocks:
        misfit = wave - (dot(ur, c) + dot(ui, ci))
        mt = misfit.astype(bf16).T
        mr, mi = mt[:width], mt[width:]
        turned = jnp.concatenate([mi, -mr], axis=0)
        term = dot(mt, ur) + dot(turned, ui)
        total = term if total is None else total + term
    return total.T.astype(bf16)


def to_chunks(flat, adjoint):
    rank = adjoint.shape[1]
    for j in range(adjoint.shape[0]):
        adjoint[j] = flat[j * rank:(j + 1) * rank]


def row_kernel(coeffs, own, ufac, near, far, corner, adjoint, *, width):
    c = coeffs[...].reshape(-1, 2 * width)
    to_chunks(row_core(c, own, ufac, near, far, corner, width), adjoint)


def row_first_kernel(coeffs, own, ufac, near, far, corner, *pieces, group, width):
    z = row_index(group)
    rank = coeffs.shape[1]
    c = coeffs[...].reshape(-1, 2 * width)
    flat = row_core(c, own, ufac, near, far, corner, width)

    def place(scratch):
        for j in range(flat.shape[0] // rank):
            scratch[jnp.bitwise_xor(z, j // group), j % group] = flat[j * rank:(j + 1) * rank]
        for b, piece in enumerate(pieces):
            piece[...] = scratch[b]

    pl.run_scoped(place, pltpu.VMEM((len(pieces),) + pieces[0].shape, bf16))


def row_last_kernel(*refs, group, width, count):
    pieces, (own, ufac, near, far, corner, adjoint, coeffs) = refs[:count], refs[count:]
    z = row_index(group)

    def run(scratch):
        for b, piece in enumerate(pieces):
            scratch[jnp.bitwise_xor(z, b)] = piece[...]
        c = scratch[...].reshape(-1, 2 * width)
        coeffs[...] = c
        to_chunks(row_core(c, own, ufac, near, far, corner, width), adjoint)

    pl.run_scoped(run, pltpu.VMEM((count,) + pieces[0].shape, bf16))


def middle_columns_kernel(*refs, group, width, count):
    pieces, refs = refs[:count], refs[count:]
    (x_own, v_own, near, v_near, far, shared, corner), refs = refs[:7], refs[7:]
    outs, (adj_own, adj_near, adj_far) = refs[:count], refs[count:]
    q = group_index(group)
    z = row_index(group)
    sources, lanes = near.shape[0], near.shape[1] // 2
    rank = pieces[0].shape[1]
    side = count * rank
    tall = 2 * side

    half = sources // 2

    def factors(ref):
        wide = ref.shape[1]
        cuts = [ref[half + h * tall:half + (h + 1) * tall] for h in range(sources // wide)]
        return jnp.concatenate(cuts, axis=1)

    def run(adj, coeffs):
        for b, piece in enumerate(pieces):
            for k in range(group):
                adj[k, jnp.bitwise_xor(z, b)] = piece[jnp.bitwise_xor(q, k)]
        exact = near[...].astype(f32)
        columns = (
            (half_blocks(x_own, lax.div(q, 2), lax.rem(q, 2), lanes)[0], flat_factors(v_own)),
            (exact[:, :lanes] + exact[:, lanes:], flat_factors(v_near)),
            (far[...].astype(f32), factors(shared)),
            (
                jnp.concatenate([corner[:half, :lanes], corner[:half, lanes:]], axis=0).astype(f32),
                factors(corner),
            ),
        )
        for k, (x, vcat) in enumerate(columns):
            a = adj[k].reshape(side, lanes)
            if k == 0:
                adj_own[...] = a
            elif k == 1:
                adj_near[...] = a
            else:
                adj_far[k - 2] = a
            turned = times_i(a.astype(f32)).astype(bf16)
            s = x + STEP * dot(vcat, jnp.concatenate([a, turned], axis=0), ((0,), (0,)))
            square = s * s
            factor = shrink_factor(square + swap_halves(square))
            t = dot(vcat, (s * factor).astype(bf16))
            c = (t[:side] - times_i(t[side:])).astype(bf16)
            for i in range(count):
                coeffs[i, jnp.bitwise_xor(q, k)] = c[i * rank:(i + 1) * rank]
        for b, out in enumerate(outs):
            out[...] = coeffs[jnp.bitwise_xor(z, b)]

    pl.run_scoped(
        run,
        pltpu.VMEM((group, count, rank, lanes), bf16),
        pltpu.VMEM((count, group, rank, lanes), bf16),
    )


def own_column_kernel(adj_own, adj_near, adj_far, adj_corner, x, vfac, x_new, *, group, width):
    q = group_index(group)

    def run(scratch):
        scratch[0] = adj_own[...]
        scratch[1] = adj_near[...]
        scratch[2] = adj_far[0]
        scratch[3] = adj_corner[1]
        sides = sides_of([scratch[jnp.bitwise_xor(q, s)].astype(f32) for s in range(group)])
        x_new[0], x_new[1] = updated(sides, x[0], x[1], flat_factors(vfac))

    pl.run_scoped(run, pltpu.VMEM((group,) + adj_own.shape, bf16))


def sides_of(quarters):
    pairs = [interleave(*quarters[k:k + 2]) for k in range(0, len(quarters), 2)]
    re = jnp.concatenate([r for r, _ in pairs], axis=1)
    im = jnp.concatenate([i for _, i in pairs], axis=1)
    real_side = jnp.concatenate([re, -im], axis=0).astype(bf16)
    imag_side = jnp.concatenate([im, re], axis=0).astype(bf16)
    return real_side, imag_side


def adjoint_sides(adjoint, *, group):
    count, rank, lanes = adjoint.shape
    rows = count // group
    a = adjoint[...].astype(f32).reshape(rows, group, rank, lanes)
    return sides_of([a[:, s].reshape(rows * rank, lanes) for s in range(group)])


def shrink_factor(square):
    return jnp.where(square > THRESHOLD * THRESHOLD, 1.0 - THRESHOLD * lax.rsqrt(square), 0.0)


def shrink(sr, si):
    factor = shrink_factor(sr * sr + si * si)
    return sr * factor, si * factor


def updated(sides, xr, xi, vcat):
    gr, gi = (dot(vcat, side, ((0,), (0,))) for side in sides)
    return shrink(xr + STEP * gr, xi + STEP * gi)


def middle_kernel(adjoint, x, vfac, x_new, out, *, group, width):
    vcat = flat_factors(vfac)
    xr, xi = updated(adjoint_sides(adjoint, group=group), x[0], x[1], vcat)
    x_new[0] = xr
    x_new[1] = xi
    send_coeffs(vcat, xr.astype(bf16), xi.astype(bf16), out, group=group, width=width)


def last_kernel(adjoint, x, vfac, misfit, x_new, residual, *, group, width):
    sources = x.shape[1]
    piece = sources // PIECES

    def run(stage, sems):
        copies = [pltpu.make_async_copy(misfit, residual, sems.at[PIECES])]
        copies[0].start()
        sides = adjoint_sides(adjoint, group=group)
        for k in range(PIECES):
            cut = slice(k * piece, (k + 1) * piece)
            stage[0, cut], stage[1, cut] = updated(sides, x[0, cut], x[1, cut], flat_factors(vfac, cut))
            copies.append(pltpu.make_async_copy(stage.at[:, cut], x_new.at[:, cut], sems.at[k]))
            copies[-1].start()
        for copy in copies:
            copy.wait()

    pl.run_scoped(run, pltpu.VMEM(x.shape, f32), pltpu.SemaphoreType.DMA((PIECES + 1,)))


def residual_kernel(own, near, far, corner, ufac, data, out, *, group, width):
    q = group_index(group)
    lanes = 2 * width
    ur, ui = ufac[0], ufac[1]

    def place(scratch):
        for b, ref in enumerate((own, near, far, corner)):
            c = ref[...]
            scratch[b] = dot(ur, c) + dot(ui, times_i(c.astype(f32)).astype(bf16))
        for k in range(group // 2):
            cut = slice(lanes * k, lanes * (k + 1))
            pair = (scratch[jnp.bitwise_xor(q, s)] for s in (2 * k, 2 * k + 1))
            for part, predicted in enumerate(interleave(*pair)):
                out[part, :, cut] = data[part, :, cut] - predicted

    pl.run_scoped(place, pltpu.VMEM((group, data.shape[1], lanes), f32))


def call(kernel, out_shape, *args, from_hbm=False, aliases=None, **static):
    on_chip = pl.BlockSpec(memory_space=pltpu.VMEM)
    off_chip = pl.BlockSpec(memory_space=pltpu.HBM)
    space = pltpu.HBM if from_hbm else pltpu.VMEM
    many = isinstance(out_shape, tuple)

    def spec(out):
        return off_chip if isinstance(out, jax.ShapeDtypeStruct) else on_chip

    return pl.pallas_call(
        functools.partial(kernel, **static),
        out_shape=out_shape,
        in_specs=[off_chip if from_hbm else on_chip] * len(args),
        out_specs=tuple(map(spec, out_shape)) if many else spec(out_shape),
        input_output_aliases=aliases or {},
        compiler_params=pltpu.CompilerParams(vmem_limit_bytes=VMEM_LIMIT),
    )(*(pltpu.with_memory_space_constraint(arg, space) for arg in args))


def body(data, x_init, ufac, vfac):
    tiles = lax.axis_size("tile")
    tile_rows, rank, _ = vfac.shape[1:]
    rows = data.shape[1]
    points = data.shape[2]
    group = tiles // tile_rows
    assert group == 4
    width = points // group
    lanes = 2 * width
    static = dict(group=group, width=width)
    shape = pltpu.VMEM
    result = jax.ShapeDtypeStruct

    def exchange(value, bit):
        return lax.ppermute(value, "tile", [(s, s ^ bit) for s in range(tiles)])

    def spread(value):
        return lax.all_to_all(value, "tile", split_axis=0, concat_axis=0, tiled=True)

    wide = ufac.shape[2]
    step = rows * 2 * lanes // wide
    assert wide % (2 * lanes) == 0 and step % 16 == 0
    chunks = shape((tiles, rank, lanes), bf16)
    sources = x_init.shape[1]
    tall = 2 * tile_rows * rank
    columns = (
        shape((sources // 2 + tall * sources // (2 * lanes), 2 * lanes), bf16),
        shape((sources, lanes), bf16),
        shape((sources, 2 * lanes), bf16),
    )
    by_columns = tile_rows == 4
    coeffs, to_far, to_near, own, ufac, estimate, vfac, *columns = call(
        first_kernel,
        (
            result(chunks.shape, bf16),
            shape((2 * rows + 2 * step, wide), bf16),
            shape((2 * rows + step, wide), bf16),
            shape((rows, lanes), f32),
            shape(ufac.shape, bf16),
            shape(x_init.shape, f32),
            shape(vfac.shape, bf16),
        ) + (columns if by_columns else ()),
        data, x_init, ufac, vfac, from_hbm=True, **static,
    )
    far = exchange(to_far, 2)
    near = exchange(to_near, 1)
    corner = exchange(far, 1)
    gathered = (own, ufac, near, far, corner)
    flat = (tiles * rank, lanes)
    received = spread(coeffs)
    if by_columns:
        piece = shape((group, rank, lanes), bf16)
        side = (tile_rows * rank, lanes)
        counted = dict(count=tile_rows, **static)

        def along_rows(pieces):
            order = {b: exchange(pieces[b], b * group) for b in range(tile_rows - 1, 0, -1)}
            return [pieces[0]] + [order[b] for b in range(1, tile_rows)]

        x_shared, x_far, x_near = columns
        x_shared = exchange(x_shared, 2)
        x_far = exchange(x_far, 2)
        x_near = exchange(x_near, 1)
        v_near = exchange(vfac, 1)
        x_corner = exchange(x_shared, 1)
        pieces = call(row_first_kernel, (piece,) * tile_rows, received, *gathered, **static)
        pieces = along_rows(pieces)
        *pieces, adj_own, adj_near, adj_far = call(
            middle_columns_kernel,
            (piece,) * tile_rows + (shape(side, bf16), shape(side, bf16), shape((2,) + side, bf16)),
            *pieces, estimate, vfac, x_near, v_near, x_far, x_shared, x_corner, **counted,
        )
        pieces = along_rows(pieces)
        adj_far = exchange(adj_far, 2)
        adj_near = exchange(adj_near, 1)
        adj_corner = exchange(adj_far, 1)
        adjoint, coeffs = call(row_last_kernel, (chunks, shape(flat, bf16)), *pieces, *gathered, **counted)
        estimate = call(
            own_column_kernel, shape(x_init.shape, f32),
            adj_own, adj_near, adj_far, adj_corner, estimate, vfac, aliases={4: 0}, **static,
        )
    else:
        pieces = call(row_kernel, chunks, received, *gathered, width=width)
        estimate, coeffs = call(
            middle_kernel, (shape(x_init.shape, f32), chunks), spread(pieces), estimate, vfac, **static
        )
        received = spread(coeffs)
        adjoint = call(row_kernel, chunks, received, *gathered, width=width)
        coeffs = received.reshape(flat)
    coeffs_far = exchange(coeffs, 2)
    coeffs_near = exchange(coeffs, 1)
    coeffs_corner = exchange(coeffs_far, 1)
    adjoint = spread(adjoint)
    misfit = call(
        residual_kernel, shape(data.shape, f32),
        coeffs, coeffs_near, coeffs_far, coeffs_corner, ufac, data, **static,
    )
    return call(
        last_kernel, (result(x_init.shape, f32), result(data.shape, f32)),
        adjoint, estimate, vfac, misfit, **static,
    )


def solution(mesh):
    in_specs = (
        P("freq", "tile", None),
        P("freq", "tile", None),
        P("freq", "tile", None),
        P("freq", None, None, "tile"),
    )
    out_specs = (P("freq", "tile", None), P("freq", "tile", None))
    return jax.shard_map(body, mesh=mesh, in_specs=in_specs, out_specs=out_specs, check_vma=False)
```
